32 devices in a mesh: dp: 4 (over x, core), tensor: 8 (over z, y).
Axes of the slice: x: 2, y: 2, z: 4, core: 2. Of those that a mesh axis runs over, the one named last changes fastest.
Arguments:
- inputs: bfloat16 [16384, 1024], P(('dp', 'tensor')), may hold values from -6 to 6
- segments: int32 [8, 2048], P('dp'), may hold values from -1 to 15, as said below
- norm_gain: float32 [1024], replicated, may hold values from 0.25 to 1.75
- norm_bias: float32 [1024], replicated, may hold values from -3 to 3
- w_qkv: bfloat16 [3, 1024, 1024], P(None, None, 'tensor'), may hold values from -0.25 to 0.25
- w_out: bfloat16 [1024, 1024], P('tensor'), may hold values from -0.75 to 0.75
- w_in: bfloat16 [1024, 4096], P(None, 'tensor'), may hold values from -0.1875 to 0.1875
- b_in: float32 [4096], P('tensor'), may hold values from -3 to 3
- w_fc: bfloat16 [4096, 1024], P('tensor'), may hold values from -0.09375 to 0.09375
- b_out: float32 [1024], replicated, may hold values from -3 to 3
- cotangent: bfloat16 [16384, 1024], P(('dp', 'tensor')), may hold values from -6 to 6
Outputs:
- output: bfloat16 [16384, 1024], P(('dp', 'tensor'))
- grad_inputs: float32 [16384, 1024], P(('dp', 'tensor'))
- grad_norm_gain: float32 [1024], replicated
- grad_norm_bias: float32 [1024], replicated
- grad_w_qkv: float32 [3, 1024, 1024], P(None, None, 'tensor')
- grad_w_out: float32 [1024, 1024], P('tensor')
- grad_w_in: float32 [1024, 4096], P(None, 'tensor')
- grad_b_in: float32 [4096], P('tensor')
- grad_w_fc: float32 [4096, 1024], P('tensor')
- grad_b_out: float32 [1024], replicated
The draws below stay inside these ranges and needn't reach their ends.
Inputs may be any that keep to these rules, and one draw needn't show every extreme that they name: `segments`: in each row, ids of proteins are runs of equal values starting at 0 at the first position and rising by one; positions after a row's last protein are padding, marked -1. Some rows hold one protein of 1024 to 2048 residues; the others hold exactly 16 proteins, and 2 where that is fewer, and row 0 is always such a row.
All inputs are finite; a program needn't handle non-finite values.
Results may differ from the reference program's by a relative error of at most 0.023.
Values may be sent and summed in bfloat16 or wider, within the bound.
No kernel may reach another device: no remote copies, remote signals or barrier semaphores. Data moves between devices by JAX's collectives and lax.ppermute only.
A program may use at most 256 MiB of HBM per device.

```python
import math
import jax
import jax.numpy as jnp
from jax import lax

D = 1024
HEADS = 16
HD = 64
ROT = 32
FF = 4096
SEQ = 2048
ROWS = 8
TOKENS = 16384


def draw_segments(key, part):
    key_kind, key_length, key_starts, key_padding = jax.random.split(key, 4)
    places = lax.broadcasted_iota(jnp.int32, (ROWS, SEQ), 1)
    row_numbers = lax.broadcasted_iota(jnp.int32, (ROWS, 1), 0)
    row_kind = jax.random.randint(key_kind, (ROWS, 1), 0, 2)
    row_kind = jnp.where(row_numbers == 0, 0, row_kind)
    long_length = jax.random.randint(key_length, (ROWS, 1), SEQ // 2, SEQ + 1)
    protein_count = max(SEQ // 128, 2)
    row_keys = jax.random.split(key_starts, ROWS)
    shuffled = jax.vmap(lambda row_key: jax.random.permutation(row_key, SEQ // 2 - 1))(row_keys) + 1
    chosen = shuffled[:, :protein_count - 1]
    starts = jnp.sum((places[:, :, None] == chosen[:, None, :]).astype(jnp.int32), axis=-1)
    short_ids = jnp.cumsum(starts, axis=1)
    padding = jax.random.randint(key_padding, (ROWS, 1), 0, SEQ // 8 + 1)
    short_ids = jnp.where(places < SEQ - padding, short_ids, -1)
    long_ids = jnp.where(places < long_length, 0, -1)
    return jnp.where(row_kind == 1, long_ids, short_ids).astype(jnp.int32)


def level_of(key, shape, cuts, smallest, high):
    def one(axis_at, blocks):
        heights = jax.random.uniform(jax.random.fold_in(jax.random.fold_in(key, 6), axis_at), (blocks,), jnp.float32, smallest / len(cuts), high / len(cuts))
        return jnp.repeat(jnp.exp(heights), shape[axis_at] // blocks).reshape((-1,) + (1,) * (len(shape) - axis_at - 1))

    factor_of = one(*cuts[0])
    for cut in cuts[1:]:
        factor_of = factor_of * one(*cut)
    return factor_of


def bell_draw(key, shape, deviation, limit, shards=(), dtype=jnp.bfloat16):
    factor_of = level_of(key, shape, shards, -0.22, 0.18) if shards else 1.0
    entries = jax.random.normal(key, shape, jnp.float32) * deviation * factor_of
    return jnp.minimum(jnp.maximum(entries, -limit), limit).astype(dtype)


def setup_inputs(seed: int = 0) -> dict:
    splits = jax.random.split(jax.random.key(seed), 12)
    return {
        "inputs": bell_draw(splits[0], (TOKENS, D), 1.0, 6.0, ((0, 32),)),
        "segments": draw_segments(jax.random.fold_in(splits[11], 71), 0),
        "norm_gain": jnp.clip(1.0 + 0.15 * jax.random.normal(splits[2], (D,), jnp.float32), 0.25, 1.75),
        "norm_bias": bell_draw(splits[3], (D,), 0.5, 3.0, (), jnp.float32),
        "w_qkv": bell_draw(splits[4], (3, D, D), (D // 2) ** -0.5, 0.25, ((2, 8),)),
        "w_out": bell_draw(splits[5], (D, D), (D // 16) ** -0.5, 0.75, ((0, 8),)),
        "w_in": bell_draw(splits[6], (D, FF), D ** -0.5, 0.1875, ((1, 8),)),
        "b_in": bell_draw(splits[7], (FF,), 0.5, 3.0, ((0, 8),), jnp.float32),
        "w_fc": bell_draw(splits[8], (FF, D), FF ** -0.5, 0.09375, ((0, 8),)),
        "b_out": bell_draw(splits[9], (D,), 0.5, 3.0, (), jnp.float32),
        "cotangent": bell_draw(splits[10], (TOKENS, D), 1.0, 6.0, ((0, 32),)),
    }


@jax.custom_vjp
def low(v):
    return lax.optimization_barrier(v.astype(jnp.bfloat16)).astype(jnp.float32)

@jax.custom_vjp
def low_back(v):
    return v

def low_keep(v):
    return (low(v), None)

def low_pass(kept, grad):
    return (grad,)

def back_keep(v):
    return (v, None)

def back_low(kept, grad):
    return (low(grad),)
low.defvjp(low_keep, low_pass)
low_back.defvjp(back_keep, back_low)
EPSILON = 1e-05
HIGHEST = lax.Precision.HIGHEST
NEG_LARGE = -1e+30

def rope_tables(segments):
    places = lax.broadcasted_iota(jnp.int32, segments.shape, 1)
    leading = jnp.ones_like(segments[:, :1])
    changes = jnp.concatenate([leading, (segments[:, 1:] != segments[:, :-1]).astype(jnp.int32)], axis=1)
    starts = lax.cummax(places * changes, axis=1)
    offsets = (places - starts).astype(jnp.float32)
    half_rot = ROT // 2
    frequency = jnp.exp(lax.broadcasted_iota(jnp.float32, (half_rot,), 0) * (-2.0 * math.log(10000.0) / ROT))
    angles = offsets[:, :, None] * frequency
    return (jnp.cos(angles)[:, :, None, :], jnp.sin(angles)[:, :, None, :])

def rotate(tensor, cos_table, sin_table):
    half_rot = ROT // 2
    first_half = tensor[..., :half_rot]
    second_half = tensor[..., half_rot:ROT]
    return jnp.concatenate([first_half * cos_table - second_half * sin_table, second_half * cos_table + first_half * sin_table, tensor[..., ROT:]], axis=-1)

def allowed_mask(query_ids, key_ids, query_places, key_places):
    same_protein = query_ids[..., :, None] == key_ids[..., None, :]
    earlier = key_places[None, :] <= query_places[:, None]
    itself = key_places[None, :] == query_places[:, None]
    real_token = query_ids[..., :, None] >= 0
    return earlier & same_protein & real_token | itself

def attend_head(queries, keys, values, seg_row):
    places = lax.broadcasted_iota(jnp.int32, (SEQ,), 0)
    score_scale = HD ** (-0.5)
    scores = low_back(jnp.dot(queries, keys.T, preferred_element_type=jnp.float32, precision=HIGHEST) * score_scale)
    scores = jnp.where(allowed_mask(seg_row, seg_row, places, places), scores, NEG_LARGE)
    attn_probs = jax.nn.softmax(scores, axis=-1)
    return low_back(jnp.dot(low(attn_probs), values, preferred_element_type=jnp.float32, precision=HIGHEST))

def block_layer(params, block_rows, segments):
    norm_gain, norm_bias, w_qkv, w_out, w_in, b_in, w_fc, b_out = params
    row_count = segments.shape[0]
    row_mean = lax.optimization_barrier(jnp.mean(block_rows, axis=-1, keepdims=True))
    centred = block_rows - row_mean
    variance = lax.optimization_barrier(jnp.mean(centred * centred, axis=-1, keepdims=True))
    normed = low(centred * lax.rsqrt(variance + EPSILON) * norm_gain + norm_bias)
    cos_table, sin_table = rope_tables(segments)

    def project(member):
        made = jnp.dot(normed, w_qkv[member], preferred_element_type=jnp.float32, precision=HIGHEST)
        return low_back(made).reshape(row_count, SEQ, HEADS, HD)
    queries = low(rotate(project(0), cos_table, sin_table))
    keys = low(rotate(project(1), cos_table, sin_table))
    values = low(project(2))

    def heads_first(tensor):
        return jnp.transpose(tensor, (0, 2, 1, 3)).reshape(row_count * HEADS, SEQ, HD)
    seg_items = jnp.repeat(segments, HEADS, axis=0)
    checked = jax.checkpoint(attend_head)
    attended = lax.map(lambda pieces: checked(pieces[0], pieces[1], pieces[2], pieces[3]), (heads_first(queries), heads_first(keys), heads_first(values), seg_items))
    attended = low(jnp.transpose(attended.reshape(row_count, HEADS, SEQ, HD), (0, 2, 1, 3)).reshape(row_count * SEQ, D))
    attn = jnp.dot(attended, w_out, preferred_element_type=jnp.float32, precision=HIGHEST)
    pre_act = low_back(jnp.dot(normed, w_in, preferred_element_type=jnp.float32, precision=HIGHEST) + b_in)
    hidden = low(jax.nn.gelu(pre_act, approximate=True))
    mlp = jnp.dot(hidden, w_fc, preferred_element_type=jnp.float32, precision=HIGHEST)
    return block_rows + attn + mlp + b_out

def reference(inputs, segments, norm_gain, norm_bias, w_qkv, w_out, w_in, b_in, w_fc, b_out, cotangent):
    params = tuple((weight.astype(jnp.float32) for weight in (norm_gain, norm_bias, w_qkv, w_out, w_in, b_in, w_fc, b_out)))
    inputs_f = inputs.astype(jnp.float32)

    def forward(params_in, rows_in):
        row_blocks = rows_in.reshape(ROWS // 2, 2 * SEQ, D)
        seg_blocks = segments.reshape(ROWS // 2, 2, SEQ)
        checked = jax.checkpoint(block_layer)

        def advance(state_in, pieces):
            return (state_in, checked(params_in, pieces[0], pieces[1]))
        _, outputs = lax.scan(advance, jnp.zeros((), jnp.float32), (row_blocks, seg_blocks))
        return outputs.reshape(TOKENS, D)
    result, pullback = jax.vjp(forward, params, inputs_f)
    weight_grads, grad_inputs = pullback(cotangent.astype(jnp.float32))
    grad_gain, grad_bias, grad_qkv, grad_out, grad_in, grad_b_in, grad_fc, grad_b_out = weight_grads
    return (result.astype(jnp.bfloat16), grad_inputs, grad_gain, grad_bias, grad_qkv, grad_out, grad_in, grad_b_in, grad_fc, grad_b_out)
```

```python
import math

import jax
import jax.numpy as jnp
from jax import lax
from jax.experimental import pallas as pl
from jax.experimental.pallas import tpu as pltpu
from jax.sharding import PartitionSpec as P

HD = 64
ROT = 32
EPSILON = 1e-05
NEG_LARGE = -1e30
BF16 = jnp.bfloat16
F32 = jnp.float32
LANES = 128
VMEM_BYTES = 60 * 1024 * 1024


def nn(a, b):
    return lax.dot_general(a, b, (((1,), (0,)), ((), ())), preferred_element_type=F32)


def nt(a, b):
    return lax.dot_general(a, b, (((1,), (1,)), ((), ())), preferred_element_type=F32)


def tn(a, b):
    return lax.dot_general(a, b, (((0,), (0,)), ((), ())), preferred_element_type=F32)


def resident(shape):
    return pl.BlockSpec(shape, lambda *_: (0,) * len(shape), pipeline_mode=pl.Buffered(1))


def params():
    return pltpu.CompilerParams(vmem_limit_bytes=VMEM_BYTES)


def cost(flops, moved, trans=0):
    return pl.CostEstimate(flops=int(flops), bytes_accessed=int(moved), transcendentals=int(trans))


def bit_list(count):
    return [1 << n for n in range(count.bit_length() - 1)]


def gather_slots(mine, axis, size, bits):
    pieces = {0: mine}
    for bit in bits:
        perm = [(i, i ^ bit) for i in range(size)]
        order = sorted(pieces)
        if len(order) == 1:
            got = [lax.ppermute(pieces[0], axis, perm)]
        else:
            got = lax.ppermute(jnp.stack([pieces[k] for k in order]), axis, perm)
        for place, k in enumerate(order):
            pieces[k ^ bit] = got[place]
    return pieces


def reduce_slots(slots, axis, size, bits):
    pieces = dict(slots)
    for bit in bits:
        perm = [(i, i ^ bit) for i in range(size)]
        away = sorted(k for k in pieces if k & bit)
        if len(away) == 1:
            got = [lax.ppermute(pieces[away[0]], axis, perm)]
        else:
            got = lax.ppermute(jnp.stack([pieces[k] for k in away]), axis, perm)
        for place, k in enumerate(away):
            kept = k ^ bit
            pieces[kept] = (pieces[kept].astype(F32) + got[place].astype(F32)).astype(pieces[kept].dtype)
            del pieces[k]
    return pieces[0]


def gather_rows(block, size, group):
    half = block.shape[0] // 2
    bits = bit_list(group)
    first = gather_slots(block[:half], "tensor", size, bits)
    second = gather_slots(block[half:], "tensor", size, bits[::-1])
    return jnp.concatenate([part[k] for k in range(group) for part in (first, second)], axis=0)


def reduce_rows(whole, size, group):
    half = whole.shape[0] // group // 2
    bits = bit_list(group)
    parts = whole.reshape(group, 2, half, whole.shape[1])
    first = reduce_slots({k: parts[k, 0] for k in range(group)}, "tensor", size, bits[::-1])
    second = reduce_slots({k: parts[k, 1] for k in range(group)}, "tensor", size, bits)
    return jnp.concatenate([first, second], axis=0)


def natural(pieces, me):
    stacked = jnp.stack([pieces[k] for k in range(len(pieces))])
    count = stacked.shape[0]
    return jnp.concatenate(
        [lax.dynamic_slice_in_dim(stacked, jnp.bitwise_xor(me, n), 1, axis=0) for n in range(count)],
        axis=0,
    )


def to_slots(indexed, me):
    count = indexed.shape[0]
    return {
        k: lax.dynamic_index_in_dim(indexed, jnp.bitwise_xor(me, k), 0, keepdims=False)
        for k in range(count)
    }


def widen(rows, width):
    times = width // rows.shape[-1]
    if times == 1:
        return rows
    lead = rows.shape[:-2]
    short = rows.shape[-2] // times
    cut = rows.reshape(lead + (times, short, rows.shape[-1]))
    return jnp.concatenate([cut[..., n, :, :] for n in range(times)], axis=-1)


def narrow(rows, width):
    times = rows.shape[-1] // width
    if times == 1:
        return rows
    return jnp.concatenate(
        [rows[..., n * width : (n + 1) * width] for n in range(times)], axis=-2
    )


def project_kernel(place_ref, n_ref, w_ref, c_ref, s1_ref, s2_ref, qt_ref, kt_ref, vt_ref, q_ref, k_ref, v_ref):
    wide = qt_ref.shape[0]
    heads = wide // HD
    made = nn(n_ref[...], w_ref[...])
    times = wide // LANES
    cos = jnp.concatenate([c_ref[...]] * times, axis=1)
    sin1 = jnp.concatenate([s1_ref[...]] * times, axis=1)
    sin2 = jnp.concatenate([s2_ref[...]] * times, axis=1)

    def turn(t):
        return (
            t * cos
            + pltpu.roll(t, wide - ROT // 2, 1) * sin1
            + pltpu.roll(t, ROT // 2, 1) * sin2
        )

    scale = HD**-0.5
    queries = turn(made[:, :wide]).astype(BF16).astype(F32) * scale
    keys = turn(made[:, wide : 2 * wide])
    values = made[:, 2 * wide :]
    for t_ref, h_ref, tile in (
        (qt_ref, q_ref, queries),
        (kt_ref, k_ref, keys),
        (vt_ref, v_ref, values),
    ):
        t_ref[...] = tile.T.astype(BF16)
        for h in range(heads):
            h_ref[h] = tile[:, h * HD : (h + 1) * HD].astype(BF16)


def project(normed, weights, tables, place, group):
    seq, d = normed.shape
    tile = seq // group
    wide = weights.shape[1] // 3
    heads = wide // HD
    flat = jax.ShapeDtypeStruct((wide, seq), BF16)
    split = jax.ShapeDtypeStruct((heads, seq, HD), BF16)
    flat_spec = pl.BlockSpec((wide, tile), lambda i, place: (0, i))
    split_spec = pl.BlockSpec((heads, tile, HD), lambda i, place: (0, i, 0))
    table_spec = pl.BlockSpec((tile, LANES), lambda i, place: (i, 0))
    return pl.pallas_call(
        project_kernel,
        out_shape=(flat,) * 3 + (split,) * 3,
        grid_spec=pltpu.PrefetchScalarGridSpec(
            num_scalar_prefetch=1,
            grid=(group,),
            in_specs=[
                pl.BlockSpec((tile, d), lambda i, place: (place[i], 0)),
                resident(weights.shape),
                table_spec,
                table_spec,
                table_spec,
            ],
            out_specs=(flat_spec,) * 3 + (split_spec,) * 3,
        ),
        compiler_params=params(),
        cost_estimate=cost(2 * seq * d * 3 * wide, seq * d * 2 + d * wide * 6 + 9 * wide * seq * 2),
        name="project",
    )(place, normed, weights, *tables)


def mask_scores(scores, start, key_base, query_base, diagonal):
    key_places = key_base + lax.broadcasted_iota(jnp.int32, scores.shape, 0)
    keep = key_places >= start
    if diagonal:
        query_places = query_base + lax.broadcasted_iota(jnp.int32, scores.shape, 1)
        keep = keep & (key_places <= query_places)
    return jnp.where(keep, scores, NEG_LARGE)


def attend_kernel(low_ref, start_ref, qt_ref, k_ref, vt_ref, ot_ref, lse_ref, m_ref, l_ref, acc_ref):
    block = qt_ref.shape[1]
    i = pl.program_id(1)
    queries = qt_ref[...]
    start = start_ref[...]

    def step(j, diagonal):
        base = pl.multiple_of(j * block, block)
        scores = nn(k_ref[0, pl.ds(base, block), :], queries)
        scores = mask_scores(scores, start, base, i * block, diagonal)
        peak = jnp.max(scores, axis=0, keepdims=True)
        values = vt_ref[:, pl.ds(base, block)]
        if diagonal:
            weights = jnp.exp(scores - peak)
            m_ref[...] = peak
            l_ref[...] = jnp.sum(weights, axis=0, keepdims=True)
            acc_ref[...] = nn(values, weights.astype(BF16))
        else:
            before = m_ref[...]
            peak = jnp.maximum(before, peak)
            shrink = jnp.exp(before - peak)
            weights = jnp.exp(scores - peak)
            m_ref[...] = peak
            l_ref[...] = l_ref[...] * shrink + jnp.sum(weights, axis=0, keepdims=True)
            acc_ref[...] = acc_ref[...] * shrink + nn(values, weights.astype(BF16))

    step(i, True)

    def body(j, carry):
        step(j, False)
        return carry

    lax.fori_loop(low_ref[i], i, body, 0)
    total = l_ref[...]
    ot_ref[...] = acc_ref[...] * (1.0 / total)
    lse_ref[0] = m_ref[...] + jnp.log(total)


def attend(low, start, qt, k, vt, block):
    wide, seq = qt.shape
    heads = wide // HD
    blocks = seq // block
    return pl.pallas_call(
        attend_kernel,
        out_shape=(
            jax.ShapeDtypeStruct((wide, seq), F32),
            jax.ShapeDtypeStruct((heads, 1, seq), F32),
        ),
        grid_spec=pltpu.PrefetchScalarGridSpec(
            num_scalar_prefetch=1,
            grid=(heads, blocks),
            in_specs=[
                pl.BlockSpec((1, block), lambda h, i, low: (0, i)),
                pl.BlockSpec((HD, block), lambda h, i, low: (h, i)),
                pl.BlockSpec((1, seq, HD), lambda h, i, low: (h, 0, 0)),
                pl.BlockSpec((HD, seq), lambda h, i, low: (h, 0)),
            ],
            out_specs=(
                pl.BlockSpec((HD, block), lambda h, i, low: (h, i)),
                pl.BlockSpec((1, 1, block), lambda h, i, low: (h, 0, i)),
            ),
            scratch_shapes=[
                pltpu.VMEM((1, block), F32),
                pltpu.VMEM((1, block), F32),
                pltpu.VMEM((HD, block), F32),
            ],
        ),
        compiler_params=params(),
        cost_estimate=cost(
            heads * seq * seq * 512, wide * seq * 12, heads * seq * seq // 2
        ),
        name="attend",
    )(low, start, qt, k, vt)


def attend_back_kernel(
    high_ref, start_ref, lse_ref, cos_ref, sin_ref, qt_ref, kt_ref, gt_ref, ot_ref, q_ref, k_ref, v_ref, g_ref,
    dqt_out, dkt_out, dvt_out, dqt_ref, dk_ref, dv_ref, delta_ref
):
    seq = qt_ref.shape[1]
    blocks = high_ref.shape[0]
    block = seq // blocks
    delta_ref[...] = jnp.sum(gt_ref[...].astype(F32) * ot_ref[...], axis=0, keepdims=True)
    dqt_ref[...] = jnp.zeros_like(dqt_ref)

    def pair(i, j, diagonal):
        qs = pl.ds(pl.multiple_of(i * block, block), block)
        ks = pl.ds(pl.multiple_of(j * block, block), block)
        scores = nn(k_ref[0, ks, :], qt_ref[:, qs])
        scores = mask_scores(scores, start_ref[:, qs], j * block, i * block, diagonal)
        probs = jnp.exp(scores - lse_ref[0, :, qs])
        grad_probs = nn(v_ref[0, ks, :], gt_ref[:, qs])
        grad_scores = (probs * (grad_probs - delta_ref[:, qs])).astype(BF16)
        dv = nn(probs.astype(BF16), g_ref[0, qs, :])
        dk = nn(grad_scores, q_ref[0, qs, :])
        if diagonal:
            dv_ref[ks, :] = dv
            dk_ref[ks, :] = dk
        else:
            dv_ref[ks, :] += dv
            dk_ref[ks, :] += dk
        dqt_ref[:, qs] += nn(kt_ref[:, ks], grad_scores)

    def keys(j, carry):
        pair(j, j, True)

        def queries(i, inner):
            pair(i, j, False)
            return inner

        lax.fori_loop(j + 1, high_ref[j], queries, 0)
        return carry

    lax.fori_loop(0, blocks, keys, 0)
    cos, sin = cos_ref[...], sin_ref[...]
    half = ROT // 2

    def store(out, t):
        a, b = t[:half], t[half:ROT]
        out[:half] = (a * cos + b * sin).astype(BF16)
        out[half:ROT] = (b * cos - a * sin).astype(BF16)
        out[ROT:] = t[ROT:].astype(BF16)

    store(dqt_out, dqt_ref[...] * (HD**-0.5))
    store(dkt_out, dk_ref[...].T)
    dvt_out[...] = dv_ref[...].T.astype(BF16)


def attend_back(high, start, lse, cos, sin, qt, kt, gt, ot, q, k, v, g):
    wide, seq = qt.shape
    heads = wide // HD
    flat = pl.BlockSpec((HD, seq), lambda h, high: (h, 0))
    split = pl.BlockSpec((1, seq, HD), lambda h, high: (h, 0, 0))
    row = pl.BlockSpec((1, seq), lambda h, high: (0, 0))
    table = pl.BlockSpec((ROT // 2, seq), lambda h, high: (0, 0))
    return pl.pallas_call(
        attend_back_kernel,
        out_shape=(jax.ShapeDtypeStruct((wide, seq), BF16),) * 3,
        grid_spec=pltpu.PrefetchScalarGridSpec(
            num_scalar_prefetch=1,
            grid=(heads,),
            in_specs=[
                row,
                pl.BlockSpec((1, 1, seq), lambda h, high: (h, 0, 0)),
                table,
                table,
                flat,
                flat,
                flat,
                flat,
                split,
                split,
                split,
                split,
            ],
            out_specs=(flat,) * 3,
            scratch_shapes=[
                pltpu.VMEM((HD, seq), F32),
                pltpu.VMEM((seq, HD), F32),
                pltpu.VMEM((seq, HD), F32),
                pltpu.VMEM((1, seq), F32),
            ],
        ),
        compiler_params=params(),
        cost_estimate=cost(heads * seq * seq * 1280, wide * seq * 24, heads * seq * seq // 2),
        name="attend_back",
    )(high, start, lse, cos, sin, qt, kt, gt, ot, q, k, v, g)


def feed_kernel(place_ref, n_ref, ot_ref, win_ref, bin_ref, wfc_ref, wout_ref, out_ref, hid_ref, slope_ref):
    pre = nn(n_ref[...], win_ref[...]) + bin_ref[...]
    root = math.sqrt(2.0 / math.pi)
    square = pre * pre
    bent = jnp.tanh(root * (pre + 0.044715 * (pre * square)))
    half = 0.5 * (1.0 + bent)
    hidden = (pre * half).astype(BF16)
    slope = half + 0.5 * pre * (1.0 - bent * bent) * (root * (1.0 + 0.134145 * square))
    hid_ref[...] = hidden
    slope_ref[...] = slope.astype(BF16)
    made = nn(hidden, wfc_ref[...]) + tn(ot_ref[...].astype(BF16), wout_ref[...])
    out_ref[...] = made.astype(BF16)


def feed(place, normed, ot, w_in, b_in, w_fc, w_out, group):
    seq, d = normed.shape
    tile = seq // group
    wide, units = ot.shape[0], w_in.shape[1]
    rows = pl.BlockSpec((tile, d), lambda i, place: (i, 0))
    unit_rows = pl.BlockSpec((tile, units), lambda i, place: (i, 0))
    return pl.pallas_call(
        feed_kernel,
        out_shape=(
            jax.ShapeDtypeStruct((seq, d), BF16),
            jax.ShapeDtypeStruct((seq, units), BF16),
            jax.ShapeDtypeStruct((seq, units), BF16),
        ),
        grid_spec=pltpu.PrefetchScalarGridSpec(
            num_scalar_prefetch=1,
            grid=(group,),
            in_specs=[
                rows,
                pl.BlockSpec((wide, tile), lambda i, place: (0, place[i])),
                resident(w_in.shape),
                resident(b_in.shape),
                resident(w_fc.shape),
                resident(w_out.shape),
            ],
            out_specs=(rows, unit_rows, unit_rows),
        ),
        compiler_params=params(),
        cost_estimate=cost(2 * seq * d * (2 * units + wide), seq * (d * 4 + units * 4 + wide * 4) + d * units * 4, seq * units),
        name="feed",
    )(place, normed, ot, w_in, b_in, w_fc, w_out)


def feed_back_kernel(
    place_ref, n_ref, g_ref, hid_ref, slope_ref, ot_ref, wint_ref, wfct_ref, woutt_ref,
    gn_ref, gt_ref, gs_ref, gwin_ref, gwfc_ref, gwout_ref, gbin_ref, ain_ref, afc_ref, aout_ref, ab_ref
):
    step = pl.program_id(0)
    grads = g_ref[...]
    grad_pre = nn(grads, wfct_ref[...]) * slope_ref[...].astype(F32)
    rounded = grad_pre.astype(BF16)
    gn_ref[...] = nn(rounded, wint_ref[...]).astype(BF16)
    grad_att = nn(grads, woutt_ref[...])
    gt_ref[...] = grad_att.T.astype(BF16)
    for h in range(gs_ref.shape[0]):
        gs_ref[h] = grad_att[:, h * HD : (h + 1) * HD].astype(BF16)
    part_in = tn(n_ref[...], rounded)
    part_fc = tn(hid_ref[...], grads)
    part_out = nn(ot_ref[...].astype(BF16), grads)
    part_b = jnp.sum(rounded.astype(F32), axis=0, keepdims=True)

    @pl.when(step == 0)
    def _():
        ain_ref[...] = part_in
        afc_ref[...] = part_fc
        aout_ref[...] = part_out
        ab_ref[...] = part_b

    @pl.when(step > 0)
    def _():
        ain_ref[...] += part_in
        afc_ref[...] += part_fc
        aout_ref[...] += part_out
        ab_ref[...] += part_b

    @pl.when(step == pl.num_programs(0) - 1)
    def _():
        gwin_ref[...] = ain_ref[...].astype(BF16)
        gwfc_ref[...] = afc_ref[...].astype(BF16)
        gwout_ref[...] = aout_ref[...].astype(BF16)
        gbin_ref[...] = ab_ref[...]


def feed_back(place, normed, grads, hidden, slope, ot, w_in_t, w_fc_t, w_out_t, group):
    seq, d = normed.shape
    tile = seq // group
    wide, units = ot.shape[0], hidden.shape[1]
    heads = wide // HD
    rows = pl.BlockSpec((tile, d), lambda i, place: (i, 0))
    unit_rows = pl.BlockSpec((tile, units), lambda i, place: (i, 0))
    turned = pl.BlockSpec((wide, tile), lambda i, place: (0, place[i]))
    return pl.pallas_call(
        feed_back_kernel,
        out_shape=(
            jax.ShapeDtypeStruct((seq, d), BF16),
            jax.ShapeDtypeStruct((wide, seq), BF16),
            jax.ShapeDtypeStruct((heads, seq, HD), BF16),
            jax.ShapeDtypeStruct((d, units), BF16),
            jax.ShapeDtypeStruct((units, d), BF16),
            jax.ShapeDtypeStruct((wide, d), BF16),
            jax.ShapeDtypeStruct((1, units), F32),
        ),
        grid_spec=pltpu.PrefetchScalarGridSpec(
            num_scalar_prefetch=1,
            grid=(group,),
            in_specs=[
                rows,
                rows,
                unit_rows,
                unit_rows,
                turned,
                resident(w_in_t.shape),
                resident(w_fc_t.shape),
                resident(w_out_t.shape),
            ],
            out_specs=(
                rows,
                turned,
                pl.BlockSpec((heads, tile, HD), lambda i, place: (0, place[i], 0)),
                resident((d, units)),
                resident((units, d)),
                resident((wide, d)),
                resident((1, units)),
            ),
            scratch_shapes=[
                pltpu.VMEM((d, units), F32),
                pltpu.VMEM((units, d), F32),
                pltpu.VMEM((wide, d), F32),
                pltpu.VMEM((1, units), F32),
            ],
        ),
        compiler_params=params(),
        cost_estimate=cost(2 * seq * d * (4 * units + 2 * wide), seq * (d * 6 + units * 4 + wide * 8) + d * units * 8),
        name="feed_back",
    )(place, normed, grads, hidden, slope, ot, w_in_t, w_fc_t, w_out_t)


def project_back_kernel(place_ref, dq_ref, dk_ref, dv_ref, n_ref, part_ref, wt_ref, gn_ref, gw_ref, acc_ref):
    step = pl.program_id(0)
    turned = jnp.concatenate([dq_ref[...], dk_ref[...], dv_ref[...]], axis=0)
    gn_ref[...] = (part_ref[...].astype(F32) + tn(turned, wt_ref[...])).astype(BF16)
    part = nn(turned, n_ref[...])

    @pl.when(step == 0)
    def _():
        acc_ref[...] = part

    @pl.when(step > 0)
    def _():
        acc_ref[...] += part

    @pl.when(step == pl.num_programs(0) - 1)
    def _():
        gw_ref[...] = acc_ref[...].astype(BF16)


def project_back(place, dq, dk, dv, normed, part, w_t, group):
    seq, d = normed.shape
    tile = seq // group
    wide = dq.shape[0]
    rows = pl.BlockSpec((tile, d), lambda i, place: (i, 0))
    turned = pl.BlockSpec((wide, tile), lambda i, place: (0, place[i]))
    return pl.pallas_call(
        project_back_kernel,
        out_shape=(
            jax.ShapeDtypeStruct((seq, d), BF16),
            jax.ShapeDtypeStruct((3 * wide, d), BF16),
        ),
        grid_spec=pltpu.PrefetchScalarGridSpec(
            num_scalar_prefetch=1,
            grid=(group,),
            in_specs=[turned, turned, turned, rows, rows, resident(w_t.shape)],
            out_specs=(rows, resident((3 * wide, d))),
            scratch_shapes=[pltpu.VMEM((3 * wide, d), F32)],
        ),
        compiler_params=params(),
        cost_estimate=cost(2 * seq * d * 6 * wide, seq * (d * 6 + wide * 6) + d * wide * 12),
        name="project_back",
    )(place, dq, dk, dv, normed, part, w_t)


def run_starts(segments):
    places = lax.broadcasted_iota(jnp.int32, segments.shape, 1)
    leading = jnp.ones_like(segments[:, :1])
    changes = jnp.concatenate(
        [leading, (segments[:, 1:] != segments[:, :-1]).astype(jnp.int32)], axis=1
    )
    starts = lax.cummax(places * changes, axis=1)
    return places, starts


def build(dp_size, tensor_size):
    def per_device(
        inputs, segments, norm_gain, norm_bias, w_qkv, w_out, w_in, b_in, w_fc, b_out, cotangent
    ):
        row_count, seq = segments.shape
        tokens, d = inputs.shape
        group = tensor_size // row_count
        half_rot = ROT // 2
        block = 512
        me = lax.axis_index("tensor")
        dp = lax.axis_index("dp")
        row = me // group
        spot = me % group
        other = [(i, (i + group) % tensor_size) for i in range(tensor_size)]
        place = jnp.bitwise_xor(jnp.arange(group, dtype=jnp.int32), spot)

        own_rows = inputs.astype(F32)
        centred = own_rows - jnp.mean(own_rows, axis=-1, keepdims=True)
        inv_std = lax.rsqrt(jnp.mean(centred * centred, axis=-1, keepdims=True) + EPSILON)
        unit_rows = centred * inv_std
        normed_own = (unit_rows * norm_gain + norm_bias).astype(BF16)

        dp_bits = bit_list(dp_size)

        def fetch(packed):
            sent = lax.dynamic_index_in_dim(packed, dp, 0, keepdims=False)
            got = lax.ppermute(sent, "tensor", other)
            return natural(gather_slots(got, "dp", dp_size, dp_bits[::-1]), dp)

        normed = gather_rows(normed_own, tensor_size, group)
        per_head = w_qkv.shape[2]
        qkv_other = fetch(w_qkv.reshape(dp_size, -1, per_head)).reshape(w_qkv.shape)
        units, wide = w_in.shape[1], w_out.shape[0]
        packed = jnp.concatenate(
            [
                widen(w_in.reshape(dp_size, -1, units), d),
                w_fc.reshape(dp_size, -1, d),
                w_out.reshape(dp_size, -1, d),
            ],
            axis=1,
        )
        n_in, n_fc = d * units // d // dp_size, units // dp_size
        b_in_other = lax.ppermute(b_in, "tensor", other)
        got = fetch(packed)
        w_in_other = narrow(got[:, :n_in], units).reshape(w_in.shape)
        w_fc_other = got[:, n_in : n_in + n_fc].reshape(w_fc.shape)
        w_out_other = got[:, n_in + n_fc :].reshape(w_out.shape)
        w_qkv_all = jnp.concatenate(
            [part[c] for c in range(3) for part in (w_qkv, qkv_other)], axis=1
        )
        w_in_all = jnp.concatenate([w_in, w_in_other], axis=1)
        w_fc_all = jnp.concatenate([w_fc, w_fc_other], axis=0)
        w_out_all = jnp.concatenate([w_out, w_out_other], axis=0)
        b_in_all = jnp.concatenate([b_in, b_in_other], axis=0)[None]

        segs = lax.dynamic_slice_in_dim(segments, row, 1, axis=0)
        places, starts = run_starts(segs)
        first_key = jnp.where(segs >= 0, starts, places)
        offsets = (places - starts).astype(F32)
        frequency = jnp.exp(
            lax.broadcasted_iota(F32, (half_rot,), 0) * (-2.0 * math.log(10000.0) / ROT)
        )
        angles = frequency[:, None] * offsets
        cos_t, sin_t = jnp.cos(angles), jnp.sin(angles)
        ones = jnp.ones((HD - ROT, seq), F32)
        none = jnp.zeros((half_rot, seq), F32)
        rest = jnp.zeros((HD - ROT, seq), F32)
        pair = LANES // HD
        tables = tuple(
            jnp.concatenate(parts * pair, axis=0).T
            for parts in ([cos_t, cos_t, ones], [-sin_t, none, rest], [none, sin_t, rest])
        )
        blocks = seq // block
        block_first = jnp.min(first_key.reshape(blocks, block), axis=1) // block
        low = block_first.astype(jnp.int32)
        reach = low[None, :] <= jnp.arange(blocks)[:, None]
        high = jnp.max(
            jnp.where(reach, jnp.arange(1, blocks + 1, dtype=jnp.int32)[None, :], 0), axis=1
        ).astype(jnp.int32)

        qt, kt, vt, q, k, v = project(normed, w_qkv_all, tables, place, group)
        ot, lse = attend(low, first_key, qt, k, vt, block)
        out_part, hidden, slope = feed(place, normed, ot, w_in_all, b_in_all, w_fc_all, w_out_all, group)
        grads = gather_rows(cotangent, tensor_size, group)
        branch_own = reduce_rows(out_part, tensor_size, group).astype(F32)
        output = (own_rows + branch_own + b_out).astype(BF16)

        gn_part, gt, g_heads, gw_in, gw_fc, gw_out, gb_in = feed_back(
            place, normed, grads, hidden, slope, ot, w_in_all.T, w_fc_all.T, w_out_all.T, group
        )
        dqt, dkt, dvt = attend_back(high, first_key, lse, cos_t, sin_t, qt, kt, gt, ot, q, k, v, g_heads)
        gn_all, gw_qkv = project_back(place, dqt, dkt, dvt, normed, gn_part, w_qkv_all.T, group)
        grad_norm_own = reduce_rows(gn_all, tensor_size, group).astype(F32)

        scaled = grad_norm_own * norm_gain
        grad_local = inv_std * (
            scaled
            - jnp.mean(scaled, axis=-1, keepdims=True)
            - unit_rows * jnp.mean(scaled * unit_rows, axis=-1, keepdims=True)
        )
        cotangent_f = cotangent.astype(F32)
        grad_inputs = cotangent_f + grad_local

        def settle(own, away):
            own_part = reduce_slots(to_slots(own, dp), "dp", dp_size, dp_bits)
            away_part = reduce_slots(to_slots(away, dp), "dp", dp_size, dp_bits)
            got = lax.ppermute(away_part, "tensor", other)
            total = (own_part.astype(F32) + got.astype(F32)).astype(BF16)
            return natural(gather_slots(total, "dp", dp_size, dp_bits[::-1]), dp)

        def pack(n):
            return jnp.concatenate(
                [
                    widen(gw_in[:, n * units : (n + 1) * units].reshape(dp_size, -1, units), d),
                    gw_fc[n * units : (n + 1) * units].reshape(dp_size, -1, d),
                    gw_out[n * wide : (n + 1) * wide].reshape(dp_size, -1, d),
                ],
                axis=1,
            )

        settled = settle(pack(0), pack(1))
        grad_in = narrow(settled[:, :n_in], units).reshape(w_in.shape).astype(F32)
        grad_fc = settled[:, n_in : n_in + n_fc].reshape(w_fc.shape).astype(F32)
        grad_out = settled[:, n_in + n_fc :].reshape(w_out.shape).astype(F32)
        qkv_parts = gw_qkv.reshape(3, 2, per_head, d)
        qkv_settled = settle(
            qkv_parts[:, 0].reshape(dp_size, -1, d), qkv_parts[:, 1].reshape(dp_size, -1, d)
        )
        grad_qkv = jnp.swapaxes(qkv_settled.reshape(3, per_head, d), 1, 2).astype(F32)

        def everywhere(vector):
            for axis, size in (("dp", dp_size), ("tensor", tensor_size)):
                for bit in bit_list(size):
                    vector = vector + lax.ppermute(vector, axis, [(i, i ^ bit) for i in range(size)])
            return vector

        bias_parts = jnp.zeros((tensor_size, units), F32)
        bias_parts = lax.dynamic_update_slice_in_dim(bias_parts, gb_in[:, :units], me, axis=0)
        bias_parts = lax.dynamic_update_slice_in_dim(
            bias_parts, gb_in[:, units:], (me + group) % tensor_size, axis=0
        )
        early = everywhere(
            jnp.concatenate(
                [jnp.sum(cotangent_f, axis=0, keepdims=True), bias_parts.reshape(-1, d)], axis=0
            )
        )
        grad_b_out = early[0]
        grad_b_in = lax.dynamic_slice_in_dim(early[1:].reshape(tensor_size, units), me, 1, axis=0)[0]
        late = everywhere(
            jnp.stack([jnp.sum(grad_norm_own * unit_rows, axis=0), jnp.sum(grad_norm_own, axis=0)])
        )
        return (
            output,
            grad_inputs,
            late[0],
            late[1],
            grad_qkv,
            grad_out,
            grad_in,
            grad_b_in,
            grad_fc,
            grad_b_out,
        )

    return per_device


def solution(mesh):
    tokens = P(("dp", "tensor"), None)
    return jax.shard_map(
        build(mesh.shape["dp"], mesh.shape["tensor"]),
        mesh=mesh,
        in_specs=(
            tokens,
            P("dp", None),
            P(),
            P(),
            P(None, None, "tensor"),
            P("tensor", None),
            P(None, "tensor"),
            P("tensor"),
            P("tensor", None),
            P(),
            tokens,
        ),
        out_specs=(
            tokens,
            tokens,
            P(),
            P(),
            P(None, None, "tensor"),
            P("tensor", None),
            P(None, "tensor"),
            P("tensor"),
            P("tensor", None),
            P(),
        ),
        check_vma=False,
    )
```

```python
import functools
import math

import jax
import jax.numpy as jnp
from jax import lax
from jax.experimental import pallas as pl
from jax.experimental.pallas import tpu as pltpu
from jax.sharding import PartitionSpec as P

HD = 64
ROT = 32
EPSILON = 1e-05
NEG_LARGE = -1e30
BF16 = jnp.bfloat16
F32 = jnp.float32
LANES = 128
VMEM_BYTES = 60 * 1024 * 1024


def nn(a, b):
    return lax.dot_general(a, b, (((1,), (0,)), ((), ())), preferred_element_type=F32)


def nt(a, b):
    return lax.dot_general(a, b, (((1,), (1,)), ((), ())), preferred_element_type=F32)


def tn(a, b):
    return lax.dot_general(a, b, (((0,), (0,)), ((), ())), preferred_element_type=F32)


def resident(shape):
    return pl.BlockSpec(shape, lambda *_: (0,) * len(shape), pipeline_mode=pl.Buffered(1))


def params():
    return pltpu.CompilerParams(vmem_limit_bytes=VMEM_BYTES)


def cost(flops, moved, trans=0):
    return pl.CostEstimate(flops=int(flops), bytes_accessed=int(moved), transcendentals=int(trans))


def bit_list(count):
    return [1 << n for n in range(count.bit_length() - 1)]


def swap(array, axis, size, bit):
    return lax.ppermute(array, axis, [(i, i ^ bit) for i in range(size)])


def tie(*groups):
    return lax.optimization_barrier(groups)


def halves_of(block):
    rows = block.shape[0] // 2
    return block[:rows], block[rows:]


def forwards(bits):
    steps = []
    for number in range(1, len(bits)):
        for half, order in enumerate((bits, bits[::-1])):
            for k in range(1, 2 ** len(bits)):
                if not any(k & bit for bit in order[number:]):
                    steps.append((number, half, k, k ^ order[number], order[number]))
    return steps


def gather_own(block, size, bits):
    return {bit: swap(block, "tensor", size, bit) for bit in bits}


def gather_rest(block, got, size, bits):
    parts = {(bit, half): part for bit in bits for half, part in enumerate(halves_of(got[bit]))}
    for _, half, k, made, bit in forwards(bits):
        parts[made, half] = swap(parts[k, half], "tensor", size, bit)
    whole = {0: (block,), **{bit: (got[bit],) for bit in bits}}
    return {
        k: whole[k] if k in whole else (parts[k, 0], parts[k, 1]) for k in range(2 ** len(bits))
    }


def add(a, b):
    return (a.astype(F32) + b.astype(F32)).astype(a.dtype)


def reduce_sends(pieces, size, bits, stage):
    return {
        (k, half): swap(pieces[made, half], "tensor", size, bit)
        for number, half, k, made, bit in reversed(forwards(bits))
        if number == stage
    }


def reduce_adds(pieces, got):
    return {key: add(pieces[key], got[key]) if key in got else pieces[key] for key in pieces}


def reduce_last(pieces, size, bits):
    return [
        swap(jnp.concatenate([pieces[bit, 0], pieces[bit, 1]], axis=0), "tensor", size, bit)
        for bit in bits
    ]


def reduce_total(pieces, got):
    total = jnp.concatenate([pieces[0, 0], pieces[0, 1]], axis=0).astype(F32)
    for part in got:
        total = total + part.astype(F32)
    return total


def gather_slots(mine, axis, size, bits):
    pieces = {0: mine}
    for bit in bits:
        for k in sorted(pieces):
            pieces[k ^ bit] = swap(pieces[k], axis, size, bit)
    return pieces


def natural(pieces, me):
    for bit in bit_list(len(pieces)):
        odd = (me & bit) != 0
        pieces = {k: jnp.where(odd, pieces[k ^ bit], pieces[k]) for k in pieces}
    return jnp.concatenate([pieces[k] for k in range(len(pieces))], axis=0)


def turn_rows(t, cos, sin):
    half = ROT // 2
    a, b = t[:half], t[half:ROT]
    return jnp.concatenate([a * cos - b * sin, b * cos + a * sin, t[ROT:]], axis=0)


def start_pieces(info_ref, slots, refs, tokens, buf_ref, sem):
    for (k, place), piece in zip(slots, refs):
        rows = piece.shape[0]
        base = pl.multiple_of(jnp.bitwise_xor(info_ref[0], k) * tokens + place * rows, rows)
        pltpu.make_async_copy(piece, buf_ref.at[pl.ds(base, rows), :], sem.at[k // 2]).start()


def listed(blocks):
    order = [(k, place) for k in sorted(blocks) for place in range(len(blocks[k]))]
    return order, [blocks[k][place] for k, place in order]


def wait_pieces(info_ref, step, tile, buf_ref, sem):
    which = jnp.bitwise_xor(step, info_ref[0] // 2)
    view = buf_ref.at[pl.ds(0, tile), :]
    pltpu.make_async_copy(view, view, sem.at[which]).wait()


def project_kernel(slots, info_ref, *refs):
    count = len(slots)
    pieces = refs[:count]
    wt_ref, cos_ref, sin_ref = refs[count : count + 3]
    n_ref, qt_ref, kt_ref, vt_ref, q_ref, k_ref, v_ref = refs[count + 3 : count + 10]
    step = pl.program_id(0)
    tile = n_ref.shape[0]
    wide = qt_ref.shape[0]
    buf_ref, sem = refs[count + 10 :]

    @pl.when(step == 0)
    def _():
        start_pieces(info_ref, slots, pieces, tile // 2, buf_ref, sem)

    wait_pieces(info_ref, step, tile, buf_ref, sem)
    normed = buf_ref[pl.ds(pl.multiple_of(step * tile, tile), tile), :]
    n_ref[...] = normed
    store_heads(wt_ref, normed, cos_ref, sin_ref, qt_ref, kt_ref, vt_ref, q_ref, k_ref, v_ref)


def project_more_kernel(n_ref, wt_ref, cos_ref, sin_ref, *outs):
    store_heads(wt_ref, n_ref[...], cos_ref, sin_ref, *outs)


def store_heads(wt_ref, normed, cos_ref, sin_ref, qt_ref, kt_ref, vt_ref, q_ref, k_ref, v_ref):
    wide = qt_ref.shape[0]
    made = nt(wt_ref[...], normed)
    cos, sin = cos_ref[...], sin_ref[...]
    scale = HD**-0.5
    for h in range(wide // HD):
        for which, t_ref, h_ref in ((0, qt_ref, q_ref), (1, kt_ref, k_ref), (2, vt_ref, v_ref)):
            base = which * wide + h * HD
            t = made[base : base + HD]
            if which < 2:
                t = turn_rows(t, cos, sin)
            t = t.astype(BF16)
            if which == 0:
                t = (t.astype(F32) * scale).astype(BF16)
            t_ref[h * HD : (h + 1) * HD, :] = t
            h_ref[h] = t.T


def project(info, blocks, weights, cos, sin):
    gathered = isinstance(blocks, dict)
    slots, pieces = listed(blocks) if gathered else ([], [blocks])
    if gathered:
        group = len(blocks)
        tokens, d = blocks[0][0].shape
        seq = group * tokens
        tile = 2 * tokens
    else:
        seq, d = blocks.shape
        tile = seq // 2
    wide = weights.shape[0] // 3
    heads = wide // HD
    flat = jax.ShapeDtypeStruct((wide, seq), BF16)
    split = jax.ShapeDtypeStruct((heads, seq, HD), BF16)
    flat_spec = pl.BlockSpec((wide, tile), lambda i, *_: (0, i))
    split_spec = pl.BlockSpec((heads, tile, HD), lambda i, *_: (0, i, 0))
    table = pl.BlockSpec((ROT // 2, tile), lambda i, *_: (0, i))
    rows = pl.BlockSpec((tile, d), lambda i, *_: (i, 0))
    row_out = ((jax.ShapeDtypeStruct((seq, d), BF16), rows),) if gathered else ()
    return pl.pallas_call(
        functools.partial(project_kernel, slots) if gathered else project_more_kernel,
        out_shape=tuple(shape for shape, _ in row_out) + (flat,) * 3 + (split,) * 3,
        grid_spec=pltpu.PrefetchScalarGridSpec(
            num_scalar_prefetch=1 if gathered else 0,
            grid=(seq // tile,),
            in_specs=([pl.BlockSpec(memory_space=pl.ANY)] * len(pieces) if gathered else [rows])
            + [resident(weights.shape), table, table],
            out_specs=tuple(spec for _, spec in row_out) + (flat_spec,) * 3 + (split_spec,) * 3,
            scratch_shapes=[
                pltpu.VMEM((seq, d), BF16),
                pltpu.SemaphoreType.DMA((seq // tile,)),
            ]
            if gathered
            else [],
        ),
        compiler_params=params(),
        cost_estimate=cost(2 * seq * d * 3 * wide, seq * d * 4 + d * wide * 6 + 9 * wide * seq * 2),
        name="project",
    )(*((info,) if gathered else ()), *pieces, weights, cos, sin)


def store_pieces(info_ref, step, made, outs):
    rows = outs[0].shape[0]
    odd = info_ref[0] % 2
    for pair in range(len(outs) // 4):
        for bit in range(2):

            @pl.when((step == pair) & (odd == bit))
            def _():
                for u in range(2):
                    for half in range(2):
                        base = (2 * (u ^ bit) + half) * rows
                        outs[4 * pair + 2 * u + half][...] = made[base : base + rows]


def feed_kernel(info_ref, n_ref, ot_own, ot_other, *refs):
    (win_own, win_other, b_own, b_other, fc_own, fc_other, wo_own, wo_other) = refs[:8]
    hid_ref, slope_ref = refs[8:10]
    outs = refs[10:]
    normed = n_ref[...]
    units = win_own.shape[1]
    root = math.sqrt(2.0 / math.pi)
    made = tn(ot_own[...].astype(BF16), wo_own[...]) + tn(ot_other[...].astype(BF16), wo_other[...])
    for number, (w_ref, b_ref, fc_ref) in enumerate(
        ((win_own, b_own, fc_own), (win_other, b_other, fc_other))
    ):
        pre = nn(normed, w_ref[...]) + b_ref[...]
        square = pre * pre
        half = 0.5 + 0.5 * jnp.tanh(pre * (root + (0.044715 * root) * square))
        gelu = pre * half
        slope = half + (gelu - gelu * half) * (2.0 * root + (0.26829 * root) * square)
        hidden = gelu.astype(BF16)
        hid_ref[:, number * units : (number + 1) * units] = hidden
        slope_ref[:, number * units : (number + 1) * units] = slope.astype(BF16)
        made = made + nn(hidden, fc_ref[...])
    store_pieces(info_ref, pl.program_id(0), made.astype(BF16), outs)


def paired(i, info):
    return jnp.bitwise_xor(i, info[0] // 2)


def feed(info, normed, ot, w_in, b_in, w_fc, w_out, group):
    seq, d = normed.shape
    rows = seq // group // 2
    tile = 4 * rows
    ph, units = ot[0].shape[0], 2 * w_in[0].shape[1]
    wide = 2 * ph
    unit_rows = pl.BlockSpec((tile, units), lambda i, info: (paired(i, info), 0))
    weights = [*w_in, *b_in, *w_fc, *w_out]
    made = pl.pallas_call(
        feed_kernel,
        out_shape=(jax.ShapeDtypeStruct((seq, units), BF16),) * 2
        + (jax.ShapeDtypeStruct((rows, d), BF16),) * (2 * group),
        grid_spec=pltpu.PrefetchScalarGridSpec(
            num_scalar_prefetch=1,
            grid=(seq // tile,),
            in_specs=[
                pl.BlockSpec((tile, d), lambda i, info: (paired(i, info), 0)),
                pl.BlockSpec((ph, tile), lambda i, info: (0, paired(i, info))),
                pl.BlockSpec((ph, tile), lambda i, info: (0, paired(i, info))),
            ]
            + [resident(w.shape) for w in weights],
            out_specs=(unit_rows,) * 2 + (resident((rows, d)),) * (2 * group),
        ),
        compiler_params=params(),
        cost_estimate=cost(2 * seq * d * (2 * units + wide), seq * (d * 4 + units * 4 + wide * 4) + d * units * 4, seq * units),
        name="feed",
    )(info, normed, *ot, *weights)
    return made[0], made[1], made[2:]


def feed_back_kernel(slots, info_ref, *refs):
    count = len(slots)
    pieces = refs[:count]
    n_ref, hid_ref, slope_ref, ot_own, ot_other = refs[count : count + 5]
    win_own, win_other, fc_own, fc_other, wo_own, wo_other = refs[count + 5 : count + 11]
    gn_ref, gt_ref, gs_ref, delta_ref, keep_ref, away_ref, gwout_ref, gbin_ref = refs[
        count + 11 : count + 19
    ]
    buf_ref, ain_ref, afc_ref, aout_ref, sem = refs[count + 19 :]
    step = pl.program_id(0)
    tile, d = n_ref.shape
    units = win_own.shape[1]
    ph = wo_own.shape[0]

    @pl.when(step == 0)
    def _():
        start_pieces(info_ref, slots, pieces, tile // 2, buf_ref, sem)

    wait_pieces(info_ref, step, tile, buf_ref, sem)
    grads = buf_ref[pl.ds(pl.multiple_of(step * tile, tile), tile), :]
    parts_out = []
    for number, (wo_ref, ot_ref) in enumerate(((wo_own, ot_own), (wo_other, ot_other))):
        grad_att = nt(wo_ref[...], grads).astype(BF16)
        gt_ref[number * ph : (number + 1) * ph, :] = grad_att
        ot = ot_ref[...]
        share = grad_att.astype(F32) * ot
        for h in range(ph // HD):
            head = slice(h * HD, (h + 1) * HD)
            gs_ref[number * (ph // HD) + h] = grad_att[head].T
            delta_ref[number * (ph // HD) + h] = jnp.sum(share[head], axis=0, keepdims=True)
        parts_out.append(nn(ot.astype(BF16), grads))
    part_out = jnp.concatenate(parts_out, axis=0)
    normed = n_ref[...]
    total = None
    sums = []
    for number, (w_ref, fc_ref) in enumerate(((win_own, fc_own), (win_other, fc_other))):
        cols = slice(number * units, (number + 1) * units)
        grad_pre = nt(grads, fc_ref[...]) * slope_ref[:, cols].astype(F32)
        rounded = grad_pre.astype(BF16)
        sums.append(jnp.sum(rounded.astype(F32), axis=0, keepdims=True))
        part = nt(rounded, w_ref[...])
        total = part if total is None else total + part
        part_in = tn(normed, rounded)
        part_fc = tn(hid_ref[:, cols], grads)

        @pl.when(step == 0)
        def _():
            ain_ref[:, cols] = part_in
            afc_ref[cols, :] = part_fc

        @pl.when(step > 0)
        def _():
            ain_ref[:, cols] += part_in
            afc_ref[cols, :] += part_fc

    gn_ref[...] = total.astype(BF16)
    part_b = jnp.concatenate(sums, axis=1)

    @pl.when(step == 0)
    def _():
        aout_ref[...] = part_out
        gbin_ref[...] = part_b

    @pl.when(step > 0)
    def _():
        aout_ref[...] += part_out
        gbin_ref[...] += part_b

    @pl.when(step == pl.num_programs(0) - 1)
    def _():
        gwout_ref[...] = aout_ref[...]
        dp_size = 2 * keep_ref.shape[0]
        rows = units // dp_size
        times = d // units
        for slot in range(dp_size):
            out = (keep_ref, away_ref)[slot % 2]
            index = jnp.bitwise_xor(info_ref[1], slot)
            for shard in range(2):
                for c in range(times):
                    base = pl.multiple_of(index * (d // dp_size) + c * rows, rows)
                    out[slot // 2, shard, :rows, c * units : (c + 1) * units] = ain_ref[
                        pl.ds(base, rows), shard * units : (shard + 1) * units
                    ].astype(BF16)
                base = pl.multiple_of(shard * units + index * rows, rows)
                out[slot // 2, shard, rows:, :] = afc_ref[pl.ds(base, rows), :].astype(BF16)


def feed_back(info, blocks, normed, hidden, slope, ot, w_in, w_fc, w_out, dp_size):
    seq, d = normed.shape
    group = len(blocks)
    slots, pieces = listed(blocks)
    tile = 2 * seq // group
    ph, units = ot[0].shape[0], hidden.shape[1]
    wide = 2 * ph
    heads = wide // HD
    rows = pl.BlockSpec((tile, d), lambda i, info: (i, 0))
    unit_rows = pl.BlockSpec((tile, units), lambda i, info: (i, 0))
    turned = pl.BlockSpec((wide, tile), lambda i, info: (0, i))
    half_turned = pl.BlockSpec((ph, tile), lambda i, info: (0, i))
    packed = (dp_size // 2, 2, units // dp_size, d)
    weights = [*w_in, *w_fc, *w_out]
    return pl.pallas_call(
        functools.partial(feed_back_kernel, slots),
        out_shape=(
            jax.ShapeDtypeStruct((seq, d), BF16),
            jax.ShapeDtypeStruct((wide, seq), BF16),
            jax.ShapeDtypeStruct((heads, seq, HD), BF16),
            jax.ShapeDtypeStruct((heads, 1, seq), F32),
            jax.ShapeDtypeStruct(packed, BF16),
            jax.ShapeDtypeStruct(packed, BF16),
            jax.ShapeDtypeStruct((wide, d), F32),
            jax.ShapeDtypeStruct((1, units), F32),
        ),
        grid_spec=pltpu.PrefetchScalarGridSpec(
            num_scalar_prefetch=1,
            grid=(seq // tile,),
            in_specs=[pl.BlockSpec(memory_space=pl.ANY)] * len(pieces)
            + [rows, unit_rows, unit_rows, half_turned, half_turned]
            + [resident(w.shape) for w in weights],
            out_specs=(
                rows,
                turned,
                pl.BlockSpec((heads, tile, HD), lambda i, info: (0, i, 0)),
                pl.BlockSpec((heads, 1, tile), lambda i, info: (0, 0, i)),
                resident(packed),
                resident(packed),
                resident((wide, d)),
                resident((1, units)),
            ),
            scratch_shapes=[
                pltpu.VMEM((seq, d), BF16),
                pltpu.VMEM((d, units), F32),
                pltpu.VMEM((units, d), F32),
                pltpu.VMEM((wide, d), F32),
                pltpu.SemaphoreType.DMA((group // 2,)),
            ],
        ),
        compiler_params=params(),
        cost_estimate=cost(2 * seq * d * (4 * units + 2 * wide), seq * (d * 6 + units * 4 + wide * 8) + d * units * 8),
        name="feed_back",
    )(info, *pieces, normed, hidden, slope, *ot, *weights)


def project_back_kernel(count, info_ref, *refs):
    turned_refs, refs = refs[: 3 * count], refs[3 * count :]
    (n_ref, part_ref, wt_own, wt_other, gwout_ref), refs = refs[:5], refs[5:]
    keep_ref, away_ref, sum_ref = refs[:3]
    outs, acc_ref = refs[3:-1], refs[-1]
    step = pl.program_id(0)
    wide, d = gwout_ref.shape
    turned = jnp.concatenate([ref[...] for ref in turned_refs], axis=0)
    normed = n_ref[...]
    ph = wide // 2
    made = part_ref[...].astype(F32)
    for c in range(3):
        for shard, w_ref in enumerate((wt_own, wt_other)):
            base = c * wide + shard * ph
            made = made + tn(turned[base : base + ph], w_ref[c * ph : (c + 1) * ph])
    store_pieces(info_ref, step, made.astype(BF16), outs)
    sums = jnp.concatenate(
        [
            jnp.sum(made * normed.astype(F32), axis=0, keepdims=True),
            jnp.sum(made, axis=0, keepdims=True),
        ],
        axis=0,
    )
    part = nn(turned, normed)

    @pl.when(step == 0)
    def _():
        acc_ref[: 3 * wide, :] = part
        acc_ref[3 * wide :, :] = gwout_ref[...]
        sum_ref[...] = sums

    @pl.when(step > 0)
    def _():
        acc_ref[: 3 * wide, :] += part
        sum_ref[...] += sums

    @pl.when(step == pl.num_programs(0) - 1)
    def _():
        dp_size = 2 * keep_ref.shape[0]
        rows = keep_ref.shape[2]
        each = dp_size // 4
        for slot in range(dp_size):
            out = (keep_ref, away_ref)[slot % 2]
            index = jnp.bitwise_xor(info_ref[1], slot)
            for shard in range(2):
                base = (index // each) * wide + shard * (wide // 2) + (index % each) * rows
                out[slot // 2, shard] = acc_ref[
                    pl.ds(pl.multiple_of(base, rows), rows), :
                ].astype(BF16)


def project_back(info, turned, normed, part, w_t, gw_out, group, dp_size):
    seq, d = normed.shape
    rows = seq // group // 2
    tile = 4 * rows
    wide = gw_out.shape[0]
    tile_rows = pl.BlockSpec((tile, d), lambda i, info: (paired(i, info), 0))
    packed = (dp_size // 2, 2, 2 * wide // dp_size, d)
    made = pl.pallas_call(
        functools.partial(project_back_kernel, len(turned) // 3),
        out_shape=(
            jax.ShapeDtypeStruct(packed, BF16),
            jax.ShapeDtypeStruct(packed, BF16),
            jax.ShapeDtypeStruct((2, d), F32),
        )
        + (jax.ShapeDtypeStruct((rows, d), BF16),) * (2 * group),
        grid_spec=pltpu.PrefetchScalarGridSpec(
            num_scalar_prefetch=1,
            grid=(seq // tile,),
            in_specs=[
                pl.BlockSpec((part.shape[0], tile), lambda i, info: (0, paired(i, info)))
                for part in turned
            ]
            + [
                tile_rows,
                tile_rows,
                resident(w_t[0].shape),
                resident(w_t[1].shape),
                resident(gw_out.shape),
            ],
            out_specs=(resident(packed), resident(packed), resident((2, d)))
            + (resident((rows, d)),) * (2 * group),
            scratch_shapes=[pltpu.VMEM((4 * wide, d), F32)],
        ),
        compiler_params=params(),
        cost_estimate=cost(2 * seq * d * 6 * wide, seq * (d * 6 + wide * 6) + d * wide * 12),
        name="project_back",
    )(info, *turned, normed, part, *w_t, gw_out)
    return made[0], made[1], made[2], made[3:]


def finish_feed_kernel(info_ref, *refs):
    pieces, (gin_ref, gfc_ref) = refs[:-2], refs[-2:]
    rows, d = gfc_ref.shape
    units = gin_ref.shape[1]
    for slot, piece in enumerate(pieces):

        @pl.when(pl.program_id(0) == slot)
        def _():
            for c in range(d // units):
                gin_ref[c * rows : (c + 1) * rows, :] = piece[
                    :rows, c * units : (c + 1) * units
                ].astype(F32)
            gfc_ref[...] = piece[rows:, :].astype(F32)


def finish_feed(info, pieces, units):
    count = len(pieces)
    d = pieces[0].shape[1]
    index = lambda i, info: (jnp.bitwise_xor(i, info[1]), 0)
    return pl.pallas_call(
        finish_feed_kernel,
        out_shape=(jax.ShapeDtypeStruct((d, units), F32), jax.ShapeDtypeStruct((units, d), F32)),
        grid_spec=pltpu.PrefetchScalarGridSpec(
            num_scalar_prefetch=1,
            grid=(count,),
            in_specs=[resident(pieces[0].shape)] * count,
            out_specs=(
                pl.BlockSpec((d // count, units), index),
                pl.BlockSpec((units // count, d), index),
            ),
        ),
        compiler_params=params(),
        cost_estimate=cost(0, d * units * 12),
        name="finish_feed",
    )(info, *pieces)


def finish_project_kernel(info_ref, *refs):
    pieces, (gqkv_ref, gout_ref) = refs[:-2], refs[-2:]
    index = pl.program_id(0)
    slot_now = jnp.bitwise_xor(index, info_ref[1])
    for slot, piece in enumerate(pieces):

        @pl.when((slot_now == slot) & (index < 3))
        def _():
            gqkv_ref[0] = piece[...].astype(F32).T

        @pl.when((slot_now == slot) & (index == 3))
        def _():
            gout_ref[...] = piece[...].astype(F32)


def finish_project(info, pieces):
    rows, d = pieces[0].shape
    return pl.pallas_call(
        finish_project_kernel,
        out_shape=(jax.ShapeDtypeStruct((3, d, rows), F32), jax.ShapeDtypeStruct((rows, d), F32)),
        grid_spec=pltpu.PrefetchScalarGridSpec(
            num_scalar_prefetch=1,
            grid=(4,),
            in_specs=[resident((rows, d))] * 4,
            out_specs=(
                pl.BlockSpec((1, d, rows), lambda i, info: (jnp.minimum(i, 2), 0, 0)),
                resident((rows, d)),
            ),
        ),
        compiler_params=params(),
        cost_estimate=cost(0, d * rows * 24),
        name="finish_project",
    )(info, *pieces)


def mask_scores(scores, start, key_base, query_base, diagonal):
    key_places = key_base + lax.broadcasted_iota(jnp.int32, scores.shape, 0)
    keep = key_places >= start
    if diagonal:
        query_places = query_base + lax.broadcasted_iota(jnp.int32, scores.shape, 1)
        keep = keep & (key_places <= query_places)
    return jnp.where(keep, scores, NEG_LARGE)


def attend_kernel(low_ref, start_ref, qt_ref, k_ref, vt_ref, ot_ref, lse_ref, m_ref, l_ref, acc_ref):
    block = qt_ref.shape[1]
    i = pl.program_id(1)
    queries = qt_ref[...]
    start = start_ref[...]

    def step(j, diagonal):
        base = pl.multiple_of(j * block, block)
        scores = nn(k_ref[0, pl.ds(base, block), :], queries)
        scores = mask_scores(scores, start, base, i * block, diagonal)
        peak = jnp.max(scores, axis=0, keepdims=True)
        values = vt_ref[:, pl.ds(base, block)]
        if diagonal:
            weights = jnp.exp(scores - peak)
            m_ref[...] = peak
            l_ref[...] = jnp.sum(weights, axis=0, keepdims=True)
            acc_ref[...] = nn(values, weights.astype(BF16))
        else:
            before = m_ref[...]
            peak = jnp.maximum(before, peak)
            shrink = jnp.exp(before - peak)
            weights = jnp.exp(scores - peak)
            m_ref[...] = peak
            l_ref[...] = l_ref[...] * shrink + jnp.sum(weights, axis=0, keepdims=True)
            acc_ref[...] = acc_ref[...] * shrink + nn(values, weights.astype(BF16))

    step(i, True)

    def body(j, carry):
        step(j, False)
        return carry

    lax.fori_loop(low_ref[i], i, body, 0)
    total = l_ref[...]
    ot_ref[...] = acc_ref[...] * (1.0 / total)
    lse_ref[0] = m_ref[...] + jnp.log(total)


def attend(low, start, qt, k, vt, block, base, heads):
    seq = qt.shape[1]
    blocks = seq // block
    return pl.pallas_call(
        attend_kernel,
        out_shape=(
            jax.ShapeDtypeStruct((heads * HD, seq), F32),
            jax.ShapeDtypeStruct((heads, 1, seq), F32),
        ),
        grid_spec=pltpu.PrefetchScalarGridSpec(
            num_scalar_prefetch=1,
            grid=(heads, blocks),
            in_specs=[
                pl.BlockSpec((1, block), lambda h, i, low: (0, i)),
                pl.BlockSpec((HD, block), lambda h, i, low: (base + h, i)),
                pl.BlockSpec((1, seq, HD), lambda h, i, low: (base + h, 0, 0)),
                pl.BlockSpec((HD, seq), lambda h, i, low: (base + h, 0)),
            ],
            out_specs=(
                pl.BlockSpec((HD, block), lambda h, i, low: (h, i)),
                pl.BlockSpec((1, 1, block), lambda h, i, low: (h, 0, i)),
            ),
            scratch_shapes=[
                pltpu.VMEM((1, block), F32),
                pltpu.VMEM((1, block), F32),
                pltpu.VMEM((HD, block), F32),
            ],
        ),
        compiler_params=params(),
        cost_estimate=cost(heads * seq * seq * 512, heads * seq * HD * 12, heads * seq * seq // 2),
        name="attend",
    )(low, start, qt, k, vt)


def attend_back_kernel(
    high_ref, start_ref, lse_ref, delta_ref, cos_ref, sin_ref, qt_ref, kt_ref, gt_ref, q_ref, k_ref, v_ref, g_ref,
    dqt_out, dkt_out, dvt_out, dqt_ref, dk_ref, dv_ref
):
    seq = qt_ref.shape[1]
    blocks = high_ref.shape[0]
    block = seq // blocks
    dqt_ref[...] = jnp.zeros_like(dqt_ref)

    def pair(i, j, diagonal):
        qs = pl.ds(pl.multiple_of(i * block, block), block)
        ks = pl.ds(pl.multiple_of(j * block, block), block)
        scores = nn(k_ref[0, ks, :], qt_ref[:, qs])
        scores = mask_scores(scores, start_ref[:, qs], j * block, i * block, diagonal)
        probs = jnp.exp(scores - lse_ref[0, :, qs])
        grad_probs = nn(v_ref[0, ks, :], gt_ref[:, qs])
        grad_scores = (probs * (grad_probs - delta_ref[0, :, qs])).astype(BF16)
        dv = nn(probs.astype(BF16), g_ref[0, qs, :])
        dk = nn(grad_scores, q_ref[0, qs, :])
        if diagonal:
            dv_ref[ks, :] = dv
            dk_ref[ks, :] = dk
        else:
            dv_ref[ks, :] += dv
            dk_ref[ks, :] += dk
        dqt_ref[:, qs] += nn(kt_ref[:, ks], grad_scores)

    def keys(j, carry):
        pair(j, j, True)

        def queries(i, inner):
            pair(i, j, False)
            return inner

        lax.fori_loop(j + 1, high_ref[j], queries, 0)
        return carry

    lax.fori_loop(0, blocks, keys, 0)
    cos, sin = cos_ref[...], sin_ref[...]
    half = ROT // 2

    def store(out, t):
        a, b = t[:half], t[half:ROT]
        out[:half] = (a * cos + b * sin).astype(BF16)
        out[half:ROT] = (b * cos - a * sin).astype(BF16)
        out[ROT:] = t[ROT:].astype(BF16)

    store(dqt_out, dqt_ref[...] * (HD**-0.5))
    store(dkt_out, dk_ref[...].T)
    dvt_out[...] = dv_ref[...].T.astype(BF16)


def attend_back(high, start, lse, delta, cos, sin, qt, kt, gt, q, k, v, g, base, local, heads):
    seq = qt.shape[1]
    flat = pl.BlockSpec((HD, seq), lambda h, high: (local + h, 0))
    split = pl.BlockSpec((1, seq, HD), lambda h, high: (local + h, 0, 0))
    both_flat = pl.BlockSpec((HD, seq), lambda h, high: (base + h, 0))
    both_split = pl.BlockSpec((1, seq, HD), lambda h, high: (base + h, 0, 0))
    row = pl.BlockSpec((1, seq), lambda h, high: (0, 0))
    head_row = pl.BlockSpec((1, 1, seq), lambda h, high: (base + h, 0, 0))
    own_row = pl.BlockSpec((1, 1, seq), lambda h, high: (local + h, 0, 0))
    table = pl.BlockSpec((ROT // 2, seq), lambda h, high: (0, 0))
    return pl.pallas_call(
        attend_back_kernel,
        out_shape=(jax.ShapeDtypeStruct((heads * HD, seq), BF16),) * 3,
        grid_spec=pltpu.PrefetchScalarGridSpec(
            num_scalar_prefetch=1,
            grid=(heads,),
            in_specs=[row, own_row, head_row, table, table]
            + [flat, flat, both_flat]
            + [split, split, split, both_split],
            out_specs=(pl.BlockSpec((HD, seq), lambda h, high: (h, 0)),) * 3,
            scratch_shapes=[
                pltpu.VMEM((HD, seq), F32),
                pltpu.VMEM((seq, HD), F32),
                pltpu.VMEM((seq, HD), F32),
            ],
        ),
        compiler_params=params(),
        cost_estimate=cost(heads * seq * seq * 1280, heads * HD * seq * 24, heads * seq * seq // 2),
        name="attend_back",
    )(high, start, lse, delta, cos, sin, qt, kt, gt, q, k, v, g)


def run_starts(segments):
    places = lax.broadcasted_iota(jnp.int32, segments.shape, 1)
    leading = jnp.ones_like(segments[:, :1])
    changes = jnp.concatenate(
        [leading, (segments[:, 1:] != segments[:, :-1]).astype(jnp.int32)], axis=1
    )
    starts = lax.cummax(places * changes, axis=1)
    return places, starts


def build(dp_size, tensor_size):
    def per_device(
        inputs, segments, norm_gain, norm_bias, w_qkv, w_out, w_in, b_in, w_fc, b_out, cotangent
    ):
        row_count, seq = segments.shape
        tokens, d = inputs.shape
        group = tensor_size // row_count
        half_rot = ROT // 2
        block = 512
        me = lax.axis_index("tensor")
        dp = lax.axis_index("dp")
        row = me // group
        info = jnp.stack([me % group, dp]).astype(jnp.int32)
        other = [(i, (i + group) % tensor_size) for i in range(tensor_size)]
        bits = bit_list(group)
        dp_bits = bit_list(dp_size)
        def normalize(rows):
            rows = rows.astype(F32)
            centred = rows - jnp.mean(rows, axis=-1, keepdims=True)
            inv_std = lax.rsqrt(jnp.mean(centred * centred, axis=-1, keepdims=True) + EPSILON)
            return centred * inv_std, inv_std

        normed_own = (normalize(inputs)[0] * norm_gain + norm_bias).astype(BF16)
        n_got = gather_own(normed_own, tensor_size, bits)

        def slice_of(indexed):
            return lax.dynamic_index_in_dim(indexed, dp, 0, keepdims=False)

        def fetch(part):
            return lax.ppermute(part, "tensor", other)

        def share(got):
            return gather_slots(got, "dp", dp_size, dp_bits[::-1])

        def rows_of(pieces, start, stop):
            return natural({k: pieces[k][start:stop] for k in pieces}, dp)

        units, per_head = w_in.shape[1], w_qkv.shape[2]
        shard_heads = per_head // HD
        fc_rows = units // dp_size
        qkv_slice = slice_of(w_qkv.reshape(dp_size, -1, per_head))
        in_slice = slice_of(w_in.reshape(dp_size, -1, units))
        fc_slice = jnp.concatenate(
            [slice_of(w_fc.reshape(dp_size, -1, d)), slice_of(w_out.reshape(dp_size, -1, d))], axis=0
        )
        wt_own = jnp.concatenate([w_qkv[c].T for c in range(3)], axis=0)

        segs = lax.dynamic_slice_in_dim(segments, row, 1, axis=0)
        places, starts = run_starts(segs)
        first_key = jnp.where(segs >= 0, starts, places)
        offsets = (places - starts).astype(F32)
        frequency = jnp.exp(
            lax.broadcasted_iota(F32, (half_rot,), 0) * (-2.0 * math.log(10000.0) / ROT)
        )
        angles = frequency[:, None] * offsets
        cos_t, sin_t = jnp.cos(angles), jnp.sin(angles)
        blocks = seq // block
        low = (jnp.min(first_key.reshape(blocks, block), axis=1) // block).astype(jnp.int32)
        reach = low[None, :] <= jnp.arange(blocks)[:, None]
        high = jnp.max(
            jnp.where(reach, jnp.arange(1, blocks + 1, dtype=jnp.int32)[None, :], 0), axis=1
        ).astype(jnp.int32)

        prepared = (wt_own, cos_t, sin_t, first_key, low, high)
        n_got, (qkv_slice, in_slice, fc_slice), prepared = tie(
            n_got, (qkv_slice, in_slice, fc_slice), prepared
        )
        wt_own, cos_t, sin_t, first_key, low, high = prepared
        n_blocks = gather_rest(normed_own, n_got, tensor_size, bits)
        qkv_got = fetch(qkv_slice)
        n_blocks, (in_slice, fc_slice, cot) = tie(n_blocks, (in_slice, fc_slice, cotangent))
        in_got, fc_got, b_in_other = fetch(in_slice), fetch(fc_slice), fetch(b_in)
        g_got = gather_own(cot, tensor_size, bits)

        made = project(info, n_blocks, wt_own, cos_t, sin_t)
        made, qkv_got = tie(made, qkv_got)
        normed, own = made[0], made[1:]
        qkv_pieces = share(qkv_got)
        ot_own, lse_own = attend(low, first_key, own[0], own[4], own[2], block, 0, shard_heads)
        (ot_own, lse_own), qkv_pieces, in_got, normed = tie(
            (ot_own, lse_own), qkv_pieces, in_got, normed
        )
        qkv_other = rows_of(qkv_pieces, 0, None).reshape(w_qkv.shape)
        wt_other = jnp.concatenate([qkv_other[c].T for c in range(3)], axis=0)
        in_pieces = share(in_got)
        rest = project(None, normed, wt_other, cos_t, sin_t)
        rest, in_pieces, fc_got, g_got = tie(rest, in_pieces, fc_got, g_got)
        fc_pieces = share(fc_got)
        g_blocks = gather_rest(cot, g_got, tensor_size, bits)
        ot_other, lse_other = attend(low, first_key, rest[0], rest[4], rest[2], block, 0, shard_heads)
        (ot_other, lse_other), in_pieces, fc_pieces = tie((ot_other, lse_other), in_pieces, fc_pieces)
        w_in_other = rows_of(in_pieces, 0, None)
        w_fc_other = rows_of(fc_pieces, 0, fc_rows)
        w_out_other = rows_of(fc_pieces, fc_rows, None)
        ot = (ot_own, ot_other)
        w_in_both, w_fc_both, w_out_both = (w_in, w_in_other), (w_fc, w_fc_other), (w_out, w_out_other)
        hidden, slope, out_pieces = feed(
            info, normed, ot, w_in_both, (b_in[None], b_in_other[None]), w_fc_both, w_out_both, group
        )

        def by_slot(pieces):
            return {(k, half): pieces[2 * k + half] for k in range(group) for half in range(2)}

        last_stage = len(bits) - 1
        out_parts = by_slot(out_pieces)
        out_got = reduce_sends(out_parts, tensor_size, bits, last_stage)
        made = feed_back(
            info, g_blocks, normed, hidden, slope, ot, w_in_both, w_fc_both, w_out_both, dp_size
        )
        made, out_got = tie(made, out_got)
        gn_part, gt, g_heads, delta, keep1, away1, gw_out, gb_in = made
        out_parts = reduce_adds(out_parts, out_got)
        for stage in range(last_stage - 1, 0, -1):
            out_parts = reduce_adds(out_parts, reduce_sends(out_parts, tensor_size, bits, stage))
        out_got = reduce_last(out_parts, tensor_size, bits)

        def settle_split(keep, got):
            return {
                2 * j: tuple(add(keep[j, s], got[j, s]) for s in range(2))
                for j in range(keep.shape[0])
            }

        def settle_dp(parts, bit):
            got = {
                k ^ bit: [swap(part, "dp", dp_size, bit) for part in parts[k]]
                for k in sorted(parts)
                if k & bit
            }
            return {k: parts[k] for k in got}, got

        def settle_add(kept, got):
            return {k: tuple(add(a, b) for a, b in zip(kept[k], got[k])) for k in kept}

        def settle_rest(parts, got):
            for bit in dp_bits[2:]:
                parts, got = settle_dp(settle_add(parts, got), bit)
            own_sum, other_sum = settle_add(parts, got)[0]
            return own_sum, fetch(other_sum)

        def settle_share(total):
            pieces = gather_slots(total, "dp", dp_size, dp_bits[::-1])
            return [pieces[k] for k in range(dp_size)]

        def heads_back(shard, base, count):
            qt, kt, vt, q, k, v = (own, rest)[shard]
            return attend_back(
                high, first_key, (lse_own, lse_other)[shard], delta, cos_t, sin_t, qt, kt, gt, q, k, v, g_heads,
                shard * shard_heads + base, base, count
            )

        got1 = swap(away1, "dp", dp_size, dp_bits[0])
        turned = [heads_back(0, 0, shard_heads)]
        turned, got1, out_got, gt = tie(turned, got1, out_got, gt)
        kept1, got1 = settle_dp(settle_split(keep1, got1), dp_bits[1])
        output = (inputs.astype(F32) + reduce_total(out_parts, out_got) + b_out).astype(BF16)
        turned.append(heads_back(1, 0, shard_heads))
        turned, got1, output = tie(turned, got1, output)
        own1, other1 = settle_rest(kept1, got1)
        keep2, away2, sums, gn_pieces = project_back(
            info,
            [parts[c] for c in range(3) for parts in turned],
            normed,
            gn_part,
            (wt_own, wt_other),
            gw_out,
            group,
            dp_size,
        )
        gn_parts = by_slot(gn_pieces)
        for stage in range(last_stage, 0, -1):
            gn_parts = reduce_adds(gn_parts, reduce_sends(gn_parts, tensor_size, bits, stage))
        gn_got = reduce_last(gn_parts, tensor_size, bits)
        got2 = swap(away2, "dp", dp_size, dp_bits[0])
        own2, other2 = settle_rest(*settle_dp(settle_split(keep2, got2), dp_bits[1]))
        total1 = add(own1, other1)
        total2 = add(own2, other2)

        unit_rows, inv_std = normalize(inputs)
        grad_norm_own = reduce_total(gn_parts, gn_got)
        scaled = grad_norm_own * norm_gain
        grad_local = inv_std * (
            scaled
            - jnp.mean(scaled, axis=-1, keepdims=True)
            - unit_rows * jnp.mean(scaled * unit_rows, axis=-1, keepdims=True)
        )
        cotangent_f = cotangent.astype(F32)
        grad_inputs = cotangent_f + grad_local

        grad_in, grad_fc = finish_feed(info, settle_share(total1), units)
        pieces2 = settle_share(total2)
        if dp_size == 4 and per_head % LANES == 0:
            grad_qkv, grad_out = finish_project(info, pieces2)
        else:
            stacked = natural(dict(enumerate(pieces2)), dp)
            grad_qkv = jnp.swapaxes(
                stacked[: 3 * per_head].reshape(3, per_head, d), 1, 2
            ).astype(F32)
            grad_out = stacked[3 * per_head :].astype(F32)

        bias_parts = jnp.zeros((tensor_size, units), F32)
        bias_parts = lax.dynamic_update_slice_in_dim(bias_parts, gb_in[:, :units], me, axis=0)
        bias_parts = lax.dynamic_update_slice_in_dim(
            bias_parts, gb_in[:, units:], (me + group) % tensor_size, axis=0
        )
        total = jnp.concatenate(
            [sums, jnp.sum(cotangent_f, axis=0, keepdims=True), bias_parts.reshape(-1, d)], axis=0
        )
        for axis, size in (("dp", dp_size), ("tensor", tensor_size)):
            for bit in bit_list(size):
                total = total + swap(total, axis, size, bit)
        grad_bias = total[1]
        grad_gain = (total[0] - norm_bias * grad_bias) / norm_gain
        grad_b_out = total[2]
        grad_b_in = lax.dynamic_slice_in_dim(total[3:].reshape(tensor_size, units), me, 1, axis=0)[0]
        return (
            output,
            grad_inputs,
            grad_gain,
            grad_bias,
            grad_qkv,
            grad_out,
            grad_in,
            grad_b_in,
            grad_fc,
            grad_b_out,
        )

    return per_device


def solution(mesh):
    tokens = P(("dp", "tensor"), None)
    return jax.shard_map(
        build(mesh.shape["dp"], mesh.shape["tensor"]),
        mesh=mesh,
        in_specs=(
            tokens,
            P("dp", None),
            P(),
            P(),
            P(None, None, "tensor"),
            P("tensor", None),
            P(None, "tensor"),
            P("tensor"),
            P("tensor", None),
            P(),
            tokens,
        ),
        out_specs=(
            tokens,
            tokens,
            P(),
            P(),
            P(None, None, "tensor"),
            P("tensor", None),
            P(None, "tensor"),
            P("tensor"),
            P("tensor", None),
            P(),
        ),
        check_vma=False,
    )
```

```python
import functools
import math

import jax
import jax.numpy as jnp
from jax import lax
from jax.experimental import pallas as pl
from jax.experimental.pallas import tpu as pltpu
from jax.sharding import PartitionSpec as P

HD = 64
ROT = 32
EPSILON = 1e-05
NEG_LARGE = -1e30
BF16 = jnp.bfloat16
F32 = jnp.float32
LANES = 128
MIB = 1024 * 1024


def nn(a, b):
    return lax.dot_general(a, b, (((1,), (0,)), ((), ())), preferred_element_type=F32)


def nt(a, b):
    return lax.dot_general(a, b, (((1,), (1,)), ((), ())), preferred_element_type=F32)


def tn(a, b):
    return lax.dot_general(a, b, (((0,), (0,)), ((), ())), preferred_element_type=F32)


def resident(shape):
    return pl.BlockSpec(shape, lambda *_: (0,) * len(shape), pipeline_mode=pl.Buffered(1))


def params(mib):
    return pltpu.CompilerParams(vmem_limit_bytes=mib * MIB)


def cost(flops, moved, trans=0):
    return pl.CostEstimate(flops=int(flops), bytes_accessed=int(moved), transcendentals=int(trans))


def bit_list(count):
    return [1 << n for n in range(count.bit_length() - 1)]


def swap(array, axis, size, bit):
    return lax.ppermute(array, axis, [(i, i ^ bit) for i in range(size)])


def tie(*groups):
    return lax.optimization_barrier(groups)


def halves_of(block):
    rows = block.shape[0] // 2
    return block[:rows], block[rows:]


def forwards(bits):
    steps = []
    for number in range(1, len(bits)):
        for half, order in enumerate((bits, bits[::-1])):
            for k in range(1, 2 ** len(bits)):
                if not any(k & bit for bit in order[number:]):
                    steps.append((number, half, k, k ^ order[number], order[number]))
    return steps


def gather_own(block, size, bits):
    return {bit: swap(block, "tensor", size, bit) for bit in bits}


def gather_rest(block, got, size, bits):
    parts = {(bit, half): part for bit in bits for half, part in enumerate(halves_of(got[bit]))}
    for _, half, k, made, bit in forwards(bits):
        parts[made, half] = swap(parts[k, half], "tensor", size, bit)
    whole = {0: (block,), **{bit: (got[bit],) for bit in bits}}
    return {
        k: whole[k] if k in whole else (parts[k, 0], parts[k, 1]) for k in range(2 ** len(bits))
    }


def add(a, b):
    return (a.astype(F32) + b.astype(F32)).astype(a.dtype)


def reduce_sends(pieces, size, bits, stage):
    return {
        (k, half): swap(pieces[made, half], "tensor", size, bit)
        for number, half, k, made, bit in reversed(forwards(bits))
        if number == stage
    }


def reduce_adds(pieces, got):
    return {key: add(pieces[key], got[key]) if key in got else pieces[key] for key in pieces}


def reduce_last(pieces, size, bits):
    return [
        swap(jnp.concatenate([pieces[bit, 0], pieces[bit, 1]], axis=0), "tensor", size, bit)
        for bit in bits
    ]


def reduce_total(pieces, got):
    total = jnp.concatenate([pieces[0, 0], pieces[0, 1]], axis=0).astype(F32)
    for part in got:
        total = total + part.astype(F32)
    return total


def gather_slots(mine, axis, size, bits):
    pieces = {0: mine}
    for bit in bits:
        for k in sorted(pieces):
            pieces[k ^ bit] = swap(pieces[k], axis, size, bit)
    return pieces


def natural(pieces, me):
    for bit in bit_list(len(pieces)):
        odd = (me & bit) != 0
        pieces = {k: jnp.where(odd, pieces[k ^ bit], pieces[k]) for k in pieces}
    return jnp.concatenate([pieces[k] for k in range(len(pieces))], axis=0)


def turn_rows(t, cos, sin):
    half = ROT // 2
    a, b = t[:half], t[half:ROT]
    return jnp.concatenate([a * cos - b * sin, b * cos + a * sin, t[ROT:]], axis=0)


def start_pieces(info_ref, slots, refs, tokens, buf_ref, sem):
    for (k, place), piece in zip(slots, refs):
        rows = piece.shape[0]
        base = pl.multiple_of(jnp.bitwise_xor(info_ref[0], k) * tokens + place * rows, rows)
        pltpu.make_async_copy(piece, buf_ref.at[pl.ds(base, rows), :], sem.at[k // 2]).start()


def listed(blocks):
    order = [(k, place) for k in sorted(blocks) for place in range(len(blocks[k]))]
    return order, [blocks[k][place] for k, place in order]


def wait_pieces(info_ref, step, tile, buf_ref, sem):
    which = jnp.bitwise_xor(step, info_ref[0] // 2)
    view = buf_ref.at[pl.ds(0, tile), :]
    pltpu.make_async_copy(view, view, sem.at[which]).wait()


def project_kernel(slots, info_ref, *refs):
    count = len(slots)
    pieces = refs[:count]
    wt_ref, cos_ref, sin_ref = refs[count : count + 3]
    n_ref, qt_ref, kt_ref, vt_ref, q_ref, k_ref, v_ref = refs[count + 3 : count + 10]
    step = pl.program_id(0)
    tile = n_ref.shape[0]
    wide = qt_ref.shape[0]
    buf_ref, sem = refs[count + 10 :]

    @pl.when(step == 0)
    def _():
        start_pieces(info_ref, slots, pieces, tile // 2, buf_ref, sem)

    wait_pieces(info_ref, step, tile, buf_ref, sem)
    normed = buf_ref[pl.ds(pl.multiple_of(step * tile, tile), tile), :]
    n_ref[...] = normed
    store_heads(wt_ref, normed, cos_ref, sin_ref, qt_ref, kt_ref, vt_ref, q_ref, k_ref, v_ref)


def project_more_kernel(n_ref, wt_ref, cos_ref, sin_ref, *outs):
    store_heads(wt_ref, n_ref[...], cos_ref, sin_ref, *outs)


def store_heads(wt_ref, normed, cos_ref, sin_ref, qt_ref, kt_ref, vt_ref, q_ref, k_ref, v_ref):
    wide = qt_ref.shape[0]
    made = nt(wt_ref[...], normed)
    cos, sin = cos_ref[...], sin_ref[...]
    scale = HD**-0.5
    for h in range(wide // HD):
        for which, t_ref, h_ref in ((0, qt_ref, q_ref), (1, kt_ref, k_ref), (2, vt_ref, v_ref)):
            base = which * wide + h * HD
            t = made[base : base + HD]
            if which < 2:
                t = turn_rows(t, cos, sin)
            t = t.astype(BF16)
            if which == 0:
                t = (t.astype(F32) * scale).astype(BF16)
            t_ref[h * HD : (h + 1) * HD, :] = t
            h_ref[h] = t.T


def project(info, blocks, weights, cos, sin):
    gathered = isinstance(blocks, dict)
    slots, pieces = listed(blocks) if gathered else ([], [blocks])
    if gathered:
        group = len(blocks)
        tokens, d = blocks[0][0].shape
        seq = group * tokens
        tile = 2 * tokens
    else:
        seq, d = blocks.shape
        tile = seq // 2
    wide = weights.shape[0] // 3
    heads = wide // HD
    flat = jax.ShapeDtypeStruct((wide, seq), BF16)
    split = jax.ShapeDtypeStruct((heads, seq, HD), BF16)
    flat_spec = pl.BlockSpec((wide, tile), lambda i, *_: (0, i))
    split_spec = pl.BlockSpec((heads, tile, HD), lambda i, *_: (0, i, 0))
    table = pl.BlockSpec((ROT // 2, tile), lambda i, *_: (0, i))
    rows = pl.BlockSpec((tile, d), lambda i, *_: (i, 0))
    row_out = ((jax.ShapeDtypeStruct((seq, d), BF16), rows),) if gathered else ()
    return pl.pallas_call(
        functools.partial(project_kernel, slots) if gathered else project_more_kernel,
        out_shape=tuple(shape for shape, _ in row_out) + (flat,) * 3 + (split,) * 3,
        grid_spec=pltpu.PrefetchScalarGridSpec(
            num_scalar_prefetch=1 if gathered else 0,
            grid=(seq // tile,),
            in_specs=([pl.BlockSpec(memory_space=pl.ANY)] * len(pieces) if gathered else [rows])
            + [resident(weights.shape), table, table],
            out_specs=tuple(spec for _, spec in row_out) + (flat_spec,) * 3 + (split_spec,) * 3,
            scratch_shapes=[
                pltpu.VMEM((seq, d), BF16),
                pltpu.SemaphoreType.DMA((seq // tile,)),
            ]
            if gathered
            else [],
        ),
        compiler_params=params(26),
        cost_estimate=cost(2 * seq * d * 3 * wide, seq * d * 4 + d * wide * 6 + 9 * wide * seq * 2),
        name="project",
    )(*((info,) if gathered else ()), *pieces, weights, cos, sin)


def send_pieces(info_ref, step, made_ref, outs, sem, wait):
    rows = outs[0].shape[0]
    odd = info_ref[0] % 2
    for pair in range(len(outs) // 4):

        @pl.when(step == pair)
        def _():
            for u in range(2):
                for half in range(2):
                    base = pl.multiple_of((2 * jnp.bitwise_xor(u, odd) + half) * rows, rows)
                    number = 4 * pair + 2 * u + half
                    copy = pltpu.make_async_copy(
                        made_ref.at[pair, pl.ds(base, rows), :], outs[number], sem.at[number]
                    )
                    if wait:
                        copy.wait()
                    else:
                        copy.start()


def wait_all_pieces(info_ref, made_ref, outs, sem):
    for pair in range(len(outs) // 4):
        send_pieces(info_ref, pair, made_ref, outs, sem, True)


def start_weights(sources, places, sem):
    for number, (source, place) in enumerate(zip(sources, places)):
        pltpu.make_async_copy(source, place, sem.at[number]).start()


def wait_weights(step, sources, places, sem, numbers):
    @pl.when(step == 0)
    def _():
        for number in numbers:
            pltpu.make_async_copy(sources[number], places[number], sem.at[number]).wait()


def weight_places(win_ref, fc_ref, wo_ref):
    units, ph = win_ref.shape[1] // 2, wo_ref.shape[0] // 2
    return [
        win_ref.at[:, :units],
        win_ref.at[:, units:],
        fc_ref.at[:units, :],
        fc_ref.at[units:, :],
        wo_ref.at[:ph, :],
        wo_ref.at[ph:, :],
    ]


def chunks_of(count):
    width = min(256, count)
    return [slice(base, base + width) for base in range(0, count, width)]


def feed_kernel(info_ref, n_ref, ot_own, ot_other, *refs):
    sources, (b_own, b_other) = refs[:6], refs[6:8]
    hid_ref, slope_ref = refs[8:10]
    outs = refs[10:-6]
    win_ref, fc_ref, wo_ref, made_ref, sem, out_sem = refs[-6:]
    step = pl.program_id(0)
    places = weight_places(win_ref, fc_ref, wo_ref)

    @pl.when(step == 0)
    def _():
        start_weights(sources, places, sem)

    normed = n_ref[...]
    root = math.sqrt(2.0 / math.pi)
    bias = jnp.concatenate([b_own[...], b_other[...]], axis=1)
    wait_weights(step, sources, places, sem, range(6))
    cols = chunks_of(hid_ref.shape[1])
    made = None
    pre = nn(normed, win_ref[:, cols[0]])
    for number, cut in enumerate(cols):
        now = pre + bias[:, cut]
        if number + 1 < len(cols):
            pre = nn(normed, win_ref[:, cols[number + 1]])
        square = now * now
        half = 0.5 + 0.5 * jnp.tanh(now * (root + (0.044715 * root) * square))
        gelu = now * half
        slope = half + (gelu - gelu * half) * (2.0 * root + (0.26829 * root) * square)
        hid_ref[:, cut] = gelu.astype(BF16)
        slope_ref[:, cut] = slope.astype(BF16)
    hidden = hid_ref[...]
    att = jnp.concatenate([ot_own[...], ot_other[...]], axis=0).T.astype(BF16)
    for cut in chunks_of(fc_ref.shape[1]):
        made = nn(hidden, fc_ref[:, cut]) + nn(att, wo_ref[:, cut])
        made_ref[step, :, cut] = made.astype(BF16)
    send_pieces(info_ref, step, made_ref, outs, out_sem, False)

    @pl.when(step == pl.num_programs(0) - 1)
    def _():
        wait_all_pieces(info_ref, made_ref, outs, out_sem)


def paired(i, info):
    return jnp.bitwise_xor(i, info[0] // 2)


def feed(info, normed, ot, w_in, b_in, w_fc, w_out, group):
    seq, d = normed.shape
    rows = seq // group // 2
    tile = 4 * rows
    ph, units = ot[0].shape[0], 2 * w_in[0].shape[1]
    wide = 2 * ph
    unit_rows = pl.BlockSpec((tile, units), lambda i, info: (paired(i, info), 0))
    made = pl.pallas_call(
        feed_kernel,
        out_shape=(jax.ShapeDtypeStruct((seq, units), BF16),) * 2
        + (jax.ShapeDtypeStruct((rows, d), BF16),) * (2 * group),
        grid_spec=pltpu.PrefetchScalarGridSpec(
            num_scalar_prefetch=1,
            grid=(seq // tile,),
            in_specs=[
                pl.BlockSpec((tile, d), lambda i, info: (paired(i, info), 0)),
                pl.BlockSpec((ph, tile), lambda i, info: (0, paired(i, info))),
                pl.BlockSpec((ph, tile), lambda i, info: (0, paired(i, info))),
            ]
            + [pl.BlockSpec(memory_space=pl.ANY)] * 6
            + [resident(b_in[0].shape)] * 2,
            out_specs=(unit_rows,) * 2 + (pl.BlockSpec(memory_space=pl.ANY),) * (2 * group),
            scratch_shapes=[
                pltpu.VMEM((d, units), BF16),
                pltpu.VMEM((units, d), BF16),
                pltpu.VMEM((wide, d), BF16),
                pltpu.VMEM((seq // tile, tile, d), BF16),
                pltpu.SemaphoreType.DMA((6,)),
                pltpu.SemaphoreType.DMA((2 * group,)),
            ],
        ),
        compiler_params=params(44),
        cost_estimate=cost(2 * seq * d * (2 * units + wide), seq * (d * 4 + units * 4 + wide * 4) + d * units * 4, seq * units),
        name="feed",
    )(info, normed, *ot, *w_in, *w_fc, *w_out, *b_in)
    return made[0], made[1], made[2:]


def feed_back_kernel(slots, info_ref, *refs):
    count = len(slots)
    pieces, refs = refs[:count], refs[count:]
    n_any, hid_any, slope_ref, ot_own, ot_other = refs[:5]
    sources, refs = refs[5:11], refs[11:]
    gn_ref, gt_ref, gs_ref, delta_ref, keep_ref, away_ref, gwout_ref, gbin_ref = refs[:8]
    g_buf, n_buf, hid_buf, pre_buf, win_ref, fc_ref, wo_ref, acc_ref, g_sem, w_sem, sem = refs[8:]
    step = pl.program_id(0)
    last = pl.num_programs(0) - 1
    tile, units = slope_ref.shape
    ph = wo_ref.shape[0] // 2
    places = weight_places(win_ref, fc_ref, wo_ref)
    order = (2, 3, 0, 1, 4, 5)
    whole = (
        pltpu.make_async_copy(n_any, n_buf, sem.at[0]),
        pltpu.make_async_copy(hid_any, hid_buf, sem.at[1]),
    )

    @pl.when(step == 0)
    def _():
        start_weights([sources[k] for k in order[:2]], [places[k] for k in order[:2]], w_sem.at[pl.ds(2, 2)])
        start_pieces(info_ref, slots, pieces, tile // 2, g_buf, g_sem)
        for k in (0, 1, 4, 5):
            pltpu.make_async_copy(sources[k], places[k], w_sem.at[k]).start()
        for copy in whole:
            copy.start()

    wait_weights(step, sources, places, w_sem, (2, 3))
    wait_pieces(info_ref, step, tile, g_buf, g_sem)
    rows = pl.ds(pl.multiple_of(step * tile, tile), tile)
    grads = g_buf[rows, :]
    cols = chunks_of(units)
    sums = []
    for cut in cols:
        grad_pre = nt(grads, fc_ref[cut, :]) * slope_ref[:, cut].astype(F32)
        rounded = grad_pre.astype(BF16)
        pre_buf[rows, cut] = rounded
        sums.append(jnp.sum(rounded.astype(F32), axis=0, keepdims=True))
    part_b = jnp.concatenate(sums, axis=1)
    wait_weights(step, sources, places, w_sem, (0, 1, 4, 5))
    rounded = pre_buf[rows, :]
    for cut in chunks_of(gn_ref.shape[1]):
        gn_ref[:, cut] = nt(rounded, win_ref[cut, :]).astype(BF16)
    grad_att = nt(wo_ref[...], grads).astype(BF16)
    gt_ref[...] = grad_att
    ot = jnp.concatenate([ot_own[...], ot_other[...]], axis=0)
    share = grad_att.astype(F32) * ot
    for h in range(gs_ref.shape[0]):
        head = slice(h * HD, (h + 1) * HD)
        gs_ref[h] = grad_att[head].T
        delta_ref[h] = jnp.sum(share[head], axis=0, keepdims=True)
    part_out = nn(ot.astype(BF16), grads)

    @pl.when(step == 0)
    def _():
        gwout_ref[...] = part_out
        gbin_ref[...] = part_b

    @pl.when(step > 0)
    def _():
        gwout_ref[...] += part_out
        gbin_ref[...] += part_b

    @pl.when(step == last)
    def _():
        for copy in whole:
            copy.wait()
        dp_size = 2 * keep_ref.shape[0]
        each = units // 2 // dp_size
        for which, (a_buf, b_buf) in enumerate(((hid_buf, g_buf), (pre_buf, n_buf))):
            acc_ref[...] = tn(a_buf[...], b_buf[...])
            for slot in range(dp_size):
                out = (keep_ref, away_ref)[slot % 2]
                index = jnp.bitwise_xor(info_ref[1], slot)
                for shard in range(2):
                    base = pl.multiple_of(shard * (units // 2) + index * each, each)
                    out[slot // 2, shard, which * each : (which + 1) * each, :] = acc_ref[
                        pl.ds(base, each), :
                    ].astype(BF16)


def feed_back(info, blocks, normed, hidden, slope, ot, w_in, w_fc, w_out, dp_size):
    seq, d = normed.shape
    group = len(blocks)
    slots, pieces = listed(blocks)
    tile = 2 * seq // group
    ph, units = ot[0].shape[0], hidden.shape[1]
    wide = 2 * ph
    heads = wide // HD
    rows = pl.BlockSpec((tile, d), lambda i, info: (i, 0))
    unit_rows = pl.BlockSpec((tile, units), lambda i, info: (i, 0))
    turned = pl.BlockSpec((wide, tile), lambda i, info: (0, i))
    half_turned = pl.BlockSpec((ph, tile), lambda i, info: (0, i))
    packed = (dp_size // 2, 2, units // dp_size, d)
    anywhere = pl.BlockSpec(memory_space=pl.ANY)
    return pl.pallas_call(
        functools.partial(feed_back_kernel, slots),
        out_shape=(
            jax.ShapeDtypeStruct((seq, d), BF16),
            jax.ShapeDtypeStruct((wide, seq), BF16),
            jax.ShapeDtypeStruct((heads, seq, HD), BF16),
            jax.ShapeDtypeStruct((heads, 1, seq), F32),
            jax.ShapeDtypeStruct(packed, BF16),
            jax.ShapeDtypeStruct(packed, BF16),
            jax.ShapeDtypeStruct((wide, d), F32),
            jax.ShapeDtypeStruct((1, units), F32),
        ),
        grid_spec=pltpu.PrefetchScalarGridSpec(
            num_scalar_prefetch=1,
            grid=(seq // tile,),
            in_specs=[anywhere] * len(pieces)
            + [anywhere, anywhere, unit_rows, half_turned, half_turned]
            + [anywhere] * 6,
            out_specs=(
                rows,
                turned,
                pl.BlockSpec((heads, tile, HD), lambda i, info: (0, i, 0)),
                pl.BlockSpec((heads, 1, tile), lambda i, info: (0, 0, i)),
                resident(packed),
                resident(packed),
                resident((wide, d)),
                resident((1, units)),
            ),
            scratch_shapes=[
                pltpu.VMEM((seq, d), BF16),
                pltpu.VMEM((seq, d), BF16),
                pltpu.VMEM((seq, units), BF16),
                pltpu.VMEM((seq, units), BF16),
                pltpu.VMEM((d, units), BF16),
                pltpu.VMEM((units, d), BF16),
                pltpu.VMEM((wide, d), BF16),
                pltpu.VMEM((units, d), F32),
                pltpu.SemaphoreType.DMA((group // 2,)),
                pltpu.SemaphoreType.DMA((6,)),
                pltpu.SemaphoreType.DMA((2,)),
            ],
        ),
        compiler_params=params(56),
        cost_estimate=cost(2 * seq * d * (4 * units + 2 * wide), seq * (d * 6 + units * 4 + wide * 8) + d * units * 8),
        name="feed_back",
    )(info, *pieces, normed, hidden, slope, *ot, *w_in, *w_fc, *w_out)


def rows_back_kernel(count, info_ref, *refs):
    turned_refs, refs = refs[: 3 * count], refs[3 * count :]
    (n_ref, part_ref, wt_own, wt_other), refs = refs[:4], refs[4:]
    sum_ref, outs = refs[0], refs[1:-4]
    wt_ref, made_ref, sem, out_sem = refs[-4:]
    step = pl.program_id(0)
    ph = wt_own.shape[0]
    sources, places = (wt_own, wt_other), (wt_ref.at[:ph, :], wt_ref.at[ph:, :])

    @pl.when(step == 0)
    def _():
        start_weights(sources, places, sem)

    turned = jnp.concatenate([ref[...] for ref in turned_refs], axis=0)
    wait_weights(step, sources, places, sem, (0, 1))
    sums = []
    for cut in chunks_of(n_ref.shape[1]):
        made = part_ref[:, cut].astype(F32) + tn(turned, wt_ref[:, cut])
        made_ref[step, :, cut] = made.astype(BF16)
        sums.append(
            jnp.concatenate(
                [
                    jnp.sum(made * n_ref[:, cut].astype(F32), axis=0, keepdims=True),
                    jnp.sum(made, axis=0, keepdims=True),
                ],
                axis=0,
            )
        )
    sums = jnp.concatenate(sums, axis=1)
    send_pieces(info_ref, step, made_ref, outs, out_sem, False)

    @pl.when(step == pl.num_programs(0) - 1)
    def _():
        wait_all_pieces(info_ref, made_ref, outs, out_sem)

    @pl.when(step == 0)
    def _():
        sum_ref[...] = sums

    @pl.when(step > 0)
    def _():
        sum_ref[...] += sums


def rows_back(info, turned, normed, part, w_t, group):
    seq, d = normed.shape
    rows = seq // group // 2
    tile = 4 * rows
    depth = w_t[0].shape[0]
    tile_rows = pl.BlockSpec((tile, d), lambda i, info: (paired(i, info), 0))
    made = pl.pallas_call(
        functools.partial(rows_back_kernel, len(turned) // 3),
        out_shape=(jax.ShapeDtypeStruct((2, d), F32),)
        + (jax.ShapeDtypeStruct((rows, d), BF16),) * (2 * group),
        grid_spec=pltpu.PrefetchScalarGridSpec(
            num_scalar_prefetch=1,
            grid=(seq // tile,),
            in_specs=[
                pl.BlockSpec((part.shape[0], tile), lambda i, info: (0, paired(i, info)))
                for part in turned
            ]
            + [tile_rows, tile_rows]
            + [pl.BlockSpec(memory_space=pl.ANY)] * 2,
            out_specs=(resident((2, d)),) + (pl.BlockSpec(memory_space=pl.ANY),) * (2 * group),
            scratch_shapes=[
                pltpu.VMEM((2 * depth, d), BF16),
                pltpu.VMEM((seq // tile, tile, d), BF16),
                pltpu.SemaphoreType.DMA((2,)),
                pltpu.SemaphoreType.DMA((2 * group,)),
            ],
        ),
        compiler_params=params(36),
        cost_estimate=cost(2 * seq * d * 2 * depth, seq * (d * 6 + depth * 4) + d * depth * 4),
        name="rows_back",
    )(info, *turned, normed, part, *w_t)
    return made[0], made[1:]


def weights_back_kernel(info_ref, dq_ref, dk_ref, dv_ref, n_ref, gwout_ref, keep_ref, away_ref, acc_ref):
    step = pl.program_id(0)
    ph = gwout_ref.shape[0]
    turned = jnp.concatenate([dq_ref[...], dk_ref[...], dv_ref[...]], axis=0)
    part = nn(turned, n_ref[...])

    @pl.when(step == 0)
    def _():
        acc_ref[: 3 * ph, :] = part
        acc_ref[3 * ph :, :] = gwout_ref[...]

    @pl.when(step > 0)
    def _():
        acc_ref[: 3 * ph, :] += part

    @pl.when(step == pl.num_programs(0) - 1)
    def _():
        rows = keep_ref.shape[1]
        for slot in range(2 * keep_ref.shape[0]):
            out = (keep_ref, away_ref)[slot % 2]
            base = pl.multiple_of(jnp.bitwise_xor(info_ref[1], slot) * rows, rows)
            out[slot // 2] = acc_ref[pl.ds(base, rows), :].astype(BF16)


def weights_back(info, turned, normed, gw_out, shard, group, dp_size):
    seq, d = normed.shape
    tile = 2 * seq // group
    ph = turned[0].shape[0]
    packed = (dp_size // 2, 4 * ph // dp_size, d)
    return pl.pallas_call(
        weights_back_kernel,
        out_shape=(jax.ShapeDtypeStruct(packed, BF16),) * 2,
        grid_spec=pltpu.PrefetchScalarGridSpec(
            num_scalar_prefetch=1,
            grid=(seq // tile,),
            in_specs=[pl.BlockSpec((ph, tile), lambda i, info: (0, i))] * 3
            + [
                pl.BlockSpec((tile, d), lambda i, info: (i, 0)),
                pl.BlockSpec((ph, d), lambda i, info: (shard, 0)),
            ],
            out_specs=(resident(packed),) * 2,
            scratch_shapes=[pltpu.VMEM((4 * ph, d), F32)],
        ),
        compiler_params=params(20),
        cost_estimate=cost(2 * seq * d * 3 * ph, seq * (d * 2 + ph * 6) + d * ph * 16),
        name="weights_back",
    )(info, *turned, normed, gw_out)


def finish_feed_kernel(info_ref, *refs):
    pieces, (gin_ref, gfc_ref) = refs[:-2], refs[-2:]
    rows = gfc_ref.shape[0]
    for slot, piece in enumerate(pieces):

        @pl.when(pl.program_id(0) == slot)
        def _():
            gfc_ref[...] = piece[:rows, :].astype(F32)
            gin_ref[...] = piece[rows:, :].astype(F32).T


def finish_feed(info, pieces, units):
    count = len(pieces)
    d = pieces[0].shape[1]
    return pl.pallas_call(
        finish_feed_kernel,
        out_shape=(jax.ShapeDtypeStruct((d, units), F32), jax.ShapeDtypeStruct((units, d), F32)),
        grid_spec=pltpu.PrefetchScalarGridSpec(
            num_scalar_prefetch=1,
            grid=(count,),
            in_specs=[resident(pieces[0].shape)] * count,
            out_specs=(
                pl.BlockSpec((d, units // count), lambda i, info: (0, jnp.bitwise_xor(i, info[1]))),
                pl.BlockSpec((units // count, d), lambda i, info: (jnp.bitwise_xor(i, info[1]), 0)),
            ),
        ),
        compiler_params=params(16),
        cost_estimate=cost(0, d * units * 12),
        name="finish_feed",
    )(info, *pieces)


def finish_project_kernel(info_ref, *refs):
    pieces, (gqkv_ref, gout_ref) = refs[:-2], refs[-2:]
    index = pl.program_id(0)
    slot_now = jnp.bitwise_xor(index, info_ref[1])
    for slot, piece in enumerate(pieces):

        @pl.when((slot_now == slot) & (index < 3))
        def _():
            gqkv_ref[0] = piece[...].astype(F32).T

        @pl.when((slot_now == slot) & (index == 3))
        def _():
            gout_ref[...] = piece[...].astype(F32)


def finish_project(info, pieces):
    rows, d = pieces[0].shape
    return pl.pallas_call(
        finish_project_kernel,
        out_shape=(jax.ShapeDtypeStruct((3, d, rows), F32), jax.ShapeDtypeStruct((rows, d), F32)),
        grid_spec=pltpu.PrefetchScalarGridSpec(
            num_scalar_prefetch=1,
            grid=(4,),
            in_specs=[resident((rows, d))] * 4,
            out_specs=(
                pl.BlockSpec((1, d, rows), lambda i, info: (jnp.minimum(i, 2), 0, 0)),
                resident((rows, d)),
            ),
        ),
        compiler_params=params(16),
        cost_estimate=cost(0, d * rows * 24),
        name="finish_project",
    )(info, *pieces)


def mask_scores(scores, start, key_base, query_base, diagonal):
    key_places = key_base + lax.broadcasted_iota(jnp.int32, scores.shape, 0)
    keep = key_places >= start
    if diagonal:
        query_places = query_base + lax.broadcasted_iota(jnp.int32, scores.shape, 1)
        keep = keep & (key_places <= query_places)
    return jnp.where(keep, scores, NEG_LARGE)


def attend_kernel(low_ref, start_ref, qt_ref, k_ref, vt_ref, ot_ref, lse_ref, m_ref, l_ref, acc_ref):
    block = qt_ref.shape[1]
    i = pl.program_id(1)
    queries = qt_ref[...]
    start = start_ref[...]

    def step(j, diagonal):
        base = pl.multiple_of(j * block, block)
        scores = nn(k_ref[0, pl.ds(base, block), :], queries)
        scores = mask_scores(scores, start, base, i * block, diagonal)
        peak = jnp.max(scores, axis=0, keepdims=True)
        values = vt_ref[:, pl.ds(base, block)]
        if diagonal:
            weights = jnp.exp(scores - peak)
            m_ref[...] = peak
            l_ref[...] = jnp.sum(weights, axis=0, keepdims=True)
            acc_ref[...] = nn(values, weights.astype(BF16))
        else:
            before = m_ref[...]
            peak = jnp.maximum(before, peak)
            shrink = jnp.exp(before - peak)
            weights = jnp.exp(scores - peak)
            m_ref[...] = peak
            l_ref[...] = l_ref[...] * shrink + jnp.sum(weights, axis=0, keepdims=True)
            acc_ref[...] = acc_ref[...] * shrink + nn(values, weights.astype(BF16))

    step(i, True)

    def body(j, carry):
        step(j, False)
        return carry

    lax.fori_loop(low_ref[i], i, body, 0)
    total = l_ref[...]
    ot_ref[...] = acc_ref[...] * (1.0 / total)
    lse_ref[0] = m_ref[...] + jnp.log(total)


def attend(low, start, qt, k, vt, block, base, heads):
    seq = qt.shape[1]
    blocks = seq // block
    return pl.pallas_call(
        attend_kernel,
        out_shape=(
            jax.ShapeDtypeStruct((heads * HD, seq), F32),
            jax.ShapeDtypeStruct((heads, 1, seq), F32),
        ),
        grid_spec=pltpu.PrefetchScalarGridSpec(
            num_scalar_prefetch=1,
            grid=(heads, blocks),
            in_specs=[
                pl.BlockSpec((1, block), lambda h, i, low: (0, i)),
                pl.BlockSpec((HD, block), lambda h, i, low: (base + h, i)),
                pl.BlockSpec((1, seq, HD), lambda h, i, low: (base + h, 0, 0)),
                pl.BlockSpec((HD, seq), lambda h, i, low: (base + h, 0)),
            ],
            out_specs=(
                pl.BlockSpec((HD, block), lambda h, i, low: (h, i)),
                pl.BlockSpec((1, 1, block), lambda h, i, low: (h, 0, i)),
            ),
            scratch_shapes=[
                pltpu.VMEM((1, block), F32),
                pltpu.VMEM((1, block), F32),
                pltpu.VMEM((HD, block), F32),
            ],
        ),
        compiler_params=params(12),
        cost_estimate=cost(heads * seq * seq * 512, heads * seq * HD * 12, heads * seq * seq // 2),
        name="attend",
    )(low, start, qt, k, vt)


def attend_back_kernel(
    high_ref, start_ref, lse_ref, delta_ref, cos_ref, sin_ref, qt_ref, kt_ref, gt_ref, q_ref, k_ref, v_ref, g_ref,
    dqt_out, dkt_out, dvt_out, dqt_ref, dk_ref, dv_ref
):
    seq = qt_ref.shape[1]
    blocks = high_ref.shape[0]
    block = seq // blocks
    dqt_ref[...] = jnp.zeros_like(dqt_ref)

    def pair(i, j, diagonal):
        qs = pl.ds(pl.multiple_of(i * block, block), block)
        ks = pl.ds(pl.multiple_of(j * block, block), block)
        scores = nn(k_ref[0, ks, :], qt_ref[:, qs])
        scores = mask_scores(scores, start_ref[:, qs], j * block, i * block, diagonal)
        probs = jnp.exp(scores - lse_ref[0, :, qs])
        grad_probs = nn(v_ref[0, ks, :], gt_ref[:, qs])
        grad_scores = (probs * (grad_probs - delta_ref[0, :, qs])).astype(BF16)
        dv = nn(probs.astype(BF16), g_ref[0, qs, :])
        dk = nn(grad_scores, q_ref[0, qs, :])
        if diagonal:
            dv_ref[ks, :] = dv
            dk_ref[ks, :] = dk
        else:
            dv_ref[ks, :] += dv
            dk_ref[ks, :] += dk
        dqt_ref[:, qs] += nn(kt_ref[:, ks], grad_scores)

    def keys(j, carry):
        pair(j, j, True)

        def queries(i, inner):
            pair(i, j, False)
            return inner

        lax.fori_loop(j + 1, high_ref[j], queries, 0)
        return carry

    lax.fori_loop(0, blocks, keys, 0)
    cos, sin = cos_ref[...], sin_ref[...]
    half = ROT // 2

    def store(out, t):
        a, b = t[:half], t[half:ROT]
        out[:half] = (a * cos + b * sin).astype(BF16)
        out[half:ROT] = (b * cos - a * sin).astype(BF16)
        out[ROT:] = t[ROT:].astype(BF16)

    store(dqt_out, dqt_ref[...] * (HD**-0.5))
    store(dkt_out, dk_ref[...].T)
    dvt_out[...] = dv_ref[...].T.astype(BF16)


def attend_back(high, start, lse, delta, cos, sin, qt, kt, gt, q, k, v, g, base, local, heads):
    seq = qt.shape[1]
    flat = pl.BlockSpec((HD, seq), lambda h, high: (local + h, 0))
    split = pl.BlockSpec((1, seq, HD), lambda h, high: (local + h, 0, 0))
    both_flat = pl.BlockSpec((HD, seq), lambda h, high: (base + h, 0))
    both_split = pl.BlockSpec((1, seq, HD), lambda h, high: (base + h, 0, 0))
    row = pl.BlockSpec((1, seq), lambda h, high: (0, 0))
    head_row = pl.BlockSpec((1, 1, seq), lambda h, high: (base + h, 0, 0))
    own_row = pl.BlockSpec((1, 1, seq), lambda h, high: (local + h, 0, 0))
    table = pl.BlockSpec((ROT // 2, seq), lambda h, high: (0, 0))
    return pl.pallas_call(
        attend_back_kernel,
        out_shape=(jax.ShapeDtypeStruct((heads * HD, seq), BF16),) * 3,
        grid_spec=pltpu.PrefetchScalarGridSpec(
            num_scalar_prefetch=1,
            grid=(heads,),
            in_specs=[row, own_row, head_row, table, table]
            + [flat, flat, both_flat]
            + [split, split, split, both_split],
            out_specs=(pl.BlockSpec((HD, seq), lambda h, high: (h, 0)),) * 3,
            scratch_shapes=[
                pltpu.VMEM((HD, seq), F32),
                pltpu.VMEM((seq, HD), F32),
                pltpu.VMEM((seq, HD), F32),
            ],
        ),
        compiler_params=params(20),
        cost_estimate=cost(heads * seq * seq * 1280, heads * HD * seq * 24, heads * seq * seq // 2),
        name="attend_back",
    )(high, start, lse, delta, cos, sin, qt, kt, gt, q, k, v, g)


def run_starts(segments):
    places = lax.broadcasted_iota(jnp.int32, segments.shape, 1)
    leading = jnp.ones_like(segments[:, :1])
    changes = jnp.concatenate(
        [leading, (segments[:, 1:] != segments[:, :-1]).astype(jnp.int32)], axis=1
    )
    starts = lax.cummax(places * changes, axis=1)
    return places, starts


def build(dp_size, tensor_size):
    def per_device(
        inputs, segments, norm_gain, norm_bias, w_qkv, w_out, w_in, b_in, w_fc, b_out, cotangent
    ):
        row_count, seq = segments.shape
        tokens, d = inputs.shape
        group = tensor_size // row_count
        half_rot = ROT // 2
        block = 512
        me = lax.axis_index("tensor")
        dp = lax.axis_index("dp")
        row = me // group
        info = jnp.stack([me % group, dp]).astype(jnp.int32)
        other = [(i, (i + group) % tensor_size) for i in range(tensor_size)]
        bits = bit_list(group)
        dp_bits = bit_list(dp_size)
        def normalize(rows):
            rows = rows.astype(F32)
            centred = rows - jnp.mean(rows, axis=-1, keepdims=True)
            inv_std = lax.rsqrt(jnp.mean(centred * centred, axis=-1, keepdims=True) + EPSILON)
            return centred * inv_std, inv_std

        normed_own = (normalize(inputs)[0] * norm_gain + norm_bias).astype(BF16)
        n_got = gather_own(normed_own, tensor_size, bits)

        def slice_of(indexed):
            return lax.dynamic_index_in_dim(indexed, dp, 0, keepdims=False)

        def fetch(part):
            return lax.ppermute(part, "tensor", other)

        def share(got):
            return gather_slots(got, "dp", dp_size, dp_bits[::-1])

        def rows_of(pieces, start, stop):
            return natural({k: pieces[k][start:stop] for k in pieces}, dp)

        units, per_head = w_in.shape[1], w_qkv.shape[2]
        shard_heads = per_head // HD
        fc_rows = units // dp_size
        qkv_slice = slice_of(w_qkv.reshape(dp_size, -1, per_head))
        in_slice = slice_of(w_in.reshape(dp_size, -1, units))
        fc_slice = jnp.concatenate(
            [slice_of(w_fc.reshape(dp_size, -1, d)), slice_of(w_out.reshape(dp_size, -1, d))], axis=0
        )
        wt_own = jnp.concatenate([w_qkv[c].T for c in range(3)], axis=0)

        segs = lax.dynamic_slice_in_dim(segments, row, 1, axis=0)
        places, starts = run_starts(segs)
        first_key = jnp.where(segs >= 0, starts, places)
        offsets = (places - starts).astype(F32)
        frequency = jnp.exp(
            lax.broadcasted_iota(F32, (half_rot,), 0) * (-2.0 * math.log(10000.0) / ROT)
        )
        angles = frequency[:, None] * offsets
        cos_t, sin_t = jnp.cos(angles), jnp.sin(angles)
        blocks = seq // block
        low = (jnp.min(first_key.reshape(blocks, block), axis=1) // block).astype(jnp.int32)
        reach = low[None, :] <= jnp.arange(blocks)[:, None]
        high = jnp.max(
            jnp.where(reach, jnp.arange(1, blocks + 1, dtype=jnp.int32)[None, :], 0), axis=1
        ).astype(jnp.int32)

        prepared = (wt_own, cos_t, sin_t, first_key, low, high)
        n_got, (qkv_slice, in_slice, fc_slice), prepared = tie(
            n_got, (qkv_slice, in_slice, fc_slice), prepared
        )
        wt_own, cos_t, sin_t, first_key, low, high = prepared
        n_blocks = gather_rest(normed_own, n_got, tensor_size, bits)
        qkv_got, in_got, fc_got, b_in_other = (
            fetch(part) for part in (qkv_slice, in_slice, fc_slice, b_in)
        )
        n_blocks, cot = tie(n_blocks, cotangent)
        g_got = gather_own(cot, tensor_size, bits)

        def heads_forward(made, base, count):
            return attend(low, first_key, made[0], made[4], made[2], block, base, count)

        cut = shard_heads // 2
        made = project(info, n_blocks, wt_own, cos_t, sin_t)
        normed, own = made[0], made[1:]
        attended = []
        if cut:
            attended.append(heads_forward(own, 0, cut))
            (attended[0], qkv_got), own = tie((attended[0], qkv_got), own)
        qkv_pieces = share(qkv_got)
        attended.append(heads_forward(own, cut, shard_heads - cut))
        attended[-1], qkv_pieces, in_got, normed = tie(attended[-1], qkv_pieces, in_got, normed)
        qkv_other = rows_of(qkv_pieces, 0, None).reshape(w_qkv.shape)
        wt_other = jnp.concatenate([qkv_other[c].T for c in range(3)], axis=0)
        in_pieces = share(in_got)
        rest = project(None, normed, wt_other, cos_t, sin_t)
        attended_rest = []
        if cut:
            attended_rest.append(heads_forward(rest, 0, cut))
            attended_rest[0], in_pieces, fc_got, g_got, rest = tie(
                attended_rest[0], in_pieces, fc_got, g_got, rest
            )
        fc_pieces = share(fc_got)
        w_in_other = rows_of(in_pieces, 0, None)
        g_blocks = gather_rest(cot, g_got, tensor_size, bits)
        attended_rest.append(heads_forward(rest, cut, shard_heads - cut))
        attended_rest[-1], fc_pieces, w_in_other = tie(attended_rest[-1], fc_pieces, w_in_other)
        (ot_own, lse_own), (ot_other, lse_other) = (
            tuple(jnp.concatenate([part[n] for part in parts], axis=0) for n in range(2))
            for parts in (attended, attended_rest)
        )
        w_fc_other = rows_of(fc_pieces, 0, fc_rows)
        w_out_other = rows_of(fc_pieces, fc_rows, None)
        ot = (ot_own, ot_other)
        w_in_both, w_fc_both, w_out_both = (w_in, w_in_other), (w_fc, w_fc_other), (w_out, w_out_other)
        hidden, slope, out_pieces = feed(
            info, normed, ot, w_in_both, (b_in[None], b_in_other[None]), w_fc_both, w_out_both, group
        )

        def by_slot(pieces):
            return {(k, half): pieces[2 * k + half] for k in range(group) for half in range(2)}

        last_stage = len(bits) - 1
        out_parts = by_slot(out_pieces)
        out_got = reduce_sends(out_parts, tensor_size, bits, last_stage)
        made = feed_back(
            info, g_blocks, normed, hidden, slope, ot, w_in_both, w_fc_both, w_out_both, dp_size
        )
        made, out_got = tie(made, out_got)
        gn_part, gt, g_heads, delta, keep1, away1, gw_out, gb_in = made
        out_parts = reduce_adds(out_parts, out_got)
        for stage in range(last_stage - 1, 0, -1):
            out_parts = reduce_adds(out_parts, reduce_sends(out_parts, tensor_size, bits, stage))
        out_got = reduce_last(out_parts, tensor_size, bits)

        def settle_dp(parts, bit):
            got = {
                k ^ bit: [swap(part, "dp", dp_size, bit) for part in parts[k]]
                for k in sorted(parts)
                if k & bit
            }
            return {k: parts[k] for k in got}, got

        def settle_add(kept, got):
            return {k: tuple(add(a, b) for a, b in zip(kept[k], got[k])) for k in kept}

        def settle_rest(parts, got):
            for bit in dp_bits[2:]:
                parts, got = settle_dp(settle_add(parts, got), bit)
            return settle_add(parts, got)[0]

        def settle_share(total):
            pieces = gather_slots(total, "dp", dp_size, dp_bits[::-1])
            return [pieces[k] for k in range(dp_size)]

        def heads_back(shard):
            qt, kt, vt, q, k, v = (own, rest)[shard]
            return attend_back(
                high, first_key, (lse_own, lse_other)[shard], delta, cos_t, sin_t, qt, kt, gt, q, k, v, g_heads,
                shard * shard_heads, 0, shard_heads
            )

        got1 = swap(away1, "dp", dp_size, dp_bits[0])
        turned_other = heads_back(1)
        turned_other, got1, gt = tie(turned_other, got1, gt)
        kept1, got1 = settle_dp(
            {
                2 * j: tuple(add(keep1[j, s], got1[j, s]) for s in range(2))
                for j in range(dp_size // 2)
            },
            dp_bits[1],
        )
        keep2, away2 = weights_back(info, turned_other, normed, gw_out, 1, group, dp_size)
        got2 = swap(away2, "dp", dp_size, dp_bits[0])
        (keep2, gt), _ = tie((keep2, gt), kept1)
        turned_own = heads_back(0)
        turned_own, got1, got2, out_got = tie(turned_own, got1, got2, out_got)
        kept2, got2 = settle_dp(
            {2 * j: (add(keep2[j], got2[j]),) for j in range(dp_size // 2)}, dp_bits[1]
        )
        own1, other1 = settle_rest(kept1, got1)
        other1 = fetch(other1)
        output = (inputs.astype(F32) + reduce_total(out_parts, out_got) + b_out).astype(BF16)
        turned_own, _ = tie(turned_own, (kept2, own1, output))
        sums, gn_pieces = rows_back(
            info, [*turned_own, *turned_other], normed, gn_part, (wt_own, wt_other), group
        )
        gn_parts = by_slot(gn_pieces)
        gn_got = reduce_sends(gn_parts, tensor_size, bits, last_stage)
        sums, turned_own, got2 = tie(sums, turned_own, got2)
        (other2,) = settle_rest(kept2, got2)
        other2_got = fetch(other2)
        keep3, away3 = weights_back(info, turned_own, normed, gw_out, 0, group, dp_size)
        got3 = swap(away3, "dp", dp_size, dp_bits[0])

        bias_parts = jnp.zeros((tensor_size, units), F32)
        bias_parts = lax.dynamic_update_slice_in_dim(bias_parts, gb_in[:, :units], me, axis=0)
        bias_parts = lax.dynamic_update_slice_in_dim(
            bias_parts, gb_in[:, units:], (me + group) % tensor_size, axis=0
        )
        cotangent_f = cotangent.astype(F32)
        total = jnp.concatenate(
            [sums, jnp.sum(cotangent_f, axis=0, keepdims=True), bias_parts.reshape(-1, d)], axis=0
        )

        def stage(total, axis, size, numbers):
            for number in numbers:
                total = total + swap(total, axis, size, bit_list(size)[number])
            return total

        total = stage(total, "dp", dp_size, [0])
        keep3, got3, total = tie(keep3, got3, total)
        kept3, got3 = settle_dp(
            {2 * j: (add(keep3[j], got3[j]),) for j in range(dp_size // 2)}, dp_bits[1]
        )
        total = stage(total, "dp", dp_size, range(1, len(dp_bits)))
        gn_got, kept3, other1, total = tie(gn_got, kept3, other1, total)
        gn_parts = reduce_adds(gn_parts, gn_got)
        for number in range(last_stage - 1, 0, -1):
            gn_parts = reduce_adds(gn_parts, reduce_sends(gn_parts, tensor_size, bits, number))
        gn_got = reduce_last(gn_parts, tensor_size, bits)
        total1 = add(own1, other1)
        got3, other2_got, total1, gn_parts = tie(got3, other2_got, total1, gn_parts)
        (own3,) = settle_rest(kept3, got3)
        total2 = add(own3, other2_got)
        total, total2 = tie(total, total2)
        total = stage(total, "tensor", tensor_size, range(len(bit_list(tensor_size))))
        pieces1, pieces2 = settle_share(total1), settle_share(total2)
        pieces1, total = tie(pieces1, total)

        unit_rows, inv_std = normalize(inputs)
        grad_norm_own = reduce_total(gn_parts, gn_got)
        scaled = grad_norm_own * norm_gain
        grad_local = inv_std * (
            scaled
            - jnp.mean(scaled, axis=-1, keepdims=True)
            - unit_rows * jnp.mean(scaled * unit_rows, axis=-1, keepdims=True)
        )
        grad_inputs = cotangent_f + grad_local

        if fc_rows % LANES == 0:
            grad_in, grad_fc = finish_feed(info, pieces1, units)
        else:
            pieces1 = dict(enumerate(pieces1))
            grad_fc = rows_of(pieces1, 0, fc_rows).astype(F32)
            grad_in = rows_of(pieces1, fc_rows, None).T.astype(F32)
        if dp_size == 4 and per_head % LANES == 0:
            grad_qkv, grad_out = finish_project(info, pieces2)
        else:
            stacked = natural(dict(enumerate(pieces2)), dp)
            grad_qkv = jnp.swapaxes(
                stacked[: 3 * per_head].reshape(3, per_head, d), 1, 2
            ).astype(F32)
            grad_out = stacked[3 * per_head :].astype(F32)

        grad_bias = total[1]
        grad_gain = (total[0] - norm_bias * grad_bias) / norm_gain
        grad_b_out = total[2]
        grad_b_in = lax.dynamic_slice_in_dim(total[3:].reshape(tensor_size, units), me, 1, axis=0)[0]
        return (
            output,
            grad_inputs,
            grad_gain,
            grad_bias,
            grad_qkv,
            grad_out,
            grad_in,
            grad_b_in,
            grad_fc,
            grad_b_out,
        )

    return per_device


def solution(mesh):
    tokens = P(("dp", "tensor"), None)
    return jax.shard_map(
        build(mesh.shape["dp"], mesh.shape["tensor"]),
        mesh=mesh,
        in_specs=(
            tokens,
            P("dp", None),
            P(),
            P(),
            P(None, None, "tensor"),
            P("tensor", None),
            P(None, "tensor"),
            P("tensor"),
            P("tensor", None),
            P(),
            tokens,
        ),
        out_specs=(
            tokens,
            tokens,
            P(),
            P(),
            P(None, None, "tensor"),
            P("tensor", None),
            P(None, "tensor"),
            P("tensor"),
            P("tensor", None),
            P(),
        ),
        check_vma=False,
    )
```

```python
import functools
import math

import jax
import jax.numpy as jnp
from jax import lax
from jax.experimental import pallas as pl
from jax.experimental.pallas import tpu as pltpu
from jax.sharding import PartitionSpec as P

HD = 64
ROT = 32
EPSILON = 1e-05
NEG_LARGE = -1e30
BF16 = jnp.bfloat16
F32 = jnp.float32
LANES = 128
MIB = 1024 * 1024


def nn(a, b):
    return lax.dot_general(a, b, (((1,), (0,)), ((), ())), preferred_element_type=F32)


def nt(a, b):
    return lax.dot_general(a, b, (((1,), (1,)), ((), ())), preferred_element_type=F32)


def tn(a, b):
    return lax.dot_general(a, b, (((0,), (0,)), ((), ())), preferred_element_type=F32)


def resident(shape):
    return pl.BlockSpec(shape, lambda *_: (0,) * len(shape), pipeline_mode=pl.Buffered(1))


def params(mib):
    return pltpu.CompilerParams(vmem_limit_bytes=mib * MIB)


def cost(flops, moved, trans=0):
    return pl.CostEstimate(flops=int(flops), bytes_accessed=int(moved), transcendentals=int(trans))


def bit_list(count):
    return [1 << n for n in range(count.bit_length() - 1)]


def swap(array, axis, size, bit):
    return lax.ppermute(array, axis, [(i, i ^ bit) for i in range(size)])


def tie(*groups):
    return lax.optimization_barrier(groups)


def halves_of(block):
    rows = block.shape[0] // 2
    return block[:rows], block[rows:]


def forwards(bits):
    steps = []
    for number in range(1, len(bits)):
        for half, order in enumerate((bits, bits[::-1])):
            for k in range(1, 2 ** len(bits)):
                if not any(k & bit for bit in order[number:]):
                    steps.append((number, half, k, k ^ order[number], order[number]))
    return steps


def gather_own(halves, size, bits):
    orders = (bits, bits[::-1])
    return {
        (order[n], half): swap(halves[half], "tensor", size, order[n])
        for n in range(len(bits))
        for half, order in enumerate(orders)
    }


def gather_rest(halves, got, size, bits):
    parts = {**got, (0, 0): halves[0], (0, 1): halves[1]}
    for _, half, k, made, bit in forwards(bits):
        parts[made, half] = swap(parts[k, half], "tensor", size, bit)
    return {k: (parts[k, 0], parts[k, 1]) for k in range(2 ** len(bits))}


def add(a, b):
    return (a.astype(F32) + b.astype(F32)).astype(a.dtype)


def reduce_sends(pieces, size, bits, stage):
    return {
        (k, half): swap(pieces[made, half], "tensor", size, bit)
        for number, half, k, made, bit in reversed(forwards(bits))
        if number == stage
    }


def reduce_adds(pieces, got):
    return {key: add(pieces[key], got[key]) if key in got else pieces[key] for key in pieces}


def reduce_early(pieces, size, bits):
    waiting = {(k, half) for _, half, k, _, _ in forwards(bits)}
    return {
        (bit, half): swap(pieces[bit, half], "tensor", size, bit)
        for bit in bits
        for half in range(2)
        if (bit, half) not in waiting
    }


def reduce_late(pieces, early, size, bits):
    return {
        (bit, half): swap(pieces[bit, half], "tensor", size, bit)
        for bit in bits
        for half in range(2)
        if (bit, half) not in early
    }


def reduce_total(pieces, got):
    halves = []
    for half in range(2):
        total = pieces[0, half].astype(F32)
        for k, which in sorted(got):
            if which == half:
                total = total + got[k, half].astype(F32)
        halves.append(total)
    return jnp.concatenate(halves, axis=0)


def gather_slots(mine, axis, size, bits):
    return gather_more({0: mine}, axis, size, bits)


def gather_more(pieces, axis, size, bits):
    pieces = dict(pieces)
    for bit in bits:
        for k in sorted(pieces):
            pieces[k ^ bit] = swap(pieces[k], axis, size, bit)
    return pieces


def natural(pieces, me):
    for bit in bit_list(len(pieces)):
        odd = (me & bit) != 0
        pieces = {k: jnp.where(odd, pieces[k ^ bit], pieces[k]) for k in pieces}
    return jnp.concatenate([pieces[k] for k in range(len(pieces))], axis=0)


def turn_rows(t, cos, sin):
    half = ROT // 2
    a, b = t[:half], t[half:ROT]
    return jnp.concatenate([a * cos - b * sin, b * cos + a * sin, t[ROT:]], axis=0)


def start_pieces(info_ref, slots, refs, tokens, buf_ref, sem):
    for (k, place), piece in zip(slots, refs):
        rows = piece.shape[0]
        base = pl.multiple_of(jnp.bitwise_xor(info_ref[0], k) * tokens + place * rows, rows)
        pltpu.make_async_copy(piece, buf_ref.at[pl.ds(base, rows), :], sem.at[k // 2]).start()


def listed(blocks):
    order = [(k, place) for k in sorted(blocks) for place in range(len(blocks[k]))]
    return order, [blocks[k][place] for k, place in order]


def wait_pieces(info_ref, step, tile, buf_ref, sem):
    which = jnp.bitwise_xor(step, info_ref[0] // 2)
    view = buf_ref.at[pl.ds(0, tile), :]
    pltpu.make_async_copy(view, view, sem.at[which]).wait()


def project_kernel(slots, info_ref, *refs):
    count = len(slots)
    pieces = refs[:count]
    wt_ref, cos_ref, sin_ref = refs[count : count + 3]
    n_ref, qt_ref, kt_ref, vt_ref, q_ref, k_ref, v_ref = refs[count + 3 : count + 10]
    step = pl.program_id(0)
    tile = n_ref.shape[0]
    wide = qt_ref.shape[0]
    buf_ref, sem = refs[count + 10 :]

    @pl.when(step == 0)
    def _():
        start_pieces(info_ref, slots, pieces, tile // 2, buf_ref, sem)

    wait_pieces(info_ref, step, tile, buf_ref, sem)
    normed = buf_ref[pl.ds(pl.multiple_of(step * tile, tile), tile), :]
    n_ref[...] = normed
    store_heads(wt_ref, normed, cos_ref, sin_ref, qt_ref, kt_ref, vt_ref, q_ref, k_ref, v_ref)


def project_more_kernel(n_ref, wt_ref, cos_ref, sin_ref, *outs):
    store_heads(wt_ref, n_ref[...], cos_ref, sin_ref, *outs)


def store_heads(wt_ref, normed, cos_ref, sin_ref, qt_ref, kt_ref, vt_ref, q_ref, k_ref, v_ref):
    wide = qt_ref.shape[0]
    made = nt(wt_ref[...], normed)
    cos, sin = cos_ref[...], sin_ref[...]
    scale = HD**-0.5
    for h in range(wide // HD):
        for which, t_ref, h_ref in ((0, qt_ref, q_ref), (1, kt_ref, k_ref), (2, vt_ref, v_ref)):
            base = which * wide + h * HD
            t = made[base : base + HD]
            if which < 2:
                t = turn_rows(t, cos, sin)
            t = t.astype(BF16)
            if which == 0:
                t = (t.astype(F32) * scale).astype(BF16)
            t_ref[h * HD : (h + 1) * HD, :] = t
            h_ref[h] = t.T


def project(info, blocks, weights, cos, sin):
    gathered = isinstance(blocks, dict)
    slots, pieces = listed(blocks) if gathered else ([], [blocks])
    if gathered:
        group = len(blocks)
        tokens, d = sum(part.shape[0] for part in blocks[0]), blocks[0][0].shape[1]
        seq = group * tokens
        tile = 2 * tokens
    else:
        seq, d = blocks.shape
        tile = seq // 2
    wide = weights.shape[0] // 3
    heads = wide // HD
    flat = jax.ShapeDtypeStruct((wide, seq), BF16)
    split = jax.ShapeDtypeStruct((heads, seq, HD), BF16)
    flat_spec = pl.BlockSpec((wide, tile), lambda i, *_: (0, i))
    split_spec = pl.BlockSpec((heads, tile, HD), lambda i, *_: (0, i, 0))
    table = pl.BlockSpec((ROT // 2, tile), lambda i, *_: (0, i))
    rows = pl.BlockSpec((tile, d), lambda i, *_: (i, 0))
    row_out = ((jax.ShapeDtypeStruct((seq, d), BF16), rows),) if gathered else ()
    return pl.pallas_call(
        functools.partial(project_kernel, slots) if gathered else project_more_kernel,
        out_shape=tuple(shape for shape, _ in row_out) + (flat,) * 3 + (split,) * 3,
        grid_spec=pltpu.PrefetchScalarGridSpec(
            num_scalar_prefetch=1 if gathered else 0,
            grid=(seq // tile,),
            in_specs=([pl.BlockSpec(memory_space=pl.ANY)] * len(pieces) if gathered else [rows])
            + [resident(weights.shape), table, table],
            out_specs=tuple(spec for _, spec in row_out) + (flat_spec,) * 3 + (split_spec,) * 3,
            scratch_shapes=[
                pltpu.VMEM((seq, d), BF16),
                pltpu.SemaphoreType.DMA((seq // tile,)),
            ]
            if gathered
            else [],
        ),
        compiler_params=params(26),
        cost_estimate=cost(2 * seq * d * 3 * wide, seq * d * 4 + d * wide * 6 + 9 * wide * seq * 2),
        name="project",
    )(*((info,) if gathered else ()), *pieces, weights, cos, sin)


def send_pieces(info_ref, step, made_ref, outs, sem, wait):
    rows = outs[0].shape[0]
    odd = info_ref[0] % 2
    for pair in range(len(outs) // 4):

        @pl.when(step == pair)
        def _():
            for u in range(2):
                for half in range(2):
                    base = pl.multiple_of((2 * jnp.bitwise_xor(u, odd) + half) * rows, rows)
                    number = 4 * pair + 2 * u + half
                    copy = pltpu.make_async_copy(
                        made_ref.at[pair, pl.ds(base, rows), :], outs[number], sem.at[number]
                    )
                    if wait:
                        copy.wait()
                    else:
                        copy.start()


def wait_all_pieces(info_ref, made_ref, outs, sem):
    for pair in range(len(outs) // 4):
        send_pieces(info_ref, pair, made_ref, outs, sem, True)


def start_weights(sources, places, sem):
    for number, (source, place) in enumerate(zip(sources, places)):
        pltpu.make_async_copy(source, place, sem.at[number]).start()


def wait_weights(step, sources, places, sem, numbers):
    @pl.when(step == 0)
    def _():
        for number in numbers:
            pltpu.make_async_copy(sources[number], places[number], sem.at[number]).wait()


def weight_places(win_ref, fc_ref, wo_ref):
    units, ph = win_ref.shape[1] // 2, wo_ref.shape[0] // 2
    return [
        win_ref.at[:, :units],
        win_ref.at[:, units:],
        fc_ref.at[:units, :],
        fc_ref.at[units:, :],
        wo_ref.at[:ph, :],
        wo_ref.at[ph:, :],
    ]


def chunks_of(count):
    width = min(256, count)
    return [slice(base, base + width) for base in range(0, count, width)]


def feed_kernel(info_ref, n_ref, ot_own, ot_other, *refs):
    sources, (b_own, b_other) = refs[:6], refs[6:8]
    hid_ref, slope_ref = refs[8:10]
    outs = refs[10:-6]
    win_ref, fc_ref, wo_ref, made_ref, sem, out_sem = refs[-6:]
    step = pl.program_id(0)
    places = weight_places(win_ref, fc_ref, wo_ref)

    @pl.when(step == 0)
    def _():
        start_weights(sources, places, sem)

    normed = n_ref[...]
    root = math.sqrt(2.0 / math.pi)
    bias = jnp.concatenate([b_own[...], b_other[...]], axis=1)
    wait_weights(step, sources, places, sem, range(6))
    cols = chunks_of(hid_ref.shape[1])
    made = None
    pre = nn(normed, win_ref[:, cols[0]])
    for number, cut in enumerate(cols):
        now = pre + bias[:, cut]
        if number + 1 < len(cols):
            pre = nn(normed, win_ref[:, cols[number + 1]])
        square = now * now
        half = 0.5 + 0.5 * jnp.tanh(now * (root + (0.044715 * root) * square))
        gelu = now * half
        slope = half + (gelu - gelu * half) * (2.0 * root + (0.26829 * root) * square)
        hid_ref[:, cut] = gelu.astype(BF16)
        slope_ref[:, cut] = slope.astype(BF16)
    hidden = hid_ref[...]
    att = jnp.concatenate([ot_own[...], ot_other[...]], axis=0).T.astype(BF16)
    for cut in chunks_of(fc_ref.shape[1]):
        made = nn(hidden, fc_ref[:, cut]) + nn(att, wo_ref[:, cut])
        made_ref[step, :, cut] = made.astype(BF16)
    send_pieces(info_ref, step, made_ref, outs, out_sem, False)

    @pl.when(step == pl.num_programs(0) - 1)
    def _():
        wait_all_pieces(info_ref, made_ref, outs, out_sem)


def paired(i, info):
    return jnp.bitwise_xor(i, info[0] // 2)


def feed(info, normed, ot, w_in, b_in, w_fc, w_out, group):
    seq, d = normed.shape
    rows = seq // group // 2
    tile = 4 * rows
    ph, units = ot[0].shape[0], 2 * w_in[0].shape[1]
    wide = 2 * ph
    unit_rows = pl.BlockSpec((tile, units), lambda i, info: (paired(i, info), 0))
    made = pl.pallas_call(
        feed_kernel,
        out_shape=(jax.ShapeDtypeStruct((seq, units), BF16),) * 2
        + (jax.ShapeDtypeStruct((rows, d), BF16),) * (2 * group),
        grid_spec=pltpu.PrefetchScalarGridSpec(
            num_scalar_prefetch=1,
            grid=(seq // tile,),
            in_specs=[
                pl.BlockSpec((tile, d), lambda i, info: (paired(i, info), 0)),
                pl.BlockSpec((ph, tile), lambda i, info: (0, paired(i, info))),
                pl.BlockSpec((ph, tile), lambda i, info: (0, paired(i, info))),
            ]
            + [pl.BlockSpec(memory_space=pl.ANY)] * 6
            + [resident(b_in[0].shape)] * 2,
            out_specs=(unit_rows,) * 2 + (pl.BlockSpec(memory_space=pl.ANY),) * (2 * group),
            scratch_shapes=[
                pltpu.VMEM((d, units), BF16),
                pltpu.VMEM((units, d), BF16),
                pltpu.VMEM((wide, d), BF16),
                pltpu.VMEM((seq // tile, tile, d), BF16),
                pltpu.SemaphoreType.DMA((6,)),
                pltpu.SemaphoreType.DMA((2 * group,)),
            ],
        ),
        compiler_params=params(44),
        cost_estimate=cost(2 * seq * d * (2 * units + wide), seq * (d * 4 + units * 4 + wide * 4) + d * units * 4, seq * units),
        name="feed",
    )(info, normed, *ot, *w_in, *w_fc, *w_out, *b_in)
    return made[0], made[1], made[2:]


def feed_back_kernel(slots, info_ref, *refs):
    count = len(slots)
    pieces, refs = refs[:count], refs[count:]
    n_any, hid_any, slope_ref, ot_own, ot_other = refs[:5]
    sources, refs = refs[5:11], refs[11:]
    gn_ref, gt_ref, gs_ref, delta_ref, keep_ref, away_ref, gwout_ref, gbin_ref = refs[:8]
    g_buf, n_buf, hid_buf, pre_buf, win_ref, fc_ref, wo_ref, acc_ref, g_sem, w_sem, sem = refs[8:]
    step = pl.program_id(0)
    last = pl.num_programs(0) - 1
    tile, units = slope_ref.shape
    ph = wo_ref.shape[0] // 2
    places = weight_places(win_ref, fc_ref, wo_ref)
    order = (2, 3, 0, 1, 4, 5)
    whole = (
        pltpu.make_async_copy(n_any, n_buf, sem.at[0]),
        pltpu.make_async_copy(hid_any, hid_buf, sem.at[1]),
    )

    @pl.when(step == 0)
    def _():
        start_weights([sources[k] for k in order[:2]], [places[k] for k in order[:2]], w_sem.at[pl.ds(2, 2)])
        start_pieces(info_ref, slots, pieces, tile // 2, g_buf, g_sem)
        for k in (0, 1, 4, 5):
            pltpu.make_async_copy(sources[k], places[k], w_sem.at[k]).start()
        for copy in whole:
            copy.start()

    wait_weights(step, sources, places, w_sem, (2, 3))
    wait_pieces(info_ref, step, tile, g_buf, g_sem)
    rows = pl.ds(pl.multiple_of(step * tile, tile), tile)
    grads = g_buf[rows, :]
    cols = chunks_of(units)
    sums = []
    for cut in cols:
        grad_pre = nt(grads, fc_ref[cut, :]) * slope_ref[:, cut].astype(F32)
        rounded = grad_pre.astype(BF16)
        pre_buf[rows, cut] = rounded
        sums.append(jnp.sum(rounded.astype(F32), axis=0, keepdims=True))
    part_b = jnp.concatenate(sums, axis=1)
    wait_weights(step, sources, places, w_sem, (0, 1, 4, 5))
    rounded = pre_buf[rows, :]
    for cut in chunks_of(gn_ref.shape[1]):
        gn_ref[:, cut] = nt(rounded, win_ref[cut, :]).astype(BF16)
    grad_att = nt(wo_ref[...], grads).astype(BF16)
    gt_ref[...] = grad_att
    ot = jnp.concatenate([ot_own[...], ot_other[...]], axis=0)
    share = grad_att.astype(F32) * ot
    for h in range(gs_ref.shape[0]):
        head = slice(h * HD, (h + 1) * HD)
        gs_ref[h] = grad_att[head].T
        delta_ref[h] = jnp.sum(share[head], axis=0, keepdims=True)
    part_out = nn(ot.astype(BF16), grads)

    @pl.when(step == 0)
    def _():
        gwout_ref[...] = part_out
        gbin_ref[...] = part_b

    @pl.when(step > 0)
    def _():
        gwout_ref[...] += part_out
        gbin_ref[...] += part_b

    @pl.when(step == last)
    def _():
        for copy in whole:
            copy.wait()
        dp_size = 2 * keep_ref.shape[0]
        each = units // 2 // dp_size
        for which, (a_buf, b_buf) in enumerate(((hid_buf, g_buf), (pre_buf, n_buf))):
            acc_ref[...] = tn(a_buf[...], b_buf[...])
            for slot in range(dp_size):
                out = (keep_ref, away_ref)[slot % 2]
                index = jnp.bitwise_xor(info_ref[1], slot)
                for shard in range(2):
                    base = pl.multiple_of(shard * (units // 2) + index * each, each)
                    out[slot // 2, shard, which * each : (which + 1) * each, :] = acc_ref[
                        pl.ds(base, each), :
                    ].astype(BF16)


def feed_back(info, blocks, normed, hidden, slope, ot, w_in, w_fc, w_out, dp_size):
    seq, d = normed.shape
    group = len(blocks)
    slots, pieces = listed(blocks)
    tile = 2 * seq // group
    ph, units = ot[0].shape[0], hidden.shape[1]
    wide = 2 * ph
    heads = wide // HD
    rows = pl.BlockSpec((tile, d), lambda i, info: (i, 0))
    unit_rows = pl.BlockSpec((tile, units), lambda i, info: (i, 0))
    turned = pl.BlockSpec((wide, tile), lambda i, info: (0, i))
    half_turned = pl.BlockSpec((ph, tile), lambda i, info: (0, i))
    packed = (dp_size // 2, 2, units // dp_size, d)
    anywhere = pl.BlockSpec(memory_space=pl.ANY)
    return pl.pallas_call(
        functools.partial(feed_back_kernel, slots),
        out_shape=(
            jax.ShapeDtypeStruct((seq, d), BF16),
            jax.ShapeDtypeStruct((wide, seq), BF16),
            jax.ShapeDtypeStruct((heads, seq, HD), BF16),
            jax.ShapeDtypeStruct((heads, 1, seq), F32),
            jax.ShapeDtypeStruct(packed, BF16),
            jax.ShapeDtypeStruct(packed, BF16),
            jax.ShapeDtypeStruct((wide, d), F32),
            jax.ShapeDtypeStruct((1, units), F32),
        ),
        grid_spec=pltpu.PrefetchScalarGridSpec(
            num_scalar_prefetch=1,
            grid=(seq // tile,),
            in_specs=[anywhere] * len(pieces)
            + [anywhere, anywhere, unit_rows, half_turned, half_turned]
            + [anywhere] * 6,
            out_specs=(
                rows,
                turned,
                pl.BlockSpec((heads, tile, HD), lambda i, info: (0, i, 0)),
                pl.BlockSpec((heads, 1, tile), lambda i, info: (0, 0, i)),
                resident(packed),
                resident(packed),
                resident((wide, d)),
                resident((1, units)),
            ),
            scratch_shapes=[
                pltpu.VMEM((seq, d), BF16),
                pltpu.VMEM((seq, d), BF16),
                pltpu.VMEM((seq, units), BF16),
                pltpu.VMEM((seq, units), BF16),
                pltpu.VMEM((d, units), BF16),
                pltpu.VMEM((units, d), BF16),
                pltpu.VMEM((wide, d), BF16),
                pltpu.VMEM((units, d), F32),
                pltpu.SemaphoreType.DMA((group // 2,)),
                pltpu.SemaphoreType.DMA((6,)),
                pltpu.SemaphoreType.DMA((2,)),
            ],
        ),
        compiler_params=params(56),
        cost_estimate=cost(2 * seq * d * (4 * units + 2 * wide), seq * (d * 6 + units * 4 + wide * 8) + d * units * 8),
        name="feed_back",
    )(info, *pieces, normed, hidden, slope, *ot, *w_in, *w_fc, *w_out)


def rows_back_kernel(count, info_ref, *refs):
    turned_refs, refs = refs[: 3 * count], refs[3 * count :]
    (n_ref, part_ref, wt_own, wt_other), refs = refs[:4], refs[4:]
    sum_ref, outs = refs[0], refs[1:-4]
    wt_ref, made_ref, sem, out_sem = refs[-4:]
    step = pl.program_id(0)
    ph = wt_own.shape[0]
    sources, places = (wt_own, wt_other), (wt_ref.at[:ph, :], wt_ref.at[ph:, :])

    @pl.when(step == 0)
    def _():
        start_weights(sources, places, sem)

    turned = jnp.concatenate([ref[...] for ref in turned_refs], axis=0)
    wait_weights(step, sources, places, sem, (0, 1))
    sums = []
    for cut in chunks_of(n_ref.shape[1]):
        made = part_ref[:, cut].astype(F32) + tn(turned, wt_ref[:, cut])
        made_ref[step, :, cut] = made.astype(BF16)
        sums.append(
            jnp.concatenate(
                [
                    jnp.sum(made * n_ref[:, cut].astype(F32), axis=0, keepdims=True),
                    jnp.sum(made, axis=0, keepdims=True),
                ],
                axis=0,
            )
        )
    sums = jnp.concatenate(sums, axis=1)
    send_pieces(info_ref, step, made_ref, outs, out_sem, False)

    @pl.when(step == pl.num_programs(0) - 1)
    def _():
        wait_all_pieces(info_ref, made_ref, outs, out_sem)

    @pl.when(step == 0)
    def _():
        sum_ref[...] = sums

    @pl.when(step > 0)
    def _():
        sum_ref[...] += sums


def rows_back(info, turned, normed, part, w_t, group):
    seq, d = normed.shape
    rows = seq // group // 2
    tile = 4 * rows
    depth = w_t[0].shape[0]
    tile_rows = pl.BlockSpec((tile, d), lambda i, info: (paired(i, info), 0))
    made = pl.pallas_call(
        functools.partial(rows_back_kernel, len(turned) // 3),
        out_shape=(jax.ShapeDtypeStruct((2, d), F32),)
        + (jax.ShapeDtypeStruct((rows, d), BF16),) * (2 * group),
        grid_spec=pltpu.PrefetchScalarGridSpec(
            num_scalar_prefetch=1,
            grid=(seq // tile,),
            in_specs=[
                pl.BlockSpec((part.shape[0], tile), lambda i, info: (0, paired(i, info)))
                for part in turned
            ]
            + [tile_rows, tile_rows]
            + [pl.BlockSpec(memory_space=pl.ANY)] * 2,
            out_specs=(resident((2, d)),) + (pl.BlockSpec(memory_space=pl.ANY),) * (2 * group),
            scratch_shapes=[
                pltpu.VMEM((2 * depth, d), BF16),
                pltpu.VMEM((seq // tile, tile, d), BF16),
                pltpu.SemaphoreType.DMA((2,)),
                pltpu.SemaphoreType.DMA((2 * group,)),
            ],
        ),
        compiler_params=params(36),
        cost_estimate=cost(2 * seq * d * 2 * depth, seq * (d * 6 + depth * 4) + d * depth * 4),
        name="rows_back",
    )(info, *turned, normed, part, *w_t)
    return made[0], made[1:]


def weights_back_kernel(info_ref, dq_ref, dk_ref, dv_ref, n_ref, gwout_ref, keep_ref, away_ref, acc_ref):
    step = pl.program_id(0)
    ph = gwout_ref.shape[0]
    turned = jnp.concatenate([dq_ref[...], dk_ref[...], dv_ref[...]], axis=0)
    part = nn(turned, n_ref[...])

    @pl.when(step == 0)
    def _():
        acc_ref[: 3 * ph, :] = part
        acc_ref[3 * ph :, :] = gwout_ref[...]

    @pl.when(step > 0)
    def _():
        acc_ref[: 3 * ph, :] += part

    @pl.when(step == pl.num_programs(0) - 1)
    def _():
        rows = keep_ref.shape[1]
        for slot in range(2 * keep_ref.shape[0]):
            out = (keep_ref, away_ref)[slot % 2]
            base = pl.multiple_of(jnp.bitwise_xor(info_ref[1], slot) * rows, rows)
            out[slot // 2] = acc_ref[pl.ds(base, rows), :].astype(BF16)


def weights_back(info, turned, normed, gw_out, shard, group, dp_size):
    seq, d = normed.shape
    tile = 2 * seq // group
    ph = turned[0].shape[0]
    packed = (dp_size // 2, 4 * ph // dp_size, d)
    return pl.pallas_call(
        weights_back_kernel,
        out_shape=(jax.ShapeDtypeStruct(packed, BF16),) * 2,
        grid_spec=pltpu.PrefetchScalarGridSpec(
            num_scalar_prefetch=1,
            grid=(seq // tile,),
            in_specs=[pl.BlockSpec((ph, tile), lambda i, info: (0, i))] * 3
            + [
                pl.BlockSpec((tile, d), lambda i, info: (i, 0)),
                pl.BlockSpec((ph, d), lambda i, info: (shard, 0)),
            ],
            out_specs=(resident(packed),) * 2,
            scratch_shapes=[pltpu.VMEM((4 * ph, d), F32)],
        ),
        compiler_params=params(20),
        cost_estimate=cost(2 * seq * d * 3 * ph, seq * (d * 2 + ph * 6) + d * ph * 16),
        name="weights_back",
    )(info, *turned, normed, gw_out)


def finish_feed_kernel(info_ref, *refs):
    pieces, (gin_ref, gfc_ref) = refs[:-2], refs[-2:]
    rows = gfc_ref.shape[0]
    for slot, piece in enumerate(pieces):

        @pl.when(pl.program_id(0) == slot)
        def _():
            gfc_ref[...] = piece[:rows, :].astype(F32)
            gin_ref[...] = piece[rows:, :].astype(F32).T


def finish_feed(info, pieces, units):
    count = len(pieces)
    d = pieces[0].shape[1]
    return pl.pallas_call(
        finish_feed_kernel,
        out_shape=(jax.ShapeDtypeStruct((d, units), F32), jax.ShapeDtypeStruct((units, d), F32)),
        grid_spec=pltpu.PrefetchScalarGridSpec(
            num_scalar_prefetch=1,
            grid=(count,),
            in_specs=[resident(pieces[0].shape)] * count,
            out_specs=(
                pl.BlockSpec((d, units // count), lambda i, info: (0, jnp.bitwise_xor(i, info[1]))),
                pl.BlockSpec((units // count, d), lambda i, info: (jnp.bitwise_xor(i, info[1]), 0)),
            ),
        ),
        compiler_params=params(16),
        cost_estimate=cost(0, d * units * 12),
        name="finish_feed",
    )(info, *pieces)


def finish_project_kernel(info_ref, *refs):
    pieces, (gqkv_ref, gout_ref) = refs[:-2], refs[-2:]
    index = pl.program_id(0)
    slot_now = jnp.bitwise_xor(index, info_ref[1])
    for slot, piece in enumerate(pieces):

        @pl.when((slot_now == slot) & (index < 3))
        def _():
            gqkv_ref[0] = piece[...].astype(F32).T

        @pl.when((slot_now == slot) & (index == 3))
        def _():
            gout_ref[...] = piece[...].astype(F32)


def finish_project(info, pieces):
    rows, d = pieces[0].shape
    return pl.pallas_call(
        finish_project_kernel,
        out_shape=(jax.ShapeDtypeStruct((3, d, rows), F32), jax.ShapeDtypeStruct((rows, d), F32)),
        grid_spec=pltpu.PrefetchScalarGridSpec(
            num_scalar_prefetch=1,
            grid=(4,),
            in_specs=[resident((rows, d))] * 4,
            out_specs=(
                pl.BlockSpec((1, d, rows), lambda i, info: (jnp.minimum(i, 2), 0, 0)),
                resident((rows, d)),
            ),
        ),
        compiler_params=params(16),
        cost_estimate=cost(0, d * rows * 24),
        name="finish_project",
    )(info, *pieces)


def mask_scores(scores, start, key_base, query_base, diagonal):
    key_places = key_base + lax.broadcasted_iota(jnp.int32, scores.shape, 0)
    keep = key_places >= start
    if diagonal:
        query_places = query_base + lax.broadcasted_iota(jnp.int32, scores.shape, 1)
        keep = keep & (key_places <= query_places)
    return jnp.where(keep, scores, NEG_LARGE)


def attend_kernel(low_ref, start_ref, qt_ref, k_ref, vt_ref, ot_ref, lse_ref, m_ref, l_ref, acc_ref):
    block = qt_ref.shape[1]
    i = pl.program_id(1)
    queries = qt_ref[...]
    start = start_ref[...]

    def step(j, diagonal):
        base = pl.multiple_of(j * block, block)
        scores = nn(k_ref[0, pl.ds(base, block), :], queries)
        scores = mask_scores(scores, start, base, i * block, diagonal)
        peak = jnp.max(scores, axis=0, keepdims=True)
        values = vt_ref[:, pl.ds(base, block)]
        if diagonal:
            weights = jnp.exp(scores - peak)
            m_ref[...] = peak
            l_ref[...] = jnp.sum(weights, axis=0, keepdims=True)
            acc_ref[...] = nn(values, weights.astype(BF16))
        else:
            before = m_ref[...]
            peak = jnp.maximum(before, peak)
            shrink = jnp.exp(before - peak)
            weights = jnp.exp(scores - peak)
            m_ref[...] = peak
            l_ref[...] = l_ref[...] * shrink + jnp.sum(weights, axis=0, keepdims=True)
            acc_ref[...] = acc_ref[...] * shrink + nn(values, weights.astype(BF16))

    step(i, True)

    def body(j, carry):
        step(j, False)
        return carry

    lax.fori_loop(low_ref[i], i, body, 0)
    total = l_ref[...]
    ot_ref[...] = acc_ref[...] * (1.0 / total)
    lse_ref[0] = m_ref[...] + jnp.log(total)


def attend(low, start, qt, k, vt, block, base, heads):
    seq = qt.shape[1]
    blocks = seq // block
    return pl.pallas_call(
        attend_kernel,
        out_shape=(
            jax.ShapeDtypeStruct((heads * HD, seq), F32),
            jax.ShapeDtypeStruct((heads, 1, seq), F32),
        ),
        grid_spec=pltpu.PrefetchScalarGridSpec(
            num_scalar_prefetch=1,
            grid=(heads, blocks),
            in_specs=[
                pl.BlockSpec((1, block), lambda h, i, low: (0, i)),
                pl.BlockSpec((HD, block), lambda h, i, low: (base + h, i)),
                pl.BlockSpec((1, seq, HD), lambda h, i, low: (base + h, 0, 0)),
                pl.BlockSpec((HD, seq), lambda h, i, low: (base + h, 0)),
            ],
            out_specs=(
                pl.BlockSpec((HD, block), lambda h, i, low: (h, i)),
                pl.BlockSpec((1, 1, block), lambda h, i, low: (h, 0, i)),
            ),
            scratch_shapes=[
                pltpu.VMEM((1, block), F32),
                pltpu.VMEM((1, block), F32),
                pltpu.VMEM((HD, block), F32),
            ],
        ),
        compiler_params=params(12),
        cost_estimate=cost(heads * seq * seq * 512, heads * seq * HD * 12, heads * seq * seq // 2),
        name="attend",
    )(low, start, qt, k, vt)


def attend_back_kernel(
    high_ref, start_ref, lse_ref, delta_ref, cos_ref, sin_ref, qt_ref, kt_ref, gt_ref, q_ref, k_ref, v_ref, g_ref,
    dqt_out, dkt_out, dvt_out, dqt_ref, dk_ref, dv_ref
):
    seq = qt_ref.shape[1]
    blocks = high_ref.shape[0]
    block = seq // blocks
    dqt_ref[...] = jnp.zeros_like(dqt_ref)

    def pair(i, j, diagonal):
        qs = pl.ds(pl.multiple_of(i * block, block), block)
        ks = pl.ds(pl.multiple_of(j * block, block), block)
        scores = nn(k_ref[0, ks, :], qt_ref[:, qs])
        scores = mask_scores(scores, start_ref[:, qs], j * block, i * block, diagonal)
        probs = jnp.exp(scores - lse_ref[0, :, qs])
        grad_probs = nn(v_ref[0, ks, :], gt_ref[:, qs])
        grad_scores = (probs * (grad_probs - delta_ref[0, :, qs])).astype(BF16)
        dv = nn(probs.astype(BF16), g_ref[0, qs, :])
        dk = nn(grad_scores, q_ref[0, qs, :])
        if diagonal:
            dv_ref[ks, :] = dv
            dk_ref[ks, :] = dk
        else:
            dv_ref[ks, :] += dv
            dk_ref[ks, :] += dk
        dqt_ref[:, qs] += nn(kt_ref[:, ks], grad_scores)

    def keys(j, carry):
        pair(j, j, True)

        def queries(i, inner):
            pair(i, j, False)
            return inner

        lax.fori_loop(j + 1, high_ref[j], queries, 0)
        return carry

    lax.fori_loop(0, blocks, keys, 0)
    cos, sin = cos_ref[...], sin_ref[...]
    half = ROT // 2

    def store(out, t):
        a, b = t[:half], t[half:ROT]
        out[:half] = (a * cos + b * sin).astype(BF16)
        out[half:ROT] = (b * cos - a * sin).astype(BF16)
        out[ROT:] = t[ROT:].astype(BF16)

    store(dqt_out, dqt_ref[...] * (HD**-0.5))
    store(dkt_out, dk_ref[...].T)
    dvt_out[...] = dv_ref[...].T.astype(BF16)


def attend_back(high, start, lse, delta, cos, sin, qt, kt, gt, q, k, v, g, base, local, heads, mib):
    seq = qt.shape[1]
    flat = pl.BlockSpec((HD, seq), lambda h, high: (local + h, 0))
    split = pl.BlockSpec((1, seq, HD), lambda h, high: (local + h, 0, 0))
    both_flat = pl.BlockSpec((HD, seq), lambda h, high: (base + h, 0))
    both_split = pl.BlockSpec((1, seq, HD), lambda h, high: (base + h, 0, 0))
    row = pl.BlockSpec((1, seq), lambda h, high: (0, 0))
    head_row = pl.BlockSpec((1, 1, seq), lambda h, high: (base + h, 0, 0))
    own_row = pl.BlockSpec((1, 1, seq), lambda h, high: (local + h, 0, 0))
    table = pl.BlockSpec((ROT // 2, seq), lambda h, high: (0, 0))
    return pl.pallas_call(
        attend_back_kernel,
        out_shape=(jax.ShapeDtypeStruct((heads * HD, seq), BF16),) * 3,
        grid_spec=pltpu.PrefetchScalarGridSpec(
            num_scalar_prefetch=1,
            grid=(heads,),
            in_specs=[row, own_row, head_row, table, table]
            + [flat, flat, both_flat]
            + [split, split, split, both_split],
            out_specs=(pl.BlockSpec((HD, seq), lambda h, high: (h, 0)),) * 3,
            scratch_shapes=[
                pltpu.VMEM((HD, seq), F32),
                pltpu.VMEM((seq, HD), F32),
                pltpu.VMEM((seq, HD), F32),
            ],
        ),
        compiler_params=params(mib),
        cost_estimate=cost(heads * seq * seq * 1280, heads * HD * seq * 24, heads * seq * seq // 2),
        name="attend_back",
    )(high, start, lse, delta, cos, sin, qt, kt, gt, q, k, v, g)


def run_starts(segments):
    places = lax.broadcasted_iota(jnp.int32, segments.shape, 1)
    leading = jnp.ones_like(segments[:, :1])
    changes = jnp.concatenate(
        [leading, (segments[:, 1:] != segments[:, :-1]).astype(jnp.int32)], axis=1
    )
    starts = lax.cummax(places * changes, axis=1)
    return places, starts


def build(dp_size, tensor_size):
    def per_device(
        inputs, segments, norm_gain, norm_bias, w_qkv, w_out, w_in, b_in, w_fc, b_out, cotangent
    ):
        row_count, seq = segments.shape
        tokens, d = inputs.shape
        group = tensor_size // row_count
        half_rot = ROT // 2
        block = 512
        me = lax.axis_index("tensor")
        dp = lax.axis_index("dp")
        row = me // group
        info = jnp.stack([me % group, dp]).astype(jnp.int32)
        other = [(i, (i + group) % tensor_size) for i in range(tensor_size)]
        bits = bit_list(group)
        dp_bits = bit_list(dp_size)
        def normalize(rows):
            rows = rows.astype(F32)
            centred = rows - jnp.mean(rows, axis=-1, keepdims=True)
            inv_std = lax.rsqrt(jnp.mean(centred * centred, axis=-1, keepdims=True) + EPSILON)
            return centred * inv_std, inv_std

        normed_own = [
            (normalize(half)[0] * norm_gain + norm_bias).astype(BF16) for half in halves_of(inputs)
        ]
        n_got = gather_own(normed_own, tensor_size, bits)
        lead = ((bits[0], 0), (bits[-1], 1))

        def slice_of(indexed):
            return lax.dynamic_index_in_dim(indexed, dp, 0, keepdims=False)

        def fetch(part):
            return lax.ppermute(part, "tensor", other)

        def share(got):
            return gather_slots(got, "dp", dp_size, dp_bits[::-1])

        def rows_of(pieces, start, stop):
            return natural({k: pieces[k][start:stop] for k in pieces}, dp)

        units, per_head = w_in.shape[1], w_qkv.shape[2]
        shard_heads = per_head // HD
        fc_rows = units // dp_size
        qkv_slice = slice_of(w_qkv.reshape(dp_size, -1, per_head))
        in_slice = slice_of(w_in.reshape(dp_size, -1, units))
        fc_slice = jnp.concatenate(
            [slice_of(w_fc.reshape(dp_size, -1, d)), slice_of(w_out.reshape(dp_size, -1, d))], axis=0
        )
        wt_own = jnp.concatenate([w_qkv[c].T for c in range(3)], axis=0)

        segs = lax.dynamic_slice_in_dim(segments, row, 1, axis=0)
        places, starts = run_starts(segs)
        first_key = jnp.where(segs >= 0, starts, places)
        offsets = (places - starts).astype(F32)
        frequency = jnp.exp(
            lax.broadcasted_iota(F32, (half_rot,), 0) * (-2.0 * math.log(10000.0) / ROT)
        )
        angles = frequency[:, None] * offsets
        cos_t, sin_t = jnp.cos(angles), jnp.sin(angles)
        blocks = seq // block
        low = (jnp.min(first_key.reshape(blocks, block), axis=1) // block).astype(jnp.int32)
        reach = low[None, :] <= jnp.arange(blocks)[:, None]
        high = jnp.max(
            jnp.where(reach, jnp.arange(1, blocks + 1, dtype=jnp.int32)[None, :], 0), axis=1
        ).astype(jnp.int32)

        prepared = (wt_own, cos_t, sin_t, first_key, low, high)
        n_lead = {key: n_got[key] for key in lead}
        n_lead, (qkv_slice, in_slice, fc_slice), prepared = tie(
            n_lead, (qkv_slice, in_slice, fc_slice), prepared
        )
        n_got = {**n_got, **n_lead}
        wt_own, cos_t, sin_t, first_key, low, high = prepared
        n_blocks = gather_rest(normed_own, n_got, tensor_size, bits)
        qkv_got, in_got, fc_got, b_in_other = (
            fetch(part) for part in (qkv_slice, in_slice, fc_slice, b_in)
        )
        n_blocks, cot = tie(n_blocks, cotangent)
        cot = halves_of(cot)
        g_got = gather_own(cot, tensor_size, bits)

        def heads_forward(made, base, count):
            return attend(low, first_key, made[0], made[4], made[2], block, base, count)

        cut = shard_heads // 2
        made = project(info, n_blocks, wt_own, cos_t, sin_t)
        normed, own = made[0], made[1:]
        attended = []
        if cut:
            attended.append(heads_forward(own, 0, cut))
            (attended[0], qkv_got), own = tie((attended[0], qkv_got), own)
        qkv_pieces = share(qkv_got)
        attended.append(heads_forward(own, cut, shard_heads - cut))
        attended[-1], qkv_pieces, in_got, normed = tie(attended[-1], qkv_pieces, in_got, normed)
        qkv_other = rows_of(qkv_pieces, 0, None).reshape(w_qkv.shape)
        wt_other = jnp.concatenate([qkv_other[c].T for c in range(3)], axis=0)
        in_pieces = share(in_got)
        rest = project(None, normed, wt_other, cos_t, sin_t)
        attended_rest = []
        if cut:
            attended_rest.append(heads_forward(rest, 0, cut))
            attended_rest[0], in_pieces, fc_got, g_got, rest = tie(
                attended_rest[0], in_pieces, fc_got, g_got, rest
            )
        fc_pieces = share(fc_got)
        w_in_other = rows_of(in_pieces, 0, None)
        g_blocks = gather_rest(cot, g_got, tensor_size, bits)
        attended_rest.append(heads_forward(rest, cut, shard_heads - cut))
        attended_rest[-1], fc_pieces, w_in_other = tie(attended_rest[-1], fc_pieces, w_in_other)
        (ot_own, lse_own), (ot_other, lse_other) = (
            tuple(jnp.concatenate([part[n] for part in parts], axis=0) for n in range(2))
            for parts in (attended, attended_rest)
        )
        w_fc_other = rows_of(fc_pieces, 0, fc_rows)
        w_out_other = rows_of(fc_pieces, fc_rows, None)
        ot = (ot_own, ot_other)
        w_in_both, w_fc_both, w_out_both = (w_in, w_in_other), (w_fc, w_fc_other), (w_out, w_out_other)
        hidden, slope, out_pieces = feed(
            info, normed, ot, w_in_both, (b_in[None], b_in_other[None]), w_fc_both, w_out_both, group
        )

        def by_slot(pieces):
            return {(k, half): pieces[2 * k + half] for k in range(group) for half in range(2)}

        last_stage = len(bits) - 1
        out_parts = by_slot(out_pieces)
        out_got = reduce_sends(out_parts, tensor_size, bits, last_stage)
        out_early = reduce_early(out_parts, tensor_size, bits)
        made = feed_back(
            info, g_blocks, normed, hidden, slope, ot, w_in_both, w_fc_both, w_out_both, dp_size
        )
        made, out_got, out_early = tie(made, out_got, out_early)
        gn_part, gt, g_heads, delta, keep1, away1, gw_out, gb_in = made
        out_parts = reduce_adds(out_parts, out_got)
        for stage in range(last_stage - 1, 0, -1):
            out_parts = reduce_adds(out_parts, reduce_sends(out_parts, tensor_size, bits, stage))

        def settle_dp(parts, bit):
            got = {
                k ^ bit: [swap(part, "dp", dp_size, bit) for part in parts[k]]
                for k in sorted(parts)
                if k & bit
            }
            return {k: parts[k] for k in got}, got

        def settle_add(kept, got):
            return {k: tuple(add(a, b) for a, b in zip(kept[k], got[k])) for k in kept}

        def settle_rest(parts, got):
            for bit in dp_bits[2:]:
                parts, got = settle_dp(settle_add(parts, got), bit)
            return settle_add(parts, got)[0]

        share_bits = dp_bits[::-1]

        def heads_back(shard):
            qt, kt, vt, q, k, v = (own, rest)[shard]
            return attend_back(
                high, first_key, (lse_own, lse_other)[shard], delta, cos_t, sin_t, qt, kt, gt, q, k, v, g_heads,
                shard * shard_heads, 0, shard_heads, (20, 56)[shard]
            )

        got1 = swap(away1, "dp", dp_size, dp_bits[0])
        got1, out_parts, gt = tie(got1, out_parts, gt)
        sums1 = {
            2 * j: tuple(add(keep1[j, s], got1[j, s]) for s in range(2)) for j in range(dp_size // 2)
        }
        sums1, out_parts, gt = tie(sums1, out_parts, gt)
        out_got = reduce_late(out_parts, out_early, tensor_size, bits)
        kept1, got1 = settle_dp(sums1, dp_bits[1])
        turned_other = heads_back(1)
        keep2, away2 = weights_back(info, turned_other, normed, gw_out, 1, group, dp_size)
        keep2, away2, got1, gt = tie(keep2, away2, got1, gt)
        got2 = swap(away2, "dp", dp_size, dp_bits[0])
        own1, other1 = settle_rest(kept1, got1)
        own1, other1, got2, gt = tie(own1, other1, got2, gt)
        sums2 = {2 * j: (add(keep2[j], got2[j]),) for j in range(dp_size // 2)}
        sums2, other1, gt = tie(sums2, other1, gt)
        kept2, got2 = settle_dp(sums2, dp_bits[1])
        other1 = fetch(other1)
        turned_own = heads_back(0)
        turned_own, got2, other1, out_got = tie(turned_own, got2, other1, out_got)
        (other2,) = settle_rest(kept2, got2)
        total1 = add(own1, other1)
        turned_own, total1, other2 = tie(turned_own, total1, other2)
        other2_got = fetch(other2)
        pieces1 = gather_slots(total1, "dp", dp_size, share_bits[:1])
        sums, gn_pieces = rows_back(
            info, [*turned_own, *turned_other], normed, gn_part, (wt_own, wt_other), group
        )
        gn_parts = by_slot(gn_pieces)
        gn_got = reduce_sends(gn_parts, tensor_size, bits, last_stage)

        bias_parts = jnp.zeros((tensor_size, units), F32)
        bias_parts = lax.dynamic_update_slice_in_dim(bias_parts, gb_in[:, :units], me, axis=0)
        bias_parts = lax.dynamic_update_slice_in_dim(
            bias_parts, gb_in[:, units:], (me + group) % tensor_size, axis=0
        )
        cotangent_f = cotangent.astype(F32)
        total = jnp.concatenate(
            [sums, jnp.sum(cotangent_f, axis=0, keepdims=True), bias_parts.reshape(-1, d)], axis=0
        )
        total, turned_own = tie(total, turned_own)
        total_got = swap(total, "dp", dp_size, dp_bits[0])
        keep3, away3 = weights_back(info, turned_own, normed, gw_out, 0, group, dp_size)
        keep3, away3, pieces1, total_got = tie(keep3, away3, pieces1, total_got)
        gn_early = reduce_early(gn_parts, tensor_size, bits)
        got3 = swap(away3, "dp", dp_size, dp_bits[0])
        pieces1 = gather_more(pieces1, "dp", dp_size, share_bits[1:])
        total = total + total_got
        for bit in dp_bits[1:]:
            total = total + swap(total, "dp", dp_size, bit)
        got3, pieces1, total, gn_got, other2_got = tie(got3, pieces1, total, gn_got, other2_got)
        gn_parts = reduce_adds(gn_parts, gn_got)
        for number in range(last_stage - 1, 0, -1):
            gn_parts = reduce_adds(gn_parts, reduce_sends(gn_parts, tensor_size, bits, number))
        sums3 = {2 * j: (add(keep3[j], got3[j]),) for j in range(dp_size // 2)}
        gn_parts, sums3, pieces1, total = tie(gn_parts, sums3, pieces1, total)
        gn_got = reduce_late(gn_parts, gn_early, tensor_size, bits)
        kept3, got3 = settle_dp(sums3, dp_bits[1])
        total_got = [swap(total, "tensor", tensor_size, k) for k in range(2, tensor_size, 2)]
        pieces1 = [pieces1[k] for k in range(dp_size)]
        if fc_rows % LANES == 0:
            grad_in, grad_fc = finish_feed(info, pieces1, units)
        else:
            pieces1 = dict(enumerate(pieces1))
            grad_fc = rows_of(pieces1, 0, fc_rows).astype(F32)
            grad_in = rows_of(pieces1, fc_rows, None).T.astype(F32)
        kept3, got3, grad_in, grad_fc, out_parts = tie(kept3, got3, grad_in, grad_fc, out_parts)
        (own3,) = settle_rest(kept3, got3)
        total2 = add(own3, other2_got)
        pieces2 = gather_slots(total2, "dp", dp_size, share_bits)
        output = (inputs.astype(F32) + reduce_total(out_parts, {**out_early, **out_got}) + b_out).astype(BF16)
        pieces2 = [pieces2[k] for k in range(dp_size)]
        if dp_size == 4 and per_head % LANES == 0:
            grad_qkv, grad_out = finish_project(info, pieces2)
        else:
            stacked = natural(dict(enumerate(pieces2)), dp)
            grad_qkv = jnp.swapaxes(
                stacked[: 3 * per_head].reshape(3, per_head, d), 1, 2
            ).astype(F32)
            grad_out = stacked[3 * per_head :].astype(F32)
        gn_got, gn_parts, total_got, grad_qkv, grad_out, output = tie(
            {**gn_early, **gn_got}, gn_parts, total_got, grad_qkv, grad_out, output
        )
        for part in total_got:
            total = total + part
        total = total + swap(total, "tensor", tensor_size, 1)

        unit_rows, inv_std = normalize(inputs)
        grad_norm_own = reduce_total(gn_parts, gn_got)
        scaled = grad_norm_own * norm_gain
        grad_local = inv_std * (
            scaled
            - jnp.mean(scaled, axis=-1, keepdims=True)
            - unit_rows * jnp.mean(scaled * unit_rows, axis=-1, keepdims=True)
        )
        grad_inputs = cotangent_f + grad_local

        grad_bias = total[1]
        grad_gain = (total[0] - norm_bias * grad_bias) / norm_gain
        grad_b_out = total[2]
        grad_b_in = lax.dynamic_slice_in_dim(total[3:].reshape(tensor_size, units), me, 1, axis=0)[0]
        return (
            output,
            grad_inputs,
            grad_gain,
            grad_bias,
            grad_qkv,
            grad_out,
            grad_in,
            grad_b_in,
            grad_fc,
            grad_b_out,
        )

    return per_device


def solution(mesh):
    tokens = P(("dp", "tensor"), None)
    return jax.shard_map(
        build(mesh.shape["dp"], mesh.shape["tensor"]),
        mesh=mesh,
        in_specs=(
            tokens,
            P("dp", None),
            P(),
            P(),
            P(None, None, "tensor"),
            P("tensor", None),
            P(None, "tensor"),
            P("tensor"),
            P("tensor", None),
            P(),
            tokens,
        ),
        out_specs=(
            tokens,
            tokens,
            P(),
            P(),
            P(None, None, "tensor"),
            P("tensor", None),
            P(None, "tensor"),
            P("tensor"),
            P("tensor", None),
            P(),
        ),
        check_vma=False,
    )
```

```python
import functools
import math

import jax
import jax.numpy as jnp
from jax import lax
from jax.experimental import pallas as pl
from jax.experimental.pallas import tpu as pltpu
from jax.sharding import PartitionSpec as P

HD = 64
ROT = 32
EPSILON = 1e-05
NEG_LARGE = -1e30
BF16 = jnp.bfloat16
F32 = jnp.float32
LANES = 128
MIB = 1024 * 1024


def nn(a, b):
    return lax.dot_general(a, b, (((1,), (0,)), ((), ())), preferred_element_type=F32)


def nt(a, b):
    return lax.dot_general(a, b, (((1,), (1,)), ((), ())), preferred_element_type=F32)


def tn(a, b):
    return lax.dot_general(a, b, (((0,), (0,)), ((), ())), preferred_element_type=F32)


def resident(shape):
    return pl.BlockSpec(shape, lambda *_: (0,) * len(shape), pipeline_mode=pl.Buffered(1))


def params(mib):
    return pltpu.CompilerParams(vmem_limit_bytes=mib * MIB)


def cost(flops, moved, trans=0):
    return pl.CostEstimate(flops=int(flops), bytes_accessed=int(moved), transcendentals=int(trans))


def bit_list(count):
    return [1 << n for n in range(count.bit_length() - 1)]


def swap(array, axis, size, bit):
    return lax.ppermute(array, axis, [(i, i ^ bit) for i in range(size)])


def tie(*groups):
    return lax.optimization_barrier(groups)


def halves_of(block):
    rows = block.shape[0] // 2
    return block[:rows], block[rows:]


def forwards(bits):
    steps = []
    for number in range(1, len(bits)):
        for half, order in enumerate((bits, bits[::-1])):
            for k in range(1, 2 ** len(bits)):
                if not any(k & bit for bit in order[number:]):
                    steps.append((number, half, k, k ^ order[number], order[number]))
    return steps


def gather_lead(halves, size, bits):
    orders = (bits, bits[::-1])
    return {(order[0], half): swap(halves[half], "tensor", size, order[0]) for half, order in enumerate(orders)}


def gather_own(halves, size, bits):
    orders = (bits, bits[::-1])
    return {
        (bit, half): swap(halves[half], "tensor", size, bit)
        for half, order in enumerate(orders)
        for bit in order[1:]
    }


def gather_rest(halves, got, size, bits):
    parts = {**got, (0, 0): halves[0], (0, 1): halves[1]}
    for _, half, k, made, bit in forwards(bits):
        parts[made, half] = swap(parts[k, half], "tensor", size, bit)
    return {k: (parts[k, 0], parts[k, 1]) for k in range(2 ** len(bits))}


def add(a, b):
    return (a.astype(F32) + b.astype(F32)).astype(a.dtype)


def reduce_sends(pieces, size, bits, stage):
    return {
        (k, half): swap(pieces[made, half], "tensor", size, bit)
        for number, half, k, made, bit in reversed(forwards(bits))
        if number == stage
    }


def reduce_adds(pieces, got):
    return {key: add(pieces[key], got[key]) if key in got else pieces[key] for key in pieces}


def reduce_early(pieces, size, bits):
    waiting = {(k, half) for _, half, k, _, _ in forwards(bits)}
    return {
        (bit, half): swap(pieces[bit, half], "tensor", size, bit)
        for bit in bits
        for half in range(2)
        if (bit, half) not in waiting
    }


def reduce_late(pieces, early, size, bits):
    return {
        (bit, half): swap(pieces[bit, half], "tensor", size, bit)
        for bit in bits
        for half in range(2)
        if (bit, half) not in early
    }


def reduce_total(pieces, got):
    halves = []
    for half in range(2):
        total = pieces[0, half].astype(F32)
        for k, which in sorted(got):
            if which == half:
                total = total + got[k, half].astype(F32)
        halves.append(total)
    return jnp.concatenate(halves, axis=0)


def gather_slots(mine, axis, size, bits):
    return gather_more({0: mine}, axis, size, bits)


def gather_more(pieces, axis, size, bits):
    pieces = dict(pieces)
    for bit in bits:
        for k in sorted(pieces):
            pieces[k ^ bit] = swap(pieces[k], axis, size, bit)
    return pieces


def natural(pieces, me):
    for bit in bit_list(len(pieces)):
        odd = (me & bit) != 0
        pieces = {k: jnp.where(odd, pieces[k ^ bit], pieces[k]) for k in pieces}
    return jnp.concatenate([pieces[k] for k in range(len(pieces))], axis=0)


def turn_rows(t, cos, sin):
    half = ROT // 2
    a, b = t[:half], t[half:ROT]
    return jnp.concatenate([a * cos - b * sin, b * cos + a * sin, t[ROT:]], axis=0)


def start_pieces(info_ref, slots, refs, tokens, buf_ref, sem):
    for (k, place), piece in zip(slots, refs):
        rows = piece.shape[0]
        base = pl.multiple_of(jnp.bitwise_xor(info_ref[0], k) * tokens + place * rows, rows)
        pltpu.make_async_copy(piece, buf_ref.at[pl.ds(base, rows), :], sem.at[k // 2]).start()


def listed(blocks):
    order = [(k, place) for k in sorted(blocks) for place in range(len(blocks[k]))]
    return order, [blocks[k][place] for k, place in order]


def wait_pieces(info_ref, step, tile, buf_ref, sem):
    which = jnp.bitwise_xor(step, info_ref[0] // 2)
    view = buf_ref.at[pl.ds(0, tile), :]
    pltpu.make_async_copy(view, view, sem.at[which]).wait()


def project_kernel(slots, info_ref, *refs):
    count = len(slots)
    pieces = refs[:count]
    wt_ref, cos_ref, sin_ref = refs[count : count + 3]
    n_ref, qt_ref, kt_ref, vt_ref, q_ref, k_ref, v_ref = refs[count + 3 : count + 10]
    step = pl.program_id(0)
    tile = n_ref.shape[0]
    wide = qt_ref.shape[0]
    buf_ref, sem = refs[count + 10 :]

    @pl.when(step == 0)
    def _():
        start_pieces(info_ref, slots, pieces, tile // 2, buf_ref, sem)

    wait_pieces(info_ref, step, tile, buf_ref, sem)
    normed = buf_ref[pl.ds(pl.multiple_of(step * tile, tile), tile), :]
    n_ref[...] = normed
    store_heads(wt_ref, normed, cos_ref, sin_ref, qt_ref, kt_ref, vt_ref, q_ref, k_ref, v_ref)


def project_more_kernel(n_ref, wt_ref, cos_ref, sin_ref, *outs):
    store_heads(wt_ref, n_ref[...], cos_ref, sin_ref, *outs)


def store_heads(wt_ref, normed, cos_ref, sin_ref, qt_ref, kt_ref, vt_ref, q_ref, k_ref, v_ref):
    wide = qt_ref.shape[0]
    made = nt(wt_ref[...], normed)
    cos, sin = cos_ref[...], sin_ref[...]
    scale = HD**-0.5
    for h in range(wide // HD):
        for which, t_ref, h_ref in ((0, qt_ref, q_ref), (1, kt_ref, k_ref), (2, vt_ref, v_ref)):
            base = which * wide + h * HD
            t = made[base : base + HD]
            if which < 2:
                t = turn_rows(t, cos, sin)
            t = t.astype(BF16)
            if which == 0:
                t = (t.astype(F32) * scale).astype(BF16)
            t_ref[h * HD : (h + 1) * HD, :] = t
            h_ref[h] = t.T


def project(info, blocks, weights, cos, sin):
    gathered = isinstance(blocks, dict)
    slots, pieces = listed(blocks) if gathered else ([], [blocks])
    if gathered:
        group = len(blocks)
        tokens, d = sum(part.shape[0] for part in blocks[0]), blocks[0][0].shape[1]
        seq = group * tokens
        tile = 2 * tokens
    else:
        seq, d = blocks.shape
        tile = seq // 2
    wide = weights.shape[0] // 3
    heads = wide // HD
    flat = jax.ShapeDtypeStruct((wide, seq), BF16)
    split = jax.ShapeDtypeStruct((heads, seq, HD), BF16)
    flat_spec = pl.BlockSpec((wide, tile), lambda i, *_: (0, i))
    split_spec = pl.BlockSpec((heads, tile, HD), lambda i, *_: (0, i, 0))
    table = pl.BlockSpec((ROT // 2, tile), lambda i, *_: (0, i))
    rows = pl.BlockSpec((tile, d), lambda i, *_: (i, 0))
    row_out = ((jax.ShapeDtypeStruct((seq, d), BF16), rows),) if gathered else ()
    return pl.pallas_call(
        functools.partial(project_kernel, slots) if gathered else project_more_kernel,
        out_shape=tuple(shape for shape, _ in row_out) + (flat,) * 3 + (split,) * 3,
        grid_spec=pltpu.PrefetchScalarGridSpec(
            num_scalar_prefetch=1 if gathered else 0,
            grid=(seq // tile,),
            in_specs=([pl.BlockSpec(memory_space=pl.ANY)] * len(pieces) if gathered else [rows])
            + [resident(weights.shape), table, table],
            out_specs=tuple(spec for _, spec in row_out) + (flat_spec,) * 3 + (split_spec,) * 3,
            scratch_shapes=[
                pltpu.VMEM((seq, d), BF16),
                pltpu.SemaphoreType.DMA((seq // tile,)),
            ]
            if gathered
            else [],
        ),
        compiler_params=params(26),
        cost_estimate=cost(2 * seq * d * 3 * wide, seq * d * 4 + d * wide * 6 + 9 * wide * seq * 2),
        name="project",
    )(*((info,) if gathered else ()), *pieces, weights, cos, sin)


def send_pieces(info_ref, step, made_ref, outs, sem, wait):
    rows = outs[0].shape[0]
    odd = info_ref[0] % 2
    for pair in range(len(outs) // 4):

        @pl.when(step == pair)
        def _():
            for u in range(2):
                for half in range(2):
                    base = pl.multiple_of((2 * jnp.bitwise_xor(u, odd) + half) * rows, rows)
                    number = 4 * pair + 2 * u + half
                    copy = pltpu.make_async_copy(
                        made_ref.at[pair, pl.ds(base, rows), :], outs[number], sem.at[number]
                    )
                    if wait:
                        copy.wait()
                    else:
                        copy.start()


def wait_all_pieces(info_ref, made_ref, outs, sem):
    for pair in range(len(outs) // 4):
        send_pieces(info_ref, pair, made_ref, outs, sem, True)


def start_weights(sources, places, sem):
    for number, (source, place) in enumerate(zip(sources, places)):
        pltpu.make_async_copy(source, place, sem.at[number]).start()


def wait_weights(step, sources, places, sem, numbers):
    @pl.when(step == 0)
    def _():
        for number in numbers:
            pltpu.make_async_copy(sources[number], places[number], sem.at[number]).wait()


def weight_places(win_ref, fc_ref, wo_ref):
    units, ph = win_ref.shape[1] // 2, wo_ref.shape[0] // 2
    return [
        win_ref.at[:, :units],
        win_ref.at[:, units:],
        fc_ref.at[:units, :],
        fc_ref.at[units:, :],
        wo_ref.at[:ph, :],
        wo_ref.at[ph:, :],
    ]


def chunks_of(count):
    width = min(256, count)
    return [slice(base, base + width) for base in range(0, count, width)]


def feed_kernel(info_ref, n_ref, ot_own, ot_other, *refs):
    sources, (b_own, b_other) = refs[:6], refs[6:8]
    hid_ref, slope_ref = refs[8:10]
    outs = refs[10:-6]
    win_ref, fc_ref, wo_ref, made_ref, sem, out_sem = refs[-6:]
    step = pl.program_id(0)
    places = weight_places(win_ref, fc_ref, wo_ref)

    @pl.when(step == 0)
    def _():
        start_weights(sources, places, sem)

    normed = n_ref[...]
    root = math.sqrt(2.0 / math.pi)
    bias = jnp.concatenate([b_own[...], b_other[...]], axis=1)
    wait_weights(step, sources, places, sem, range(6))
    cols = chunks_of(hid_ref.shape[1])
    made = None
    pre = nn(normed, win_ref[:, cols[0]])
    for number, cut in enumerate(cols):
        now = pre + bias[:, cut]
        if number + 1 < len(cols):
            pre = nn(normed, win_ref[:, cols[number + 1]])
        square = now * now
        half = 0.5 + 0.5 * jnp.tanh(now * (root + (0.044715 * root) * square))
        gelu = now * half
        slope = half + (gelu - gelu * half) * (2.0 * root + (0.26829 * root) * square)
        hid_ref[:, cut] = gelu.astype(BF16)
        slope_ref[:, cut] = slope.astype(BF16)
    hidden = hid_ref[...]
    att = jnp.concatenate([ot_own[...], ot_other[...]], axis=0).T.astype(BF16)
    for cut in chunks_of(fc_ref.shape[1]):
        made = nn(hidden, fc_ref[:, cut]) + nn(att, wo_ref[:, cut])
        made_ref[step, :, cut] = made.astype(BF16)
    send_pieces(info_ref, step, made_ref, outs, out_sem, False)

    @pl.when(step == pl.num_programs(0) - 1)
    def _():
        wait_all_pieces(info_ref, made_ref, outs, out_sem)


def paired(i, info):
    return jnp.bitwise_xor(i, info[0] // 2)


def feed(info, normed, ot, w_in, b_in, w_fc, w_out, group):
    seq, d = normed.shape
    rows = seq // group // 2
    tile = 4 * rows
    ph, units = ot[0].shape[0], 2 * w_in[0].shape[1]
    wide = 2 * ph
    unit_rows = pl.BlockSpec((tile, units), lambda i, info: (paired(i, info), 0))
    made = pl.pallas_call(
        feed_kernel,
        out_shape=(jax.ShapeDtypeStruct((seq, units), BF16),) * 2
        + (jax.ShapeDtypeStruct((rows, d), BF16),) * (2 * group),
        grid_spec=pltpu.PrefetchScalarGridSpec(
            num_scalar_prefetch=1,
            grid=(seq // tile,),
            in_specs=[
                pl.BlockSpec((tile, d), lambda i, info: (paired(i, info), 0)),
                pl.BlockSpec((ph, tile), lambda i, info: (0, paired(i, info))),
                pl.BlockSpec((ph, tile), lambda i, info: (0, paired(i, info))),
            ]
            + [pl.BlockSpec(memory_space=pl.ANY)] * 6
            + [resident(b_in[0].shape)] * 2,
            out_specs=(unit_rows,) * 2 + (pl.BlockSpec(memory_space=pl.ANY),) * (2 * group),
            scratch_shapes=[
                pltpu.VMEM((d, units), BF16),
                pltpu.VMEM((units, d), BF16),
                pltpu.VMEM((wide, d), BF16),
                pltpu.VMEM((seq // tile, tile, d), BF16),
                pltpu.SemaphoreType.DMA((6,)),
                pltpu.SemaphoreType.DMA((2 * group,)),
            ],
        ),
        compiler_params=params(44),
        cost_estimate=cost(2 * seq * d * (2 * units + wide), seq * (d * 4 + units * 4 + wide * 4) + d * units * 4, seq * units),
        name="feed",
    )(info, normed, *ot, *w_in, *w_fc, *w_out, *b_in)
    return made[0], made[1], made[2:]


def feed_back_kernel(slots, info_ref, *refs):
    count = len(slots)
    pieces, refs = refs[:count], refs[count:]
    n_any, hid_any, slope_ref, ot_own, ot_other = refs[:5]
    sources, refs = refs[5:11], refs[11:]
    gn_ref, gt_ref, gs_ref, delta_ref, keep_ref, away_ref, gwout_ref, gbin_ref = refs[:8]
    g_buf, n_buf, hid_buf, pre_buf, win_ref, fc_ref, wo_ref, acc_ref, g_sem, w_sem, sem = refs[8:]
    step = pl.program_id(0)
    last = pl.num_programs(0) - 1
    tile, units = slope_ref.shape
    ph = wo_ref.shape[0] // 2
    places = weight_places(win_ref, fc_ref, wo_ref)
    order = (2, 3, 0, 1, 4, 5)
    whole = (
        pltpu.make_async_copy(n_any, n_buf, sem.at[0]),
        pltpu.make_async_copy(hid_any, hid_buf, sem.at[1]),
    )

    @pl.when(step == 0)
    def _():
        start_weights([sources[k] for k in order[:2]], [places[k] for k in order[:2]], w_sem.at[pl.ds(2, 2)])
        start_pieces(info_ref, slots, pieces, tile // 2, g_buf, g_sem)
        for k in (0, 1, 4, 5):
            pltpu.make_async_copy(sources[k], places[k], w_sem.at[k]).start()
        for copy in whole:
            copy.start()

    wait_weights(step, sources, places, w_sem, (2, 3))
    wait_pieces(info_ref, step, tile, g_buf, g_sem)
    rows = pl.ds(pl.multiple_of(step * tile, tile), tile)
    grads = g_buf[rows, :]
    cols = chunks_of(units)
    sums = []
    for cut in cols:
        grad_pre = nt(grads, fc_ref[cut, :]) * slope_ref[:, cut].astype(F32)
        rounded = grad_pre.astype(BF16)
        pre_buf[rows, cut] = rounded
        sums.append(jnp.sum(rounded.astype(F32), axis=0, keepdims=True))
    part_b = jnp.concatenate(sums, axis=1)
    wait_weights(step, sources, places, w_sem, (0, 1, 4, 5))
    rounded = pre_buf[rows, :]
    for cut in chunks_of(gn_ref.shape[1]):
        gn_ref[:, cut] = nt(rounded, win_ref[cut, :]).astype(BF16)
    grad_att = nt(wo_ref[...], grads).astype(BF16)
    gt_ref[...] = grad_att
    ot = jnp.concatenate([ot_own[...], ot_other[...]], axis=0)
    share = grad_att.astype(F32) * ot
    for h in range(gs_ref.shape[0]):
        head = slice(h * HD, (h + 1) * HD)
        gs_ref[h] = grad_att[head].T
        delta_ref[h] = jnp.sum(share[head], axis=0, keepdims=True)
    part_out = nn(ot.astype(BF16), grads)

    @pl.when(step == 0)
    def _():
        gwout_ref[...] = part_out
        gbin_ref[...] = part_b

    @pl.when(step > 0)
    def _():
        gwout_ref[...] += part_out
        gbin_ref[...] += part_b

    @pl.when(step == last)
    def _():
        for copy in whole:
            copy.wait()
        dp_size = 2 * keep_ref.shape[0]
        each = units // 2 // dp_size
        for which, (a_buf, b_buf) in enumerate(((hid_buf, g_buf), (pre_buf, n_buf))):
            acc_ref[...] = tn(a_buf[...], b_buf[...])
            for slot in range(dp_size):
                out = (keep_ref, away_ref)[slot % 2]
                index = jnp.bitwise_xor(info_ref[1], slot)
                for shard in range(2):
                    base = pl.multiple_of(shard * (units // 2) + index * each, each)
                    out[slot // 2, shard, which * each : (which + 1) * each, :] = acc_ref[
                        pl.ds(base, each), :
                    ].astype(BF16)


def feed_back(info, blocks, normed, hidden, slope, ot, w_in, w_fc, w_out, dp_size):
    seq, d = normed.shape
    group = len(blocks)
    slots, pieces = listed(blocks)
    tile = 2 * seq // group
    ph, units = ot[0].shape[0], hidden.shape[1]
    wide = 2 * ph
    heads = wide // HD
    rows = pl.BlockSpec((tile, d), lambda i, info: (i, 0))
    unit_rows = pl.BlockSpec((tile, units), lambda i, info: (i, 0))
    turned = pl.BlockSpec((wide, tile), lambda i, info: (0, i))
    half_turned = pl.BlockSpec((ph, tile), lambda i, info: (0, i))
    packed = (dp_size // 2, 2, units // dp_size, d)
    anywhere = pl.BlockSpec(memory_space=pl.ANY)
    return pl.pallas_call(
        functools.partial(feed_back_kernel, slots),
        out_shape=(
            jax.ShapeDtypeStruct((seq, d), BF16),
            jax.ShapeDtypeStruct((wide, seq), BF16),
            jax.ShapeDtypeStruct((heads, seq, HD), BF16),
            jax.ShapeDtypeStruct((heads, 1, seq), F32),
            jax.ShapeDtypeStruct(packed, BF16),
            jax.ShapeDtypeStruct(packed, BF16),
            jax.ShapeDtypeStruct((wide, d), F32),
            jax.ShapeDtypeStruct((1, units), F32),
        ),
        grid_spec=pltpu.PrefetchScalarGridSpec(
            num_scalar_prefetch=1,
            grid=(seq // tile,),
            in_specs=[anywhere] * len(pieces)
            + [anywhere, anywhere, unit_rows, half_turned, half_turned]
            + [anywhere] * 6,
            out_specs=(
                rows,
                turned,
                pl.BlockSpec((heads, tile, HD), lambda i, info: (0, i, 0)),
                pl.BlockSpec((heads, 1, tile), lambda i, info: (0, 0, i)),
                resident(packed),
                resident(packed),
                resident((wide, d)),
                resident((1, units)),
            ),
            scratch_shapes=[
                pltpu.VMEM((seq, d), BF16),
                pltpu.VMEM((seq, d), BF16),
                pltpu.VMEM((seq, units), BF16),
                pltpu.VMEM((seq, units), BF16),
                pltpu.VMEM((d, units), BF16),
                pltpu.VMEM((units, d), BF16),
                pltpu.VMEM((wide, d), BF16),
                pltpu.VMEM((units, d), F32),
                pltpu.SemaphoreType.DMA((group // 2,)),
                pltpu.SemaphoreType.DMA((6,)),
                pltpu.SemaphoreType.DMA((2,)),
            ],
        ),
        compiler_params=params(56),
        cost_estimate=cost(2 * seq * d * (4 * units + 2 * wide), seq * (d * 6 + units * 4 + wide * 8) + d * units * 8),
        name="feed_back",
    )(info, *pieces, normed, hidden, slope, *ot, *w_in, *w_fc, *w_out)


def rows_back_kernel(count, info_ref, *refs):
    turned_refs, refs = refs[: 3 * count], refs[3 * count :]
    (n_ref, part_ref, wt_own, wt_other), refs = refs[:4], refs[4:]
    sum_ref, outs = refs[0], refs[1:-4]
    wt_ref, made_ref, sem, out_sem = refs[-4:]
    step = pl.program_id(0)
    ph = wt_own.shape[0]
    sources, places = (wt_own, wt_other), (wt_ref.at[:ph, :], wt_ref.at[ph:, :])

    @pl.when(step == 0)
    def _():
        start_weights(sources, places, sem)

    turned = jnp.concatenate([ref[...] for ref in turned_refs], axis=0)
    wait_weights(step, sources, places, sem, (0, 1))
    sums = []
    for cut in chunks_of(n_ref.shape[1]):
        made = part_ref[:, cut].astype(F32) + tn(turned, wt_ref[:, cut])
        made_ref[step, :, cut] = made.astype(BF16)
        sums.append(
            jnp.concatenate(
                [
                    jnp.sum(made * n_ref[:, cut].astype(F32), axis=0, keepdims=True),
                    jnp.sum(made, axis=0, keepdims=True),
                ],
                axis=0,
            )
        )
    sums = jnp.concatenate(sums, axis=1)
    send_pieces(info_ref, step, made_ref, outs, out_sem, False)

    @pl.when(step == pl.num_programs(0) - 1)
    def _():
        wait_all_pieces(info_ref, made_ref, outs, out_sem)

    @pl.when(step == 0)
    def _():
        sum_ref[...] = sums

    @pl.when(step > 0)
    def _():
        sum_ref[...] += sums


def rows_back(info, turned, normed, part, w_t, group):
    seq, d = normed.shape
    rows = seq // group // 2
    tile = 4 * rows
    depth = w_t[0].shape[0]
    tile_rows = pl.BlockSpec((tile, d), lambda i, info: (paired(i, info), 0))
    made = pl.pallas_call(
        functools.partial(rows_back_kernel, len(turned) // 3),
        out_shape=(jax.ShapeDtypeStruct((2, d), F32),)
        + (jax.ShapeDtypeStruct((rows, d), BF16),) * (2 * group),
        grid_spec=pltpu.PrefetchScalarGridSpec(
            num_scalar_prefetch=1,
            grid=(seq // tile,),
            in_specs=[
                pl.BlockSpec((part.shape[0], tile), lambda i, info: (0, paired(i, info)))
                for part in turned
            ]
            + [tile_rows, tile_rows]
            + [pl.BlockSpec(memory_space=pl.ANY)] * 2,
            out_specs=(resident((2, d)),) + (pl.BlockSpec(memory_space=pl.ANY),) * (2 * group),
            scratch_shapes=[
                pltpu.VMEM((2 * depth, d), BF16),
                pltpu.VMEM((seq // tile, tile, d), BF16),
                pltpu.SemaphoreType.DMA((2,)),
                pltpu.SemaphoreType.DMA((2 * group,)),
            ],
        ),
        compiler_params=params(36),
        cost_estimate=cost(2 * seq * d * 2 * depth, seq * (d * 6 + depth * 4) + d * depth * 4),
        name="rows_back",
    )(info, *turned, normed, part, *w_t)
    return made[0], made[1:]


def weights_back_kernel(info_ref, dq_ref, dk_ref, dv_ref, n_ref, gwout_ref, keep_ref, away_ref, acc_ref):
    step = pl.program_id(0)
    ph = gwout_ref.shape[0]
    turned = jnp.concatenate([dq_ref[...], dk_ref[...], dv_ref[...]], axis=0)
    part = nn(turned, n_ref[...])

    @pl.when(step == 0)
    def _():
        acc_ref[: 3 * ph, :] = part
        acc_ref[3 * ph :, :] = gwout_ref[...]

    @pl.when(step > 0)
    def _():
        acc_ref[: 3 * ph, :] += part

    @pl.when(step == pl.num_programs(0) - 1)
    def _():
        rows = keep_ref.shape[1]
        for slot in range(2 * keep_ref.shape[0]):
            out = (keep_ref, away_ref)[slot % 2]
            base = pl.multiple_of(jnp.bitwise_xor(info_ref[1], slot) * rows, rows)
            out[slot // 2] = acc_ref[pl.ds(base, rows), :].astype(BF16)


def weights_back(info, turned, normed, gw_out, shard, group, dp_size):
    seq, d = normed.shape
    tile = 2 * seq // group
    ph = turned[0].shape[0]
    packed = (dp_size // 2, 4 * ph // dp_size, d)
    return pl.pallas_call(
        weights_back_kernel,
        out_shape=(jax.ShapeDtypeStruct(packed, BF16),) * 2,
        grid_spec=pltpu.PrefetchScalarGridSpec(
            num_scalar_prefetch=1,
            grid=(seq // tile,),
            in_specs=[pl.BlockSpec((ph, tile), lambda i, info: (0, i))] * 3
            + [
                pl.BlockSpec((tile, d), lambda i, info: (i, 0)),
                pl.BlockSpec((ph, d), lambda i, info: (shard, 0)),
            ],
            out_specs=(resident(packed),) * 2,
            scratch_shapes=[pltpu.VMEM((4 * ph, d), F32)],
        ),
        compiler_params=params(20),
        cost_estimate=cost(2 * seq * d * 3 * ph, seq * (d * 2 + ph * 6) + d * ph * 16),
        name="weights_back",
    )(info, *turned, normed, gw_out)


def finish_feed_kernel(info_ref, *refs):
    pieces, (gin_ref, gfc_ref) = refs[:-2], refs[-2:]
    rows = gfc_ref.shape[0]
    for slot, piece in enumerate(pieces):

        @pl.when(pl.program_id(0) == slot)
        def _():
            gfc_ref[...] = piece[:rows, :].astype(F32)
            gin_ref[...] = piece[rows:, :].astype(F32).T


def finish_feed(info, pieces, units):
    count = len(pieces)
    d = pieces[0].shape[1]
    return pl.pallas_call(
        finish_feed_kernel,
        out_shape=(jax.ShapeDtypeStruct((d, units), F32), jax.ShapeDtypeStruct((units, d), F32)),
        grid_spec=pltpu.PrefetchScalarGridSpec(
            num_scalar_prefetch=1,
            grid=(count,),
            in_specs=[resident(pieces[0].shape)] * count,
            out_specs=(
                pl.BlockSpec((d, units // count), lambda i, info: (0, jnp.bitwise_xor(i, info[1]))),
                pl.BlockSpec((units // count, d), lambda i, info: (jnp.bitwise_xor(i, info[1]), 0)),
            ),
        ),
        compiler_params=params(16),
        cost_estimate=cost(0, d * units * 12),
        name="finish_feed",
    )(info, *pieces)


def finish_project_kernel(info_ref, *refs):
    pieces, (gqkv_ref, gout_ref) = refs[:-2], refs[-2:]
    index = pl.program_id(0)
    slot_now = jnp.bitwise_xor(index, info_ref[1])
    for slot, piece in enumerate(pieces):

        @pl.when((slot_now == slot) & (index < 3))
        def _():
            gqkv_ref[0] = piece[...].astype(F32).T

        @pl.when((slot_now == slot) & (index == 3))
        def _():
            gout_ref[...] = piece[...].astype(F32)


def finish_project(info, pieces):
    rows, d = pieces[0].shape
    return pl.pallas_call(
        finish_project_kernel,
        out_shape=(jax.ShapeDtypeStruct((3, d, rows), F32), jax.ShapeDtypeStruct((rows, d), F32)),
        grid_spec=pltpu.PrefetchScalarGridSpec(
            num_scalar_prefetch=1,
            grid=(4,),
            in_specs=[resident((rows, d))] * 4,
            out_specs=(
                pl.BlockSpec((1, d, rows), lambda i, info: (jnp.minimum(i, 2), 0, 0)),
                resident((rows, d)),
            ),
        ),
        compiler_params=params(16),
        cost_estimate=cost(0, d * rows * 24),
        name="finish_project",
    )(info, *pieces)


def mask_scores(scores, start, key_base, query_base, diagonal):
    key_places = key_base + lax.broadcasted_iota(jnp.int32, scores.shape, 0)
    keep = key_places >= start
    if diagonal:
        query_places = query_base + lax.broadcasted_iota(jnp.int32, scores.shape, 1)
        keep = keep & (key_places <= query_places)
    return jnp.where(keep, scores, NEG_LARGE)


def attend_kernel(low_ref, start_ref, qt_ref, k_ref, vt_ref, ot_ref, lse_ref, m_ref, l_ref, acc_ref):
    block = qt_ref.shape[1]
    i = pl.program_id(1)
    queries = qt_ref[...]
    start = start_ref[...]

    def step(j, diagonal):
        base = pl.multiple_of(j * block, block)
        scores = nn(k_ref[0, pl.ds(base, block), :], queries)
        scores = mask_scores(scores, start, base, i * block, diagonal)
        peak = jnp.max(scores, axis=0, keepdims=True)
        values = vt_ref[:, pl.ds(base, block)]
        if diagonal:
            weights = jnp.exp(scores - peak)
            m_ref[...] = peak
            l_ref[...] = jnp.sum(weights, axis=0, keepdims=True)
            acc_ref[...] = nn(values, weights.astype(BF16))
        else:
            before = m_ref[...]
            peak = jnp.maximum(before, peak)
            shrink = jnp.exp(before - peak)
            weights = jnp.exp(scores - peak)
            m_ref[...] = peak
            l_ref[...] = l_ref[...] * shrink + jnp.sum(weights, axis=0, keepdims=True)
            acc_ref[...] = acc_ref[...] * shrink + nn(values, weights.astype(BF16))

    step(i, True)

    def body(j, carry):
        step(j, False)
        return carry

    lax.fori_loop(low_ref[i], i, body, 0)
    total = l_ref[...]
    ot_ref[...] = acc_ref[...] * (1.0 / total)
    lse_ref[0] = m_ref[...] + jnp.log(total)


def attend(low, start, qt, k, vt, block, base, heads):
    seq = qt.shape[1]
    blocks = seq // block
    return pl.pallas_call(
        attend_kernel,
        out_shape=(
            jax.ShapeDtypeStruct((heads * HD, seq), F32),
            jax.ShapeDtypeStruct((heads, 1, seq), F32),
        ),
        grid_spec=pltpu.PrefetchScalarGridSpec(
            num_scalar_prefetch=1,
            grid=(heads, blocks),
            in_specs=[
                pl.BlockSpec((1, block), lambda h, i, low: (0, i)),
                pl.BlockSpec((HD, block), lambda h, i, low: (base + h, i)),
                pl.BlockSpec((1, seq, HD), lambda h, i, low: (base + h, 0, 0)),
                pl.BlockSpec((HD, seq), lambda h, i, low: (base + h, 0)),
            ],
            out_specs=(
                pl.BlockSpec((HD, block), lambda h, i, low: (h, i)),
                pl.BlockSpec((1, 1, block), lambda h, i, low: (h, 0, i)),
            ),
            scratch_shapes=[
                pltpu.VMEM((1, block), F32),
                pltpu.VMEM((1, block), F32),
                pltpu.VMEM((HD, block), F32),
            ],
        ),
        compiler_params=params(12),
        cost_estimate=cost(heads * seq * seq * 512, heads * seq * HD * 12, heads * seq * seq // 2),
        name="attend",
    )(low, start, qt, k, vt)


def attend_back_kernel(
    high_ref, start_ref, lse_ref, delta_ref, cos_ref, sin_ref, qt_ref, kt_ref, gt_ref, q_ref, k_ref, v_ref, g_ref,
    dqt_out, dkt_out, dvt_out, dqt_ref, dk_ref, dv_ref
):
    seq = qt_ref.shape[1]
    blocks = high_ref.shape[0]
    block = seq // blocks
    dqt_ref[...] = jnp.zeros_like(dqt_ref)

    def pair(i, j, diagonal):
        qs = pl.ds(pl.multiple_of(i * block, block), block)
        ks = pl.ds(pl.multiple_of(j * block, block), block)
        scores = nn(k_ref[0, ks, :], qt_ref[:, qs])
        scores = mask_scores(scores, start_ref[:, qs], j * block, i * block, diagonal)
        probs = jnp.exp(scores - lse_ref[0, :, qs])
        grad_probs = nn(v_ref[0, ks, :], gt_ref[:, qs])
        grad_scores = (probs * (grad_probs - delta_ref[0, :, qs])).astype(BF16)
        dv = nn(probs.astype(BF16), g_ref[0, qs, :])
        dk = nn(grad_scores, q_ref[0, qs, :])
        if diagonal:
            dv_ref[ks, :] = dv
            dk_ref[ks, :] = dk
        else:
            dv_ref[ks, :] += dv
            dk_ref[ks, :] += dk
        dqt_ref[:, qs] += nn(kt_ref[:, ks], grad_scores)

    def keys(j, carry):
        pair(j, j, True)

        def queries(i, inner):
            pair(i, j, False)
            return inner

        lax.fori_loop(j + 1, high_ref[j], queries, 0)
        return carry

    lax.fori_loop(0, blocks, keys, 0)
    cos, sin = cos_ref[...], sin_ref[...]
    half = ROT // 2

    def store(out, t):
        a, b = t[:half], t[half:ROT]
        out[:half] = (a * cos + b * sin).astype(BF16)
        out[half:ROT] = (b * cos - a * sin).astype(BF16)
        out[ROT:] = t[ROT:].astype(BF16)

    store(dqt_out, dqt_ref[...] * (HD**-0.5))
    store(dkt_out, dk_ref[...].T)
    dvt_out[...] = dv_ref[...].T.astype(BF16)


def attend_back(high, start, lse, delta, cos, sin, qt, kt, gt, q, k, v, g, base, local, heads, mib):
    seq = qt.shape[1]
    flat = pl.BlockSpec((HD, seq), lambda h, high: (local + h, 0))
    split = pl.BlockSpec((1, seq, HD), lambda h, high: (local + h, 0, 0))
    both_flat = pl.BlockSpec((HD, seq), lambda h, high: (base + h, 0))
    both_split = pl.BlockSpec((1, seq, HD), lambda h, high: (base + h, 0, 0))
    row = pl.BlockSpec((1, seq), lambda h, high: (0, 0))
    head_row = pl.BlockSpec((1, 1, seq), lambda h, high: (base + h, 0, 0))
    own_row = pl.BlockSpec((1, 1, seq), lambda h, high: (local + h, 0, 0))
    table = pl.BlockSpec((ROT // 2, seq), lambda h, high: (0, 0))
    return pl.pallas_call(
        attend_back_kernel,
        out_shape=(jax.ShapeDtypeStruct((heads * HD, seq), BF16),) * 3,
        grid_spec=pltpu.PrefetchScalarGridSpec(
            num_scalar_prefetch=1,
            grid=(heads,),
            in_specs=[row, own_row, head_row, table, table]
            + [flat, flat, both_flat]
            + [split, split, split, both_split],
            out_specs=(pl.BlockSpec((HD, seq), lambda h, high: (h, 0)),) * 3,
            scratch_shapes=[
                pltpu.VMEM((HD, seq), F32),
                pltpu.VMEM((seq, HD), F32),
                pltpu.VMEM((seq, HD), F32),
            ],
        ),
        compiler_params=params(mib),
        cost_estimate=cost(heads * seq * seq * 1280, heads * HD * seq * 24, heads * seq * seq // 2),
        name="attend_back",
    )(high, start, lse, delta, cos, sin, qt, kt, gt, q, k, v, g)


def run_starts(segments):
    places = lax.broadcasted_iota(jnp.int32, segments.shape, 1)
    leading = jnp.ones_like(segments[:, :1])
    changes = jnp.concatenate(
        [leading, (segments[:, 1:] != segments[:, :-1]).astype(jnp.int32)], axis=1
    )
    starts = lax.cummax(places * changes, axis=1)
    return places, starts


def build(dp_size, tensor_size):
    def per_device(
        inputs, segments, norm_gain, norm_bias, w_qkv, w_out, w_in, b_in, w_fc, b_out, cotangent
    ):
        row_count, seq = segments.shape
        tokens, d = inputs.shape
        group = tensor_size // row_count
        half_rot = ROT // 2
        block = 512
        me = lax.axis_index("tensor")
        dp = lax.axis_index("dp")
        row = me // group
        info = jnp.stack([me % group, dp]).astype(jnp.int32)
        other = [(i, (i + group) % tensor_size) for i in range(tensor_size)]
        bits = bit_list(group)
        dp_bits = bit_list(dp_size)
        def normalize(rows):
            rows = rows.astype(F32)
            centred = rows - jnp.mean(rows, axis=-1, keepdims=True)
            inv_std = lax.rsqrt(jnp.mean(centred * centred, axis=-1, keepdims=True) + EPSILON)
            return centred * inv_std, inv_std

        def slice_of(indexed):
            return lax.dynamic_index_in_dim(indexed, dp, 0, keepdims=False)

        def fetch(part):
            return lax.ppermute(part, "tensor", other)

        def share(got):
            return gather_slots(got, "dp", dp_size, dp_bits[::-1])

        def rows_of(pieces, start, stop):
            return natural({k: pieces[k][start:stop] for k in pieces}, dp)

        units, per_head = w_in.shape[1], w_qkv.shape[2]
        shard_heads = per_head // HD
        fc_rows = units // dp_size
        qkv_slice = slice_of(w_qkv.reshape(dp_size, -1, per_head))
        qkv_slice, rows_in = tie(qkv_slice, inputs)
        qkv_got = fetch(qkv_slice)
        normed_own = [
            (normalize(half)[0] * norm_gain + norm_bias).astype(BF16) for half in halves_of(rows_in)
        ]
        n_got = gather_lead(normed_own, tensor_size, bits)
        in_slice = slice_of(w_in.reshape(dp_size, -1, units))
        fc_slice = jnp.concatenate(
            [slice_of(w_fc.reshape(dp_size, -1, d)), slice_of(w_out.reshape(dp_size, -1, d))], axis=0
        )
        wt_own = jnp.concatenate([w_qkv[c].T for c in range(3)], axis=0)

        segs = lax.dynamic_slice_in_dim(segments, row, 1, axis=0)
        places, starts = run_starts(segs)
        first_key = jnp.where(segs >= 0, starts, places)
        offsets = (places - starts).astype(F32)
        frequency = jnp.exp(
            lax.broadcasted_iota(F32, (half_rot,), 0) * (-2.0 * math.log(10000.0) / ROT)
        )
        angles = frequency[:, None] * offsets
        cos_t, sin_t = jnp.cos(angles), jnp.sin(angles)
        blocks = seq // block
        low = (jnp.min(first_key.reshape(blocks, block), axis=1) // block).astype(jnp.int32)
        reach = low[None, :] <= jnp.arange(blocks)[:, None]
        high = jnp.max(
            jnp.where(reach, jnp.arange(1, blocks + 1, dtype=jnp.int32)[None, :], 0), axis=1
        ).astype(jnp.int32)

        cotangent_sum = jnp.sum(cotangent.astype(F32), axis=0, keepdims=True)
        prepared = (wt_own, cos_t, sin_t, first_key, low, high, cotangent_sum)
        n_got, normed_own, qkv_got, (in_slice, fc_slice), prepared = tie(
            n_got, normed_own, qkv_got, (in_slice, fc_slice), prepared
        )
        n_got = {**n_got, **gather_own(normed_own, tensor_size, bits)}
        wt_own, cos_t, sin_t, first_key, low, high, cotangent_sum = prepared
        n_blocks = gather_rest(normed_own, n_got, tensor_size, bits)
        qkv_pieces = gather_slots(qkv_got, "dp", dp_size, dp_bits[::-1][:1])
        n_blocks, qkv_pieces, in_slice, fc_slice = tie(n_blocks, qkv_pieces, in_slice, fc_slice)
        qkv_pieces = gather_more(qkv_pieces, "dp", dp_size, dp_bits[::-1][1:])
        in_got, fc_got, b_in_other = (fetch(part) for part in (in_slice, fc_slice, b_in))

        def heads_forward(made, base, count):
            return attend(low, first_key, made[0], made[4], made[2], block, base, count)

        cut = shard_heads // 2
        made = project(info, n_blocks, wt_own, cos_t, sin_t)
        normed, own = made[0], made[1:]
        attended = []
        cot = halves_of(cotangent)
        if cut:
            attended.append(heads_forward(own, 0, cut))
            (attended[0], in_got), own, cot, qkv_pieces = tie((attended[0], in_got), own, cot, qkv_pieces)
        g_got = gather_lead(cot, tensor_size, bits)
        in_pieces = gather_slots(in_got, "dp", dp_size, dp_bits[::-1][:1])
        qkv_other = rows_of(qkv_pieces, 0, None).reshape(w_qkv.shape)
        wt_other = jnp.concatenate([qkv_other[c].T for c in range(3)], axis=0)
        rest = project(None, normed, wt_other, cos_t, sin_t)
        attended.append(heads_forward(own, cut, shard_heads - cut))
        attended[-1], in_pieces, fc_got, rest = tie(attended[-1], in_pieces, fc_got, rest)
        in_pieces = gather_more(in_pieces, "dp", dp_size, dp_bits[::-1][1:])
        fc_pieces = gather_slots(fc_got, "dp", dp_size, dp_bits[::-1][:1])
        attended_rest = []
        if cut:
            attended_rest.append(heads_forward(rest, 0, cut))
            attended_rest[0], in_pieces, fc_pieces, g_got, cot, rest = tie(
                attended_rest[0], in_pieces, fc_pieces, g_got, cot, rest
            )
        g_got = {**g_got, **gather_own(cot, tensor_size, bits)}
        fc_pieces = gather_more(fc_pieces, "dp", dp_size, dp_bits[::-1][1:])
        w_in_other = rows_of(in_pieces, 0, None)
        g_blocks = gather_rest(cot, g_got, tensor_size, bits)
        attended_rest.append(heads_forward(rest, cut, shard_heads - cut))
        attended_rest[-1], fc_pieces, w_in_other = tie(attended_rest[-1], fc_pieces, w_in_other)
        (ot_own, lse_own), (ot_other, lse_other) = (
            tuple(jnp.concatenate([part[n] for part in parts], axis=0) for n in range(2))
            for parts in (attended, attended_rest)
        )
        w_fc_other = rows_of(fc_pieces, 0, fc_rows)
        w_out_other = rows_of(fc_pieces, fc_rows, None)
        ot = (ot_own, ot_other)
        w_in_both, w_fc_both, w_out_both = (w_in, w_in_other), (w_fc, w_fc_other), (w_out, w_out_other)
        hidden, slope, out_pieces = feed(
            info, normed, ot, w_in_both, (b_in[None], b_in_other[None]), w_fc_both, w_out_both, group
        )

        def by_slot(pieces):
            return {(k, half): pieces[2 * k + half] for k in range(group) for half in range(2)}

        last_stage = len(bits) - 1
        out_parts = by_slot(out_pieces)
        out_got = reduce_sends(out_parts, tensor_size, bits, last_stage)
        out_early = reduce_early(out_parts, tensor_size, bits)
        made = feed_back(
            info, g_blocks, normed, hidden, slope, ot, w_in_both, w_fc_both, w_out_both, dp_size
        )
        made, out_got, out_early = tie(made, out_got, out_early)
        gn_part, gt, g_heads, delta, keep1, away1, gw_out, gb_in = made
        out_parts = reduce_adds(out_parts, out_got)
        for stage in range(last_stage - 1, 0, -1):
            out_parts = reduce_adds(out_parts, reduce_sends(out_parts, tensor_size, bits, stage))

        def settle_dp(parts, bit):
            got = {
                k ^ bit: [swap(part, "dp", dp_size, bit) for part in parts[k]]
                for k in sorted(parts)
                if k & bit
            }
            return {k: parts[k] for k in got}, got

        def settle_add(kept, got):
            return {k: tuple(add(a, b) for a, b in zip(kept[k], got[k])) for k in kept}

        def settle_rest(parts, got):
            for bit in dp_bits[2:]:
                parts, got = settle_dp(settle_add(parts, got), bit)
            return settle_add(parts, got)[0]

        share_bits = dp_bits[::-1]

        def heads_back(shard):
            qt, kt, vt, q, k, v = (own, rest)[shard]
            return attend_back(
                high, first_key, (lse_own, lse_other)[shard], delta, cos_t, sin_t, qt, kt, gt, q, k, v, g_heads,
                shard * shard_heads, 0, shard_heads, (20, 56)[shard]
            )

        got1 = swap(away1, "dp", dp_size, dp_bits[0])
        got1, out_parts, gt = tie(got1, out_parts, gt)
        sums1 = {
            2 * j: tuple(add(keep1[j, s], got1[j, s]) for s in range(2)) for j in range(dp_size // 2)
        }
        sums1, out_parts, gt = tie(sums1, out_parts, gt)
        out_got = reduce_late(out_parts, out_early, tensor_size, bits)
        kept1, got1 = settle_dp(sums1, dp_bits[1])
        turned_other = heads_back(1)
        keep2, away2 = weights_back(info, turned_other, normed, gw_out, 1, group, dp_size)
        keep2, away2, got1, gt = tie(keep2, away2, got1, gt)
        got2 = swap(away2, "dp", dp_size, dp_bits[0])
        own1, other1 = settle_rest(kept1, got1)
        own1, other1, got2, gt = tie(own1, other1, got2, gt)
        sums2 = {2 * j: (add(keep2[j], got2[j]),) for j in range(dp_size // 2)}
        sums2, other1, gt = tie(sums2, other1, gt)
        kept2, got2 = settle_dp(sums2, dp_bits[1])
        other1 = fetch(other1)
        turned_own = heads_back(0)
        turned_own, got2, other1, out_got = tie(turned_own, got2, other1, out_got)
        (other2,) = settle_rest(kept2, got2)
        total1 = add(own1, other1)
        turned_own, total1, other2 = tie(turned_own, total1, other2)
        other2_got = fetch(other2)
        pieces1 = gather_slots(total1, "dp", dp_size, share_bits[:1])
        sums, gn_pieces = rows_back(
            info, [*turned_own, *turned_other], normed, gn_part, (wt_own, wt_other), group
        )
        gn_parts = by_slot(gn_pieces)
        gn_got = reduce_sends(gn_parts, tensor_size, bits, last_stage)

        bias_parts = jnp.zeros((tensor_size, units), F32)
        bias_parts = lax.dynamic_update_slice_in_dim(bias_parts, gb_in[:, :units], me, axis=0)
        bias_parts = lax.dynamic_update_slice_in_dim(
            bias_parts, gb_in[:, units:], (me + group) % tensor_size, axis=0
        )
        cotangent_f = cotangent.astype(F32)
        total = jnp.concatenate(
            [sums, cotangent_sum, bias_parts.reshape(-1, d)], axis=0
        )
        total, turned_own = tie(total, turned_own)
        total_got = swap(total, "dp", dp_size, dp_bits[0])
        keep3, away3 = weights_back(info, turned_own, normed, gw_out, 0, group, dp_size)
        keep3, away3, pieces1, total_got = tie(keep3, away3, pieces1, total_got)
        gn_early = reduce_early(gn_parts, tensor_size, bits)
        got3 = swap(away3, "dp", dp_size, dp_bits[0])
        pieces1 = gather_more(pieces1, "dp", dp_size, share_bits[1:])
        total = total + total_got
        for bit in dp_bits[1:]:
            total = total + swap(total, "dp", dp_size, bit)
        got3, pieces1, total, gn_got, other2_got = tie(got3, pieces1, total, gn_got, other2_got)
        gn_parts = reduce_adds(gn_parts, gn_got)
        for number in range(last_stage - 1, 0, -1):
            gn_parts = reduce_adds(gn_parts, reduce_sends(gn_parts, tensor_size, bits, number))
        sums3 = {2 * j: (add(keep3[j], got3[j]),) for j in range(dp_size // 2)}
        gn_parts, sums3, pieces1, total = tie(gn_parts, sums3, pieces1, total)
        gn_got = reduce_late(gn_parts, gn_early, tensor_size, bits)
        kept3, got3 = settle_dp(sums3, dp_bits[1])
        total_got = [swap(total, "tensor", tensor_size, k) for k in range(2, tensor_size, 2)]
        pieces1 = [pieces1[k] for k in range(dp_size)]
        if fc_rows % LANES == 0:
            grad_in, grad_fc = finish_feed(info, pieces1, units)
        else:
            pieces1 = dict(enumerate(pieces1))
            grad_fc = rows_of(pieces1, 0, fc_rows).astype(F32)
            grad_in = rows_of(pieces1, fc_rows, None).T.astype(F32)
        kept3, got3, grad_in, grad_fc, out_parts = tie(kept3, got3, grad_in, grad_fc, out_parts)
        (own3,) = settle_rest(kept3, got3)
        total2 = add(own3, other2_got)
        pieces2 = gather_slots(total2, "dp", dp_size, share_bits)
        output = (inputs.astype(F32) + reduce_total(out_parts, {**out_early, **out_got}) + b_out).astype(BF16)
        pieces2 = [pieces2[k] for k in range(dp_size)]
        if dp_size == 4 and per_head % LANES == 0:
            grad_qkv, grad_out = finish_project(info, pieces2)
        else:
            stacked = natural(dict(enumerate(pieces2)), dp)
            grad_qkv = jnp.swapaxes(
                stacked[: 3 * per_head].reshape(3, per_head, d), 1, 2
            ).astype(F32)
            grad_out = stacked[3 * per_head :].astype(F32)
        gn_got, gn_parts, total_got, grad_qkv, grad_out, output = tie(
            {**gn_early, **gn_got}, gn_parts, total_got, grad_qkv, grad_out, output
        )
        for part in total_got:
            total = total + part
        total = total + swap(total, "tensor", tensor_size, 1)

        unit_rows, inv_std = normalize(inputs)
        grad_norm_own = reduce_total(gn_parts, gn_got)
        scaled = grad_norm_own * norm_gain
        grad_local = inv_std * (
            scaled
            - jnp.mean(scaled, axis=-1, keepdims=True)
            - unit_rows * jnp.mean(scaled * unit_rows, axis=-1, keepdims=True)
        )
        grad_inputs = cotangent_f + grad_local

        grad_bias = total[1]
        grad_gain = (total[0] - norm_bias * grad_bias) / norm_gain
        grad_b_out = total[2]
        grad_b_in = lax.dynamic_slice_in_dim(total[3:].reshape(tensor_size, units), me, 1, axis=0)[0]
        return (
            output,
            grad_inputs,
            grad_gain,
            grad_bias,
            grad_qkv,
            grad_out,
            grad_in,
            grad_b_in,
            grad_fc,
            grad_b_out,
        )

    return per_device


def solution(mesh):
    tokens = P(("dp", "tensor"), None)
    return jax.shard_map(
        build(mesh.shape["dp"], mesh.shape["tensor"]),
        mesh=mesh,
        in_specs=(
            tokens,
            P("dp", None),
            P(),
            P(),
            P(None, None, "tensor"),
            P("tensor", None),
            P(None, "tensor"),
            P("tensor"),
            P("tensor", None),
            P(),
            tokens,
        ),
        out_specs=(
            tokens,
            tokens,
            P(),
            P(),
            P(None, None, "tensor"),
            P("tensor", None),
            P(None, "tensor"),
            P("tensor"),
            P("tensor", None),
            P(),
        ),
        check_vma=False,
    )
```

```python
import functools
import math

import jax
import jax.numpy as jnp
from jax import lax
from jax.experimental import pallas as pl
from jax.experimental.pallas import tpu as pltpu
from jax.sharding import PartitionSpec as P

HD = 64
ROT = 32
EPSILON = 1e-05
NEG_LARGE = -1e30
BF16 = jnp.bfloat16
F32 = jnp.float32
LANES = 128
MIB = 1024 * 1024


def nn(a, b):
    return lax.dot_general(a, b, (((1,), (0,)), ((), ())), preferred_element_type=F32)


def nt(a, b):
    return lax.dot_general(a, b, (((1,), (1,)), ((), ())), preferred_element_type=F32)


def tn(a, b):
    return lax.dot_general(a, b, (((0,), (0,)), ((), ())), preferred_element_type=F32)


def resident(shape):
    return pl.BlockSpec(shape, lambda *_: (0,) * len(shape), pipeline_mode=pl.Buffered(1))


def params(mib):
    return pltpu.CompilerParams(vmem_limit_bytes=mib * MIB)


def cost(flops, moved, trans=0):
    return pl.CostEstimate(flops=int(flops), bytes_accessed=int(moved), transcendentals=int(trans))


def bit_list(count):
    return [1 << n for n in range(count.bit_length() - 1)]


def swap(array, axis, size, bit):
    return lax.ppermute(array, axis, [(i, i ^ bit) for i in range(size)])


def tie(*groups):
    return lax.optimization_barrier(groups)


def halves_of(block):
    rows = block.shape[0] // 2
    return block[:rows], block[rows:]


def forwards(bits):
    steps = []
    for number in range(1, len(bits)):
        for half, order in enumerate((bits, bits[::-1])):
            for k in range(1, 2 ** len(bits)):
                if not any(k & bit for bit in order[number:]):
                    steps.append((number, half, k, k ^ order[number], order[number]))
    return steps


def gather_lead(halves, size, bits):
    orders = (bits, bits[::-1])
    return {(order[0], half): swap(halves[half], "tensor", size, order[0]) for half, order in enumerate(orders)}


def gather_own(halves, size, bits):
    orders = (bits, bits[::-1])
    return {
        (bit, half): swap(halves[half], "tensor", size, bit)
        for half, order in enumerate(orders)
        for bit in order[1:]
    }


def gather_rest(halves, got, size, bits):
    parts = {**got, (0, 0): halves[0], (0, 1): halves[1]}
    for _, half, k, made, bit in forwards(bits):
        parts[made, half] = swap(parts[k, half], "tensor", size, bit)
    return {k: (parts[k, 0], parts[k, 1]) for k in range(2 ** len(bits))}


def add(a, b):
    return (a.astype(F32) + b.astype(F32)).astype(a.dtype)


def reduce_sends(pieces, size, bits, stage):
    return {
        (k, half): swap(pieces[made, half], "tensor", size, bit)
        for number, half, k, made, bit in reversed(forwards(bits))
        if number == stage
    }


def reduce_adds(pieces, got):
    return {key: add(pieces[key], got[key]) if key in got else pieces[key] for key in pieces}


def reduce_early(pieces, size, bits):
    waiting = {(k, half) for _, half, k, _, _ in forwards(bits)}
    return {
        (bit, half): swap(pieces[bit, half], "tensor", size, bit)
        for bit in bits
        for half in range(2)
        if (bit, half) not in waiting
    }


def reduce_late(pieces, early, size, bits):
    return {
        (bit, half): swap(pieces[bit, half], "tensor", size, bit)
        for bit in bits
        for half in range(2)
        if (bit, half) not in early
    }


def reduce_total(pieces, got):
    halves = []
    for half in range(2):
        total = pieces[0, half].astype(F32)
        for k, which in sorted(got):
            if which == half:
                total = total + got[k, half].astype(F32)
        halves.append(total)
    return jnp.concatenate(halves, axis=0)


def gather_slots(mine, axis, size, bits):
    return gather_more({0: mine}, axis, size, bits)


def gather_more(pieces, axis, size, bits):
    pieces = dict(pieces)
    for bit in bits:
        for k in sorted(pieces):
            pieces[k ^ bit] = swap(pieces[k], axis, size, bit)
    return pieces


def natural(pieces, me):
    for bit in bit_list(len(pieces)):
        odd = (me & bit) != 0
        pieces = {k: jnp.where(odd, pieces[k ^ bit], pieces[k]) for k in pieces}
    return jnp.concatenate([pieces[k] for k in range(len(pieces))], axis=0)


def turn_rows(t, cos, sin):
    half = ROT // 2
    a, b = t[:half], t[half:ROT]
    return jnp.concatenate([a * cos - b * sin, b * cos + a * sin, t[ROT:]], axis=0)


def start_pieces(info_ref, slots, refs, tokens, buf_ref, sem):
    for (k, place), piece in zip(slots, refs):
        rows = piece.shape[0]
        base = pl.multiple_of(jnp.bitwise_xor(info_ref[0], k) * tokens + place * rows, rows)
        pltpu.make_async_copy(piece, buf_ref.at[pl.ds(base, rows), :], sem.at[k // 2]).start()


def listed(blocks):
    order = [(k, place) for k in sorted(blocks) for place in range(len(blocks[k]))]
    return order, [blocks[k][place] for k, place in order]


def wait_pieces(info_ref, step, tile, buf_ref, sem):
    which = jnp.bitwise_xor(step, info_ref[0] // 2)
    view = buf_ref.at[pl.ds(0, tile), :]
    pltpu.make_async_copy(view, view, sem.at[which]).wait()


def project_kernel(slots, info_ref, *refs):
    count = len(slots)
    pieces = refs[:count]
    wt_ref, cos_ref, sin_ref = refs[count : count + 3]
    n_ref, qt_ref, kt_ref, vt_ref, q_ref, k_ref, v_ref = refs[count + 3 : count + 10]
    step = pl.program_id(0)
    tile = n_ref.shape[0]
    wide = qt_ref.shape[0]
    buf_ref, sem = refs[count + 10 :]

    @pl.when(step == 0)
    def _():
        start_pieces(info_ref, slots, pieces, tile // 2, buf_ref, sem)

    wait_pieces(info_ref, step, tile, buf_ref, sem)
    normed = buf_ref[pl.ds(pl.multiple_of(step * tile, tile), tile), :]
    n_ref[...] = normed
    store_heads(wt_ref, normed, cos_ref, sin_ref, qt_ref, kt_ref, vt_ref, q_ref, k_ref, v_ref)


def project_more_kernel(n_ref, wt_ref, cos_ref, sin_ref, *outs):
    store_heads(wt_ref, n_ref[...], cos_ref, sin_ref, *outs)


def store_heads(wt_ref, normed, cos_ref, sin_ref, qt_ref, kt_ref, vt_ref, q_ref, k_ref, v_ref):
    wide = qt_ref.shape[0]
    made = nt(wt_ref[...], normed)
    cos, sin = cos_ref[...], sin_ref[...]
    scale = HD**-0.5
    for h in range(wide // HD):
        for which, t_ref, h_ref in ((0, qt_ref, q_ref), (1, kt_ref, k_ref), (2, vt_ref, v_ref)):
            base = which * wide + h * HD
            t = made[base : base + HD]
            if which < 2:
                t = turn_rows(t, cos, sin)
            t = t.astype(BF16)
            if which == 0:
                t = (t.astype(F32) * scale).astype(BF16)
            t_ref[h * HD : (h + 1) * HD, :] = t
            h_ref[h] = t.T


def project(info, blocks, weights, cos, sin):
    gathered = isinstance(blocks, dict)
    slots, pieces = listed(blocks) if gathered else ([], [blocks])
    if gathered:
        group = len(blocks)
        tokens, d = sum(part.shape[0] for part in blocks[0]), blocks[0][0].shape[1]
        seq = group * tokens
        tile = 2 * tokens
    else:
        seq, d = blocks.shape
        tile = seq // 2
    wide = weights.shape[0] // 3
    heads = wide // HD
    flat = jax.ShapeDtypeStruct((wide, seq), BF16)
    split = jax.ShapeDtypeStruct((heads, seq, HD), BF16)
    flat_spec = pl.BlockSpec((wide, tile), lambda i, *_: (0, i))
    split_spec = pl.BlockSpec((heads, tile, HD), lambda i, *_: (0, i, 0))
    table = pl.BlockSpec((ROT // 2, tile), lambda i, *_: (0, i))
    rows = pl.BlockSpec((tile, d), lambda i, *_: (i, 0))
    row_out = ((jax.ShapeDtypeStruct((seq, d), BF16), rows),) if gathered else ()
    return pl.pallas_call(
        functools.partial(project_kernel, slots) if gathered else project_more_kernel,
        out_shape=tuple(shape for shape, _ in row_out) + (flat,) * 3 + (split,) * 3,
        grid_spec=pltpu.PrefetchScalarGridSpec(
            num_scalar_prefetch=1 if gathered else 0,
            grid=(seq // tile,),
            in_specs=([pl.BlockSpec(memory_space=pl.ANY)] * len(pieces) if gathered else [rows])
            + [resident(weights.shape), table, table],
            out_specs=tuple(spec for _, spec in row_out) + (flat_spec,) * 3 + (split_spec,) * 3,
            scratch_shapes=[
                pltpu.VMEM((seq, d), BF16),
                pltpu.SemaphoreType.DMA((seq // tile,)),
            ]
            if gathered
            else [],
        ),
        compiler_params=params(26),
        cost_estimate=cost(2 * seq * d * 3 * wide, seq * d * 4 + d * wide * 6 + 9 * wide * seq * 2),
        name="project",
    )(*((info,) if gathered else ()), *pieces, weights, cos, sin)


def send_pieces(info_ref, step, made_ref, outs, sem, wait):
    rows = outs[0].shape[0]
    odd = info_ref[0] % 2
    for pair in range(len(outs) // 4):

        @pl.when(step == pair)
        def _():
            for u in range(2):
                for half in range(2):
                    base = pl.multiple_of((2 * jnp.bitwise_xor(u, odd) + half) * rows, rows)
                    number = 4 * pair + 2 * u + half
                    copy = pltpu.make_async_copy(
                        made_ref.at[pair, pl.ds(base, rows), :], outs[number], sem.at[number]
                    )
                    if wait:
                        copy.wait()
                    else:
                        copy.start()


def wait_all_pieces(info_ref, made_ref, outs, sem):
    for pair in range(len(outs) // 4):
        send_pieces(info_ref, pair, made_ref, outs, sem, True)


def start_weights(sources, places, sem):
    for number, (source, place) in enumerate(zip(sources, places)):
        pltpu.make_async_copy(source, place, sem.at[number]).start()


def wait_weights(step, sources, places, sem, numbers):
    @pl.when(step == 0)
    def _():
        for number in numbers:
            pltpu.make_async_copy(sources[number], places[number], sem.at[number]).wait()


def weight_places(win_ref, fc_ref, wo_ref):
    units, ph = win_ref.shape[1] // 2, wo_ref.shape[0] // 2
    return [
        win_ref.at[:, :units],
        win_ref.at[:, units:],
        fc_ref.at[:units, :],
        fc_ref.at[units:, :],
        wo_ref.at[:ph, :],
        wo_ref.at[ph:, :],
    ]


def chunks_of(count):
    width = min(256, count)
    return [slice(base, base + width) for base in range(0, count, width)]


def feed_kernel(info_ref, n_ref, ot_own, ot_other, *refs):
    sources, (b_own, b_other) = refs[:6], refs[6:8]
    hid_ref, slope_ref = refs[8:10]
    outs = refs[10:-6]
    win_ref, fc_ref, wo_ref, made_ref, sem, out_sem = refs[-6:]
    step = pl.program_id(0)
    places = weight_places(win_ref, fc_ref, wo_ref)

    @pl.when(step == 0)
    def _():
        start_weights(sources, places, sem)

    normed = n_ref[...]
    root = math.sqrt(2.0 / math.pi)
    bias = jnp.concatenate([b_own[...], b_other[...]], axis=1)
    wait_weights(step, sources, places, sem, range(6))
    cols = chunks_of(hid_ref.shape[1])
    made = None
    pre = nn(normed, win_ref[:, cols[0]])
    for number, cut in enumerate(cols):
        now = pre + bias[:, cut]
        if number + 1 < len(cols):
            pre = nn(normed, win_ref[:, cols[number + 1]])
        square = now * now
        half = 0.5 + 0.5 * jnp.tanh(now * (root + (0.044715 * root) * square))
        gelu = now * half
        slope = half + (gelu - gelu * half) * (2.0 * root + (0.26829 * root) * square)
        hid_ref[:, cut] = gelu.astype(BF16)
        slope_ref[:, cut] = slope.astype(BF16)
    hidden = hid_ref[...]
    att = jnp.concatenate([ot_own[...], ot_other[...]], axis=0).T.astype(BF16)
    for cut in chunks_of(fc_ref.shape[1]):
        made = nn(hidden, fc_ref[:, cut]) + nn(att, wo_ref[:, cut])
        made_ref[step, :, cut] = made.astype(BF16)
    send_pieces(info_ref, step, made_ref, outs, out_sem, False)

    @pl.when(step == pl.num_programs(0) - 1)
    def _():
        wait_all_pieces(info_ref, made_ref, outs, out_sem)


def paired(i, info):
    return jnp.bitwise_xor(i, info[0] // 2)


def feed(info, normed, ot, w_in, b_in, w_fc, w_out, group):
    seq, d = normed.shape
    rows = seq // group // 2
    tile = 4 * rows
    ph, units = ot[0].shape[0], 2 * w_in[0].shape[1]
    wide = 2 * ph
    unit_rows = pl.BlockSpec((tile, units), lambda i, info: (paired(i, info), 0))
    made = pl.pallas_call(
        feed_kernel,
        out_shape=(jax.ShapeDtypeStruct((seq, units), BF16),) * 2
        + (jax.ShapeDtypeStruct((rows, d), BF16),) * (2 * group),
        grid_spec=pltpu.PrefetchScalarGridSpec(
            num_scalar_prefetch=1,
            grid=(seq // tile,),
            in_specs=[
                pl.BlockSpec((tile, d), lambda i, info: (paired(i, info), 0)),
                pl.BlockSpec((ph, tile), lambda i, info: (0, paired(i, info))),
                pl.BlockSpec((ph, tile), lambda i, info: (0, paired(i, info))),
            ]
            + [pl.BlockSpec(memory_space=pl.ANY)] * 6
            + [resident(b_in[0].shape)] * 2,
            out_specs=(unit_rows,) * 2 + (pl.BlockSpec(memory_space=pl.ANY),) * (2 * group),
            scratch_shapes=[
                pltpu.VMEM((d, units), BF16),
                pltpu.VMEM((units, d), BF16),
                pltpu.VMEM((wide, d), BF16),
                pltpu.VMEM((seq // tile, tile, d), BF16),
                pltpu.SemaphoreType.DMA((6,)),
                pltpu.SemaphoreType.DMA((2 * group,)),
            ],
        ),
        compiler_params=params(44),
        cost_estimate=cost(2 * seq * d * (2 * units + wide), seq * (d * 4 + units * 4 + wide * 4) + d * units * 4, seq * units),
        name="feed",
    )(info, normed, *ot, *w_in, *w_fc, *w_out, *b_in)
    return made[0], made[1], made[2:]


def feed_back_kernel(slots, info_ref, *refs):
    count = len(slots)
    pieces, refs = refs[:count], refs[count:]
    n_any, hid_any, slope_ref, ot_own, ot_other = refs[:5]
    sources, refs = refs[5:11], refs[11:]
    gn_ref, gt_ref, gs_ref, delta_ref, keep_ref, away_ref, gwout_ref, gbin_ref = refs[:8]
    g_buf, n_buf, hid_buf, pre_buf, win_ref, fc_ref, wo_ref, acc_ref, g_sem, w_sem, sem = refs[8:]
    step = pl.program_id(0)
    last = pl.num_programs(0) - 1
    tile, units = slope_ref.shape
    ph = wo_ref.shape[0] // 2
    places = weight_places(win_ref, fc_ref, wo_ref)
    order = (2, 3, 0, 1, 4, 5)
    whole = (
        pltpu.make_async_copy(n_any, n_buf, sem.at[0]),
        pltpu.make_async_copy(hid_any, hid_buf, sem.at[1]),
    )

    @pl.when(step == 0)
    def _():
        start_weights([sources[k] for k in order[:2]], [places[k] for k in order[:2]], w_sem.at[pl.ds(2, 2)])
        start_pieces(info_ref, slots, pieces, tile // 2, g_buf, g_sem)
        for k in (0, 1, 4, 5):
            pltpu.make_async_copy(sources[k], places[k], w_sem.at[k]).start()
        for copy in whole:
            copy.start()

    wait_weights(step, sources, places, w_sem, (2, 3))
    wait_pieces(info_ref, step, tile, g_buf, g_sem)
    rows = pl.ds(pl.multiple_of(step * tile, tile), tile)
    grads = g_buf[rows, :]
    cols = chunks_of(units)
    sums = []
    for cut in cols:
        grad_pre = nt(grads, fc_ref[cut, :]) * slope_ref[:, cut].astype(F32)
        rounded = grad_pre.astype(BF16)
        pre_buf[rows, cut] = rounded
        sums.append(jnp.sum(rounded.astype(F32), axis=0, keepdims=True))
    part_b = jnp.concatenate(sums, axis=1)
    wait_weights(step, sources, places, w_sem, (0, 1, 4, 5))
    rounded = pre_buf[rows, :]
    for cut in chunks_of(gn_ref.shape[1]):
        gn_ref[:, cut] = nt(rounded, win_ref[cut, :]).astype(BF16)
    grad_att = nt(wo_ref[...], grads).astype(BF16)
    gt_ref[...] = grad_att
    ot = jnp.concatenate([ot_own[...], ot_other[...]], axis=0)
    share = grad_att.astype(F32) * ot
    for h in range(gs_ref.shape[0]):
        head = slice(h * HD, (h + 1) * HD)
        gs_ref[h] = grad_att[head].T
        delta_ref[h] = jnp.sum(share[head], axis=0, keepdims=True)
    part_out = nn(ot.astype(BF16), grads)

    @pl.when(step == 0)
    def _():
        gwout_ref[...] = part_out
        gbin_ref[...] = part_b

    @pl.when(step > 0)
    def _():
        gwout_ref[...] += part_out
        gbin_ref[...] += part_b

    @pl.when(step == last)
    def _():
        for copy in whole:
            copy.wait()
        dp_size = 2 * keep_ref.shape[0]
        each = units // 2 // dp_size
        for which, (a_buf, b_buf) in enumerate(((hid_buf, g_buf), (pre_buf, n_buf))):
            acc_ref[...] = tn(a_buf[...], b_buf[...])
            for slot in range(dp_size):
                out = (keep_ref, away_ref)[slot % 2]
                index = jnp.bitwise_xor(info_ref[1], slot)
                for shard in range(2):
                    base = pl.multiple_of(shard * (units // 2) + index * each, each)
                    out[slot // 2, shard, which * each : (which + 1) * each, :] = acc_ref[
                        pl.ds(base, each), :
                    ].astype(BF16)


def feed_back(info, blocks, normed, hidden, slope, ot, w_in, w_fc, w_out, dp_size):
    seq, d = normed.shape
    group = len(blocks)
    slots, pieces = listed(blocks)
    tile = 2 * seq // group
    ph, units = ot[0].shape[0], hidden.shape[1]
    wide = 2 * ph
    heads = wide // HD
    rows = pl.BlockSpec((tile, d), lambda i, info: (i, 0))
    unit_rows = pl.BlockSpec((tile, units), lambda i, info: (i, 0))
    turned = pl.BlockSpec((wide, tile), lambda i, info: (0, i))
    half_turned = pl.BlockSpec((ph, tile), lambda i, info: (0, i))
    packed = (dp_size // 2, 2, units // dp_size, d)
    anywhere = pl.BlockSpec(memory_space=pl.ANY)
    return pl.pallas_call(
        functools.partial(feed_back_kernel, slots),
        out_shape=(
            jax.ShapeDtypeStruct((seq, d), BF16),
            jax.ShapeDtypeStruct((wide, seq), BF16),
            jax.ShapeDtypeStruct((heads, seq, HD), BF16),
            jax.ShapeDtypeStruct((heads, 1, seq), F32),
            jax.ShapeDtypeStruct(packed, BF16),
            jax.ShapeDtypeStruct(packed, BF16),
            jax.ShapeDtypeStruct((wide, d), F32),
            jax.ShapeDtypeStruct((1, units), F32),
        ),
        grid_spec=pltpu.PrefetchScalarGridSpec(
            num_scalar_prefetch=1,
            grid=(seq // tile,),
            in_specs=[anywhere] * len(pieces)
            + [anywhere, anywhere, unit_rows, half_turned, half_turned]
            + [anywhere] * 6,
            out_specs=(
                rows,
                turned,
                pl.BlockSpec((heads, tile, HD), lambda i, info: (0, i, 0)),
                pl.BlockSpec((heads, 1, tile), lambda i, info: (0, 0, i)),
                resident(packed),
                resident(packed),
                resident((wide, d)),
                resident((1, units)),
            ),
            scratch_shapes=[
                pltpu.VMEM((seq, d), BF16),
                pltpu.VMEM((seq, d), BF16),
                pltpu.VMEM((seq, units), BF16),
                pltpu.VMEM((seq, units), BF16),
                pltpu.VMEM((d, units), BF16),
                pltpu.VMEM((units, d), BF16),
                pltpu.VMEM((wide, d), BF16),
                pltpu.VMEM((units, d), F32),
                pltpu.SemaphoreType.DMA((group // 2,)),
                pltpu.SemaphoreType.DMA((6,)),
                pltpu.SemaphoreType.DMA((2,)),
            ],
        ),
        compiler_params=params(56),
        cost_estimate=cost(2 * seq * d * (4 * units + 2 * wide), seq * (d * 6 + units * 4 + wide * 8) + d * units * 8),
        name="feed_back",
    )(info, *pieces, normed, hidden, slope, *ot, *w_in, *w_fc, *w_out)


def rows_back_kernel(count, info_ref, *refs):
    turned_refs, refs = refs[: 3 * count], refs[3 * count :]
    (n_ref, part_ref, wt_own, wt_other), refs = refs[:4], refs[4:]
    sum_ref, outs = refs[0], refs[1:-4]
    wt_ref, made_ref, sem, out_sem = refs[-4:]
    step = pl.program_id(0)
    ph = wt_own.shape[0]
    sources, places = (wt_own, wt_other), (wt_ref.at[:ph, :], wt_ref.at[ph:, :])

    @pl.when(step == 0)
    def _():
        start_weights(sources, places, sem)

    turned = jnp.concatenate([ref[...] for ref in turned_refs], axis=0)
    wait_weights(step, sources, places, sem, (0, 1))
    sums = []
    for cut in chunks_of(n_ref.shape[1]):
        made = part_ref[:, cut].astype(F32) + tn(turned, wt_ref[:, cut])
        made_ref[step, :, cut] = made.astype(BF16)
        sums.append(
            jnp.concatenate(
                [
                    jnp.sum(made * n_ref[:, cut].astype(F32), axis=0, keepdims=True),
                    jnp.sum(made, axis=0, keepdims=True),
                ],
                axis=0,
            )
        )
    sums = jnp.concatenate(sums, axis=1)
    send_pieces(info_ref, step, made_ref, outs, out_sem, False)

    @pl.when(step == pl.num_programs(0) - 1)
    def _():
        wait_all_pieces(info_ref, made_ref, outs, out_sem)

    @pl.when(step == 0)
    def _():
        sum_ref[...] = sums

    @pl.when(step > 0)
    def _():
        sum_ref[...] += sums


def rows_back(info, turned, normed, part, w_t, group):
    seq, d = normed.shape
    rows = seq // group // 2
    tile = 4 * rows
    depth = w_t[0].shape[0]
    tile_rows = pl.BlockSpec((tile, d), lambda i, info: (paired(i, info), 0))
    made = pl.pallas_call(
        functools.partial(rows_back_kernel, len(turned) // 3),
        out_shape=(jax.ShapeDtypeStruct((2, d), F32),)
        + (jax.ShapeDtypeStruct((rows, d), BF16),) * (2 * group),
        grid_spec=pltpu.PrefetchScalarGridSpec(
            num_scalar_prefetch=1,
            grid=(seq // tile,),
            in_specs=[
                pl.BlockSpec((part.shape[0], tile), lambda i, info: (0, paired(i, info)))
                for part in turned
            ]
            + [tile_rows, tile_rows]
            + [pl.BlockSpec(memory_space=pl.ANY)] * 2,
            out_specs=(resident((2, d)),) + (pl.BlockSpec(memory_space=pl.ANY),) * (2 * group),
            scratch_shapes=[
                pltpu.VMEM((2 * depth, d), BF16),
                pltpu.VMEM((seq // tile, tile, d), BF16),
                pltpu.SemaphoreType.DMA((2,)),
                pltpu.SemaphoreType.DMA((2 * group,)),
            ],
        ),
        compiler_params=params(36),
        cost_estimate=cost(2 * seq * d * 2 * depth, seq * (d * 6 + depth * 4) + d * depth * 4),
        name="rows_back",
    )(info, *turned, normed, part, *w_t)
    return made[0], made[1:]


def weights_back_kernel(info_ref, dq_ref, dk_ref, dv_ref, n_ref, gwout_ref, keep_ref, away_ref, acc_ref):
    step = pl.program_id(0)
    ph = gwout_ref.shape[0]
    turned = jnp.concatenate([dq_ref[...], dk_ref[...], dv_ref[...]], axis=0)
    part = nn(turned, n_ref[...])

    @pl.when(step == 0)
    def _():
        acc_ref[: 3 * ph, :] = part
        acc_ref[3 * ph :, :] = gwout_ref[...]

    @pl.when(step > 0)
    def _():
        acc_ref[: 3 * ph, :] += part

    @pl.when(step == pl.num_programs(0) - 1)
    def _():
        rows = keep_ref.shape[1]
        for slot in range(2 * keep_ref.shape[0]):
            out = (keep_ref, away_ref)[slot % 2]
            base = pl.multiple_of(jnp.bitwise_xor(info_ref[1], slot) * rows, rows)
            out[slot // 2] = acc_ref[pl.ds(base, rows), :].astype(BF16)


def weights_back(info, turned, normed, gw_out, shard, group, dp_size):
    seq, d = normed.shape
    tile = 2 * seq // group
    ph = turned[0].shape[0]
    packed = (dp_size // 2, 4 * ph // dp_size, d)
    return pl.pallas_call(
        weights_back_kernel,
        out_shape=(jax.ShapeDtypeStruct(packed, BF16),) * 2,
        grid_spec=pltpu.PrefetchScalarGridSpec(
            num_scalar_prefetch=1,
            grid=(seq // tile,),
            in_specs=[pl.BlockSpec((ph, tile), lambda i, info: (0, i))] * 3
            + [
                pl.BlockSpec((tile, d), lambda i, info: (i, 0)),
                pl.BlockSpec((ph, d), lambda i, info: (shard, 0)),
            ],
            out_specs=(resident(packed),) * 2,
            scratch_shapes=[pltpu.VMEM((4 * ph, d), F32)],
        ),
        compiler_params=params(20),
        cost_estimate=cost(2 * seq * d * 3 * ph, seq * (d * 2 + ph * 6) + d * ph * 16),
        name="weights_back",
    )(info, *turned, normed, gw_out)


def finish_feed_kernel(info_ref, *refs):
    pieces, (gin_ref, gfc_ref) = refs[:-2], refs[-2:]
    rows = gfc_ref.shape[0]
    for slot, piece in enumerate(pieces):

        @pl.when(pl.program_id(0) == slot)
        def _():
            gfc_ref[...] = piece[:rows, :].astype(F32)
            gin_ref[...] = piece[rows:, :].astype(F32).T


def finish_feed(info, pieces, units):
    count = len(pieces)
    d = pieces[0].shape[1]
    return pl.pallas_call(
        finish_feed_kernel,
        out_shape=(jax.ShapeDtypeStruct((d, units), F32), jax.ShapeDtypeStruct((units, d), F32)),
        grid_spec=pltpu.PrefetchScalarGridSpec(
            num_scalar_prefetch=1,
            grid=(count,),
            in_specs=[resident(pieces[0].shape)] * count,
            out_specs=(
                pl.BlockSpec((d, units // count), lambda i, info: (0, jnp.bitwise_xor(i, info[1]))),
                pl.BlockSpec((units // count, d), lambda i, info: (jnp.bitwise_xor(i, info[1]), 0)),
            ),
        ),
        compiler_params=params(16),
        cost_estimate=cost(0, d * units * 12),
        name="finish_feed",
    )(info, *pieces)


def finish_project_kernel(info_ref, *refs):
    pieces, (gqkv_ref, gout_ref) = refs[:-2], refs[-2:]
    index = pl.program_id(0)
    slot_now = jnp.bitwise_xor(index, info_ref[1])
    for slot, piece in enumerate(pieces):

        @pl.when((slot_now == slot) & (index < 3))
        def _():
            gqkv_ref[0] = piece[...].astype(F32).T

        @pl.when((slot_now == slot) & (index == 3))
        def _():
            gout_ref[...] = piece[...].astype(F32)


def finish_project(info, pieces):
    rows, d = pieces[0].shape
    return pl.pallas_call(
        finish_project_kernel,
        out_shape=(jax.ShapeDtypeStruct((3, d, rows), F32), jax.ShapeDtypeStruct((rows, d), F32)),
        grid_spec=pltpu.PrefetchScalarGridSpec(
            num_scalar_prefetch=1,
            grid=(4,),
            in_specs=[resident((rows, d))] * 4,
            out_specs=(
                pl.BlockSpec((1, d, rows), lambda i, info: (jnp.minimum(i, 2), 0, 0)),
                resident((rows, d)),
            ),
        ),
        compiler_params=params(16),
        cost_estimate=cost(0, d * rows * 24),
        name="finish_project",
    )(info, *pieces)


def mask_scores(scores, start, key_base, query_base, diagonal):
    key_places = key_base + lax.broadcasted_iota(jnp.int32, scores.shape, 0)
    keep = key_places >= start
    if diagonal:
        query_places = query_base + lax.broadcasted_iota(jnp.int32, scores.shape, 1)
        keep = keep & (key_places <= query_places)
    return jnp.where(keep, scores, NEG_LARGE)


def attend_kernel(low_ref, start_ref, qt_ref, k_ref, vt_ref, ot_ref, lse_ref, m_ref, l_ref, acc_ref):
    block = qt_ref.shape[1]
    i = pl.program_id(1)
    queries = qt_ref[...]
    start = start_ref[...]

    def step(j, diagonal):
        base = pl.multiple_of(j * block, block)
        scores = nn(k_ref[0, pl.ds(base, block), :], queries)
        scores = mask_scores(scores, start, base, i * block, diagonal)
        peak = jnp.max(scores, axis=0, keepdims=True)
        values = vt_ref[:, pl.ds(base, block)]
        if diagonal:
            weights = jnp.exp(scores - peak)
            m_ref[...] = peak
            l_ref[...] = jnp.sum(weights, axis=0, keepdims=True)
            acc_ref[...] = nn(values, weights.astype(BF16))
        else:
            before = m_ref[...]
            peak = jnp.maximum(before, peak)
            shrink = jnp.exp(before - peak)
            weights = jnp.exp(scores - peak)
            m_ref[...] = peak
            l_ref[...] = l_ref[...] * shrink + jnp.sum(weights, axis=0, keepdims=True)
            acc_ref[...] = acc_ref[...] * shrink + nn(values, weights.astype(BF16))

    step(i, True)

    def body(j, carry):
        step(j, False)
        return carry

    lax.fori_loop(low_ref[i], i, body, 0)
    total = l_ref[...]
    ot_ref[...] = acc_ref[...] * (1.0 / total)
    lse_ref[0] = m_ref[...] + jnp.log(total)


def attend(low, start, qt, k, vt, block, base, heads):
    seq = qt.shape[1]
    blocks = seq // block
    return pl.pallas_call(
        attend_kernel,
        out_shape=(
            jax.ShapeDtypeStruct((heads * HD, seq), F32),
            jax.ShapeDtypeStruct((heads, 1, seq), F32),
        ),
        grid_spec=pltpu.PrefetchScalarGridSpec(
            num_scalar_prefetch=1,
            grid=(heads, blocks),
            in_specs=[
                pl.BlockSpec((1, block), lambda h, i, low: (0, i)),
                pl.BlockSpec((HD, block), lambda h, i, low: (base + h, i)),
                pl.BlockSpec((1, seq, HD), lambda h, i, low: (base + h, 0, 0)),
                pl.BlockSpec((HD, seq), lambda h, i, low: (base + h, 0)),
            ],
            out_specs=(
                pl.BlockSpec((HD, block), lambda h, i, low: (h, i)),
                pl.BlockSpec((1, 1, block), lambda h, i, low: (h, 0, i)),
            ),
            scratch_shapes=[
                pltpu.VMEM((1, block), F32),
                pltpu.VMEM((1, block), F32),
                pltpu.VMEM((HD, block), F32),
            ],
        ),
        compiler_params=params(12),
        cost_estimate=cost(heads * seq * seq * 512, heads * seq * HD * 12, heads * seq * seq // 2),
        name="attend",
    )(low, start, qt, k, vt)


def attend_back_kernel(
    high_ref, start_ref, lse_ref, delta_ref, cos_ref, sin_ref, qt_ref, kt_ref, gt_ref, q_ref, k_ref, v_ref, g_ref,
    dqt_out, dkt_out, dvt_out, dqt_ref, dk_ref, dv_ref
):
    seq = qt_ref.shape[1]
    blocks = high_ref.shape[0]
    block = seq // blocks
    dqt_ref[...] = jnp.zeros_like(dqt_ref)

    def pair(i, j, diagonal):
        qs = pl.ds(pl.multiple_of(i * block, block), block)
        ks = pl.ds(pl.multiple_of(j * block, block), block)
        scores = nn(k_ref[0, ks, :], qt_ref[:, qs])
        scores = mask_scores(scores, start_ref[:, qs], j * block, i * block, diagonal)
        probs = jnp.exp(scores - lse_ref[0, :, qs])
        grad_probs = nn(v_ref[0, ks, :], gt_ref[:, qs])
        grad_scores = (probs * (grad_probs - delta_ref[0, :, qs])).astype(BF16)
        dv = nn(probs.astype(BF16), g_ref[0, qs, :])
        dk = nn(grad_scores, q_ref[0, qs, :])
        if diagonal:
            dv_ref[ks, :] = dv
            dk_ref[ks, :] = dk
        else:
            dv_ref[ks, :] += dv
            dk_ref[ks, :] += dk
        dqt_ref[:, qs] += nn(kt_ref[:, ks], grad_scores)

    def keys(j, carry):
        pair(j, j, True)

        def queries(i, inner):
            pair(i, j, False)
            return inner

        lax.fori_loop(j + 1, high_ref[j], queries, 0)
        return carry

    lax.fori_loop(0, blocks, keys, 0)
    cos, sin = cos_ref[...], sin_ref[...]
    half = ROT // 2

    def store(out, t):
        a, b = t[:half], t[half:ROT]
        out[:half] = (a * cos + b * sin).astype(BF16)
        out[half:ROT] = (b * cos - a * sin).astype(BF16)
        out[ROT:] = t[ROT:].astype(BF16)

    store(dqt_out, dqt_ref[...] * (HD**-0.5))
    store(dkt_out, dk_ref[...].T)
    dvt_out[...] = dv_ref[...].T.astype(BF16)


def attend_back(high, start, lse, delta, cos, sin, qt, kt, gt, q, k, v, g, base, local, heads, mib):
    seq = qt.shape[1]
    flat = pl.BlockSpec((HD, seq), lambda h, high: (local + h, 0))
    split = pl.BlockSpec((1, seq, HD), lambda h, high: (local + h, 0, 0))
    both_flat = pl.BlockSpec((HD, seq), lambda h, high: (base + h, 0))
    both_split = pl.BlockSpec((1, seq, HD), lambda h, high: (base + h, 0, 0))
    row = pl.BlockSpec((1, seq), lambda h, high: (0, 0))
    head_row = pl.BlockSpec((1, 1, seq), lambda h, high: (base + h, 0, 0))
    own_row = pl.BlockSpec((1, 1, seq), lambda h, high: (local + h, 0, 0))
    table = pl.BlockSpec((ROT // 2, seq), lambda h, high: (0, 0))
    return pl.pallas_call(
        attend_back_kernel,
        out_shape=(jax.ShapeDtypeStruct((heads * HD, seq), BF16),) * 3,
        grid_spec=pltpu.PrefetchScalarGridSpec(
            num_scalar_prefetch=1,
            grid=(heads,),
            in_specs=[row, own_row, head_row, table, table]
            + [flat, flat, both_flat]
            + [split, split, split, both_split],
            out_specs=(pl.BlockSpec((HD, seq), lambda h, high: (h, 0)),) * 3,
            scratch_shapes=[
                pltpu.VMEM((HD, seq), F32),
                pltpu.VMEM((seq, HD), F32),
                pltpu.VMEM((seq, HD), F32),
            ],
        ),
        compiler_params=params(mib),
        cost_estimate=cost(heads * seq * seq * 1280, heads * HD * seq * 24, heads * seq * seq // 2),
        name="attend_back",
    )(high, start, lse, delta, cos, sin, qt, kt, gt, q, k, v, g)


def run_starts(segments):
    places = lax.broadcasted_iota(jnp.int32, segments.shape, 1)
    leading = jnp.ones_like(segments[:, :1])
    changes = jnp.concatenate(
        [leading, (segments[:, 1:] != segments[:, :-1]).astype(jnp.int32)], axis=1
    )
    starts = lax.cummax(places * changes, axis=1)
    return places, starts


def build(dp_size, tensor_size):
    def per_device(
        inputs, segments, norm_gain, norm_bias, w_qkv, w_out, w_in, b_in, w_fc, b_out, cotangent
    ):
        row_count, seq = segments.shape
        tokens, d = inputs.shape
        group = tensor_size // row_count
        half_rot = ROT // 2
        block = 512
        me = lax.axis_index("tensor")
        dp = lax.axis_index("dp")
        row = me // group
        info = jnp.stack([me % group, dp]).astype(jnp.int32)
        other = [(i, (i + group) % tensor_size) for i in range(tensor_size)]
        bits = bit_list(group)
        dp_bits = bit_list(dp_size)
        def normalize(rows):
            rows = rows.astype(F32)
            centred = rows - jnp.mean(rows, axis=-1, keepdims=True)
            inv_std = lax.rsqrt(jnp.mean(centred * centred, axis=-1, keepdims=True) + EPSILON)
            return centred * inv_std, inv_std

        def slice_of(indexed):
            return lax.dynamic_index_in_dim(indexed, dp, 0, keepdims=False)

        def fetch(part):
            return lax.ppermute(part, "tensor", other)

        def share(got):
            return gather_slots(got, "dp", dp_size, dp_bits[::-1])

        def rows_of(pieces, start, stop):
            return natural({k: pieces[k][start:stop] for k in pieces}, dp)

        units, per_head = w_in.shape[1], w_qkv.shape[2]
        shard_heads = per_head // HD
        fc_rows = units // dp_size
        qkv_slice = slice_of(w_qkv.reshape(dp_size, -1, per_head))
        qkv_slice, rows_in = tie(qkv_slice, inputs)
        qkv_got = fetch(qkv_slice)
        normed_own = [
            (normalize(half)[0] * norm_gain + norm_bias).astype(BF16) for half in halves_of(rows_in)
        ]
        n_got = gather_lead(normed_own, tensor_size, bits)
        in_slice = slice_of(w_in.reshape(dp_size, -1, units))
        fc_slice = jnp.concatenate(
            [slice_of(w_fc.reshape(dp_size, -1, d)), slice_of(w_out.reshape(dp_size, -1, d))], axis=0
        )
        wt_own = jnp.concatenate([w_qkv[c].T for c in range(3)], axis=0)

        segs = lax.dynamic_slice_in_dim(segments, row, 1, axis=0)
        places, starts = run_starts(segs)
        first_key = jnp.where(segs >= 0, starts, places)
        offsets = (places - starts).astype(F32)
        frequency = jnp.exp(
            lax.broadcasted_iota(F32, (half_rot,), 0) * (-2.0 * math.log(10000.0) / ROT)
        )
        angles = frequency[:, None] * offsets
        cos_t, sin_t = jnp.cos(angles), jnp.sin(angles)
        blocks = seq // block
        low = (jnp.min(first_key.reshape(blocks, block), axis=1) // block).astype(jnp.int32)
        reach = low[None, :] <= jnp.arange(blocks)[:, None]
        high = jnp.max(
            jnp.where(reach, jnp.arange(1, blocks + 1, dtype=jnp.int32)[None, :], 0), axis=1
        ).astype(jnp.int32)

        cotangent_sum = jnp.sum(cotangent.astype(F32), axis=0, keepdims=True)
        prepared = (wt_own, cos_t, sin_t, first_key, low, high, cotangent_sum)
        n_got, normed_own, qkv_got, (in_slice, fc_slice), prepared = tie(
            n_got, normed_own, qkv_got, (in_slice, fc_slice), prepared
        )
        n_got = {**n_got, **gather_own(normed_own, tensor_size, bits)}
        wt_own, cos_t, sin_t, first_key, low, high, cotangent_sum = prepared
        n_blocks = gather_rest(normed_own, n_got, tensor_size, bits)
        qkv_pieces = gather_slots(qkv_got, "dp", dp_size, dp_bits[::-1][:1])
        n_blocks, qkv_pieces, in_slice, fc_slice = tie(n_blocks, qkv_pieces, in_slice, fc_slice)
        qkv_pieces = gather_more(qkv_pieces, "dp", dp_size, dp_bits[::-1][1:])
        in_got, fc_got, b_in_other = (fetch(part) for part in (in_slice, fc_slice, b_in))

        def heads_forward(made, base, count):
            return attend(low, first_key, made[0], made[4], made[2], block, base, count)

        cut = shard_heads // 2
        made = project(info, n_blocks, wt_own, cos_t, sin_t)
        normed, own = made[0], made[1:]
        attended = []
        cot = halves_of(cotangent)
        if cut:
            attended.append(heads_forward(own, 0, cut))
            (attended[0], in_got), own, cot, qkv_pieces = tie((attended[0], in_got), own, cot, qkv_pieces)
        g_got = gather_lead(cot, tensor_size, bits)
        in_pieces = gather_slots(in_got, "dp", dp_size, dp_bits[::-1][:1])
        qkv_other = rows_of(qkv_pieces, 0, None).reshape(w_qkv.shape)
        wt_other = jnp.concatenate([qkv_other[c].T for c in range(3)], axis=0)
        rest = project(None, normed, wt_other, cos_t, sin_t)
        attended.append(heads_forward(own, cut, shard_heads - cut))
        attended[-1], in_pieces, fc_got, rest = tie(attended[-1], in_pieces, fc_got, rest)
        in_pieces = gather_more(in_pieces, "dp", dp_size, dp_bits[::-1][1:])
        fc_pieces = gather_slots(fc_got, "dp", dp_size, dp_bits[::-1][:1])
        attended_rest = []
        if cut:
            attended_rest.append(heads_forward(rest, 0, cut))
            attended_rest[0], in_pieces, fc_pieces, g_got, cot, rest = tie(
                attended_rest[0], in_pieces, fc_pieces, g_got, cot, rest
            )
        g_got = {**g_got, **gather_own(cot, tensor_size, bits)}
        fc_pieces = gather_more(fc_pieces, "dp", dp_size, dp_bits[::-1][1:])
        w_in_other = rows_of(in_pieces, 0, None)
        g_blocks = gather_rest(cot, g_got, tensor_size, bits)
        attended_rest.append(heads_forward(rest, cut, shard_heads - cut))
        attended_rest[-1], fc_pieces, w_in_other = tie(attended_rest[-1], fc_pieces, w_in_other)
        (ot_own, lse_own), (ot_other, lse_other) = (
            tuple(jnp.concatenate([part[n] for part in parts], axis=0) for n in range(2))
            for parts in (attended, attended_rest)
        )
        w_fc_other = rows_of(fc_pieces, 0, fc_rows)
        w_out_other = rows_of(fc_pieces, fc_rows, None)
        ot = (ot_own, ot_other)
        w_in_both, w_fc_both, w_out_both = (w_in, w_in_other), (w_fc, w_fc_other), (w_out, w_out_other)
        hidden, slope, out_pieces = feed(
            info, normed, ot, w_in_both, (b_in[None], b_in_other[None]), w_fc_both, w_out_both, group
        )

        def by_slot(pieces):
            return {(k, half): pieces[2 * k + half] for k in range(group) for half in range(2)}

        last_stage = len(bits) - 1
        out_parts = by_slot(out_pieces)
        out_got = reduce_sends(out_parts, tensor_size, bits, last_stage)
        out_early = reduce_early(out_parts, tensor_size, bits)
        made = feed_back(
            info, g_blocks, normed, hidden, slope, ot, w_in_both, w_fc_both, w_out_both, dp_size
        )
        made, out_got, out_early = tie(made, out_got, out_early)
        gn_part, gt, g_heads, delta, keep1, away1, gw_out, gb_in = made
        out_parts = reduce_adds(out_parts, out_got)
        for stage in range(last_stage - 1, 0, -1):
            out_parts = reduce_adds(out_parts, reduce_sends(out_parts, tensor_size, bits, stage))

        def settle_dp(parts, bit):
            got = {
                k ^ bit: [swap(part, "dp", dp_size, bit) for part in parts[k]]
                for k in sorted(parts)
                if k & bit
            }
            return {k: parts[k] for k in got}, got

        def settle_add(kept, got):
            return {k: tuple(add(a, b) for a, b in zip(kept[k], got[k])) for k in kept}

        def settle_rest(parts, got):
            for bit in dp_bits[2:]:
                parts, got = settle_dp(settle_add(parts, got), bit)
            return settle_add(parts, got)[0]

        share_bits = dp_bits[::-1]

        def heads_back(shard):
            qt, kt, vt, q, k, v = (own, rest)[shard]
            return attend_back(
                high, first_key, (lse_own, lse_other)[shard], delta, cos_t, sin_t, qt, kt, gt, q, k, v, g_heads,
                shard * shard_heads, 0, shard_heads, (20, 20)[shard]
            )

        got1 = swap(away1, "dp", dp_size, dp_bits[0])
        got1, out_parts, gt = tie(got1, out_parts, gt)
        sums1 = {
            2 * j: tuple(add(keep1[j, s], got1[j, s]) for s in range(2)) for j in range(dp_size // 2)
        }
        sums1, out_parts, gt = tie(sums1, out_parts, gt)
        out_got = reduce_late(out_parts, out_early, tensor_size, bits)
        kept1, got1 = settle_dp(sums1, dp_bits[1])
        turned_other = heads_back(1)
        keep2, away2 = weights_back(info, turned_other, normed, gw_out, 1, group, dp_size)
        keep2, away2, got1, gt = tie(keep2, away2, got1, gt)
        got2 = swap(away2, "dp", dp_size, dp_bits[0])
        own1, other1 = settle_rest(kept1, got1)
        own1, other1, got2, gt = tie(own1, other1, got2, gt)
        sums2 = {2 * j: (add(keep2[j], got2[j]),) for j in range(dp_size // 2)}
        sums2, other1, gt = tie(sums2, other1, gt)
        kept2, got2 = settle_dp(sums2, dp_bits[1])
        other1 = fetch(other1)
        turned_own = heads_back(0)
        turned_own, got2, out_got = tie(turned_own, got2, out_got)
        (other2,) = settle_rest(kept2, got2)
        keep3, away3 = weights_back(info, turned_own, normed, gw_out, 0, group, dp_size)
        keep3, away3, other1, other2, turned_own = tie(keep3, away3, other1, other2, turned_own)
        got3 = swap(away3, "dp", dp_size, dp_bits[0])
        other2_got = fetch(other2)
        total1 = add(own1, other1)
        pieces1 = gather_slots(total1, "dp", dp_size, share_bits[:1])
        sums, gn_pieces = rows_back(
            info, [*turned_own, *turned_other], normed, gn_part, (wt_own, wt_other), group
        )
        sums, gn_pieces, got3 = tie(sums, gn_pieces, got3)
        gn_parts = by_slot(gn_pieces)
        gn_got = reduce_sends(gn_parts, tensor_size, bits, last_stage)
        sums3 = {2 * j: (add(keep3[j], got3[j]),) for j in range(dp_size // 2)}
        kept3, got3 = settle_dp(sums3, dp_bits[1])

        bias_parts = jnp.zeros((tensor_size, units), F32)
        bias_parts = lax.dynamic_update_slice_in_dim(bias_parts, gb_in[:, :units], me, axis=0)
        bias_parts = lax.dynamic_update_slice_in_dim(
            bias_parts, gb_in[:, units:], (me + group) % tensor_size, axis=0
        )
        cotangent_f = cotangent.astype(F32)
        total = jnp.concatenate([sums, cotangent_sum, bias_parts.reshape(-1, d)], axis=0)
        total_got = swap(total, "dp", dp_size, dp_bits[0])
        gn_got, gn_parts, kept3, got3, pieces1, total_got, other2_got = tie(
            gn_got, gn_parts, kept3, got3, pieces1, total_got, other2_got
        )
        gn_early = reduce_early(gn_parts, tensor_size, bits)
        pieces1 = gather_more(pieces1, "dp", dp_size, share_bits[1:])
        gn_parts = reduce_adds(gn_parts, gn_got)
        for number in range(last_stage - 1, 0, -1):
            gn_parts = reduce_adds(gn_parts, reduce_sends(gn_parts, tensor_size, bits, number))
        (own3,) = settle_rest(kept3, got3)
        total2 = add(own3, other2_got)
        total = total + total_got
        gn_parts, pieces1, total2, total = tie(gn_parts, pieces1, total2, total)
        gn_got = reduce_late(gn_parts, gn_early, tensor_size, bits)
        pieces2 = gather_slots(total2, "dp", dp_size, share_bits[:1])
        for bit in dp_bits[1:]:
            total = total + swap(total, "dp", dp_size, bit)
        pieces1 = [pieces1[k] for k in range(dp_size)]
        if fc_rows % LANES == 0:
            grad_in, grad_fc = finish_feed(info, pieces1, units)
        else:
            pieces1 = dict(enumerate(pieces1))
            grad_fc = rows_of(pieces1, 0, fc_rows).astype(F32)
            grad_in = rows_of(pieces1, fc_rows, None).T.astype(F32)
        pieces2, total, grad_in, grad_fc, out_parts = tie(pieces2, total, grad_in, grad_fc, out_parts)
        pieces2 = gather_more(pieces2, "dp", dp_size, share_bits[1:])
        total_got = [swap(total, "tensor", tensor_size, k) for k in range(2, tensor_size, 2)]
        output = (inputs.astype(F32) + reduce_total(out_parts, {**out_early, **out_got}) + b_out).astype(BF16)
        pieces2 = [pieces2[k] for k in range(dp_size)]
        if dp_size == 4 and per_head % LANES == 0:
            grad_qkv, grad_out = finish_project(info, pieces2)
        else:
            stacked = natural(dict(enumerate(pieces2)), dp)
            grad_qkv = jnp.swapaxes(
                stacked[: 3 * per_head].reshape(3, per_head, d), 1, 2
            ).astype(F32)
            grad_out = stacked[3 * per_head :].astype(F32)
        gn_got, gn_parts, total_got, grad_qkv, grad_out, output = tie(
            {**gn_early, **gn_got}, gn_parts, total_got, grad_qkv, grad_out, output
        )
        for part in total_got:
            total = total + part
        total = total + swap(total, "tensor", tensor_size, 1)

        unit_rows, inv_std = normalize(inputs)
        grad_norm_own = reduce_total(gn_parts, gn_got)
        scaled = grad_norm_own * norm_gain
        grad_local = inv_std * (
            scaled
            - jnp.mean(scaled, axis=-1, keepdims=True)
            - unit_rows * jnp.mean(scaled * unit_rows, axis=-1, keepdims=True)
        )
        grad_inputs = cotangent_f + grad_local

        grad_bias = total[1]
        grad_gain = (total[0] - norm_bias * grad_bias) / norm_gain
        grad_b_out = total[2]
        grad_b_in = lax.dynamic_slice_in_dim(total[3:].reshape(tensor_size, units), me, 1, axis=0)[0]
        return (
            output,
            grad_inputs,
            grad_gain,
            grad_bias,
            grad_qkv,
            grad_out,
            grad_in,
            grad_b_in,
            grad_fc,
            grad_b_out,
        )

    return per_device


def solution(mesh):
    tokens = P(("dp", "tensor"), None)
    return jax.shard_map(
        build(mesh.shape["dp"], mesh.shape["tensor"]),
        mesh=mesh,
        in_specs=(
            tokens,
            P("dp", None),
            P(),
            P(),
            P(None, None, "tensor"),
            P("tensor", None),
            P(None, "tensor"),
            P("tensor"),
            P("tensor", None),
            P(),
            tokens,
        ),
        out_specs=(
            tokens,
            tokens,
            P(),
            P(),
            P(None, None, "tensor"),
            P("tensor", None),
            P(None, "tensor"),
            P("tensor"),
            P("tensor", None),
            P(),
        ),
        check_vma=False,
    )
```
